32 devices in a mesh: rep: 2 (over core), shard: 16 (over z, y, x).
Axes of the slice: x: 2, y: 2, z: 4, core: 2. Of those that a mesh axis runs over, the one named last changes fastest.
Arguments:
- hidden_states: bfloat16 [4096, 768], P(('rep', 'shard')), may hold values from -40 to 40
- cotangent: bfloat16 [4096, 768], P(('rep', 'shard')), may hold values from -6 to 6
- lengths: int32 [32], P(('rep', 'shard')), may hold values from 32 to 128, as said below
- params: float32 [7087104], P('shard'), may hold values from -4 to 4
- first_moment: float32 [7087104], P('shard'), may hold values from -12 to 12
- second_moment: float32 [7087104], P('shard'), may hold values from 1 to 100
Outputs:
- block_output: bfloat16 [4096, 768], P(('rep', 'shard'))
- input_grad: bfloat16 [4096, 768], P(('rep', 'shard'))
- weight_grad: float32 [7087104], P('shard')
- new_params: float32 [7087104], P('shard')
- new_first: float32 [7087104], P('shard')
- new_second: float32 [7087104], P('shard')
The draws below stay inside these ranges and needn't reach their ends.
Inputs may be any that keep to these rules, and one draw needn't show every extreme that they name: `lengths`: at least one sequence is entirely valid.
All inputs are finite; a program needn't handle non-finite values.
Results may differ from the reference program's by a relative error of at most 0.013.
The reference program's roundings to bfloat16 on the way count: a program that leaves them out, or rounds other values in their place, can miss the bound.
Values may be sent and summed in bfloat16 or wider, within the bound.
No kernel may reach another device: no remote copies, remote signals or barrier semaphores. Data moves between devices by JAX's collectives and lax.ppermute only.
A program may use at most 192 MiB of HBM per device.

```python
import math
import jax
import jax.numpy as jnp
from jax import lax

D = 768
HEADS = 12
HEAD = 64
FF = 3072
TOK_DEV = 128
STEP = 3
HW = 768
PARAMS = 7087104
SEQS = 32
TOKENS = 4096


def noise_vector(key, amount, scale):
    return jax.random.normal(key, (amount,), jnp.float32) * scale


def draw_params(key, part):
    keys = jax.random.split(key, 13)
    out_scale = math.sqrt(TOK_DEV / (2.0 * HW))
    plan = [(D * 3 * HW, 1.0 / math.sqrt(D), 0.0), (HW * D, out_scale, 0.0), (D * FF, 1.0 / math.sqrt(D), 0.0), (FF * D, 1.0 / math.sqrt(FF), 0.0), (HW, 0.5, 0.0), (HW, 0.5, 0.0), (D, 0.5, 0.0), (D, 0.25, 1.0), (D, 0.3, 0.0), (FF, 0.5, 0.0), (D, 0.5, 0.0), (D, 0.25, 1.0), (D, 0.3, 0.0)]
    pieces = []
    for index_num, entry in enumerate(plan):
        pieces.append(entry[2] + noise_vector(keys[index_num], entry[0], entry[1]))
    return jnp.clip(jnp.concatenate(pieces), -4.0, 4.0).astype(jnp.float32)


def draw_lengths(key, part):
    key_base, key_full = jax.random.split(key)
    base = jax.random.randint(key_base, (SEQS,), TOK_DEV // 4, TOK_DEV + 1)
    full_at = jax.random.randint(key_full, (), 0, SEQS)
    return jnp.where(jnp.arange(SEQS) == full_at, TOK_DEV, base).astype(jnp.int32)


def draw_hidden_states(key, part):
    keys = jax.random.split(key, 1)
    base = jax.random.normal(keys[0], (TOKENS, D), jnp.float32)
    return jnp.clip(base, -40.0, 40.0).astype(jnp.bfloat16)


def steps_of(rng, dims, cuts, least, high):
    def one(axis_at, parts):
        draws = jax.random.uniform(jax.random.fold_in(jax.random.fold_in(rng, 6), axis_at), (parts,), jnp.float32, least / len(cuts), high / len(cuts))
        return jnp.repeat(jnp.exp(draws), dims[axis_at] // parts).reshape((-1,) + (1,) * (len(dims) - axis_at - 1))

    factor_of = one(*cuts[0])
    for cut in cuts[1:]:
        factor_of = factor_of * one(*cut)
    return factor_of


def centred(rng, extent, scale, most, cuts=(), held_as=jnp.bfloat16):
    entries = jax.random.normal(rng, extent, jnp.float32) * scale
    if len(cuts) > 0:
        entries = steps_of(rng, extent, cuts, -0.22, 0.18) * entries
    return jnp.clip(entries, min=-most, max=most).astype(held_as)


def setup_inputs(seed: int = 0) -> dict:
    key_of = jax.random.split(jax.random.key(seed), 7)
    return {
        "hidden_states": draw_hidden_states(jax.random.fold_in(key_of[6], 71), 0),
        "cotangent": centred(key_of[1], (TOKENS, D), 1.0, 6.0, ((0, 32),)),
        "lengths": draw_lengths(jax.random.fold_in(key_of[6], 71), 0),
        "params": draw_params(jax.random.fold_in(key_of[6], 71), 0),
        "first_moment": centred(key_of[4], (PARAMS,), 2.0, 12.0, ((0, 16),), jnp.float32),
        "second_moment": jnp.clip(jnp.exp(math.log(100.0) - 4.6051702 * jax.random.uniform(key_of[5], (PARAMS,), jnp.float32) ** steps_of(key_of[5], (PARAMS,), ((0, 16),), -0.2, 0.2)), 1.0, 100.0),
    }


norm_eps = 1e-05
adam_eps = 1e-06
beta_one = 0.9
beta_two = 0.98
learn_rate = 0.01
decay_rate = 0.01
masked_score = -1e+30
inv_sqrt_two = 1.0 / math.sqrt(2.0)
inv_sqrt_tau = 1.0 / math.sqrt(2.0 * math.pi)

def layout():
    return [('triple_weight', (D, 3 * HW)), ('output_weight', (HW, D)), ('expand_weight', (D, FF)), ('reduce_weight', (FF, D)), ('query_bias', (HW,)), ('value_bias', (HW,)), ('output_bias', (D,)), ('first_gain', (D,)), ('first_shift', (D,)), ('expand_bias', (FF,)), ('reduce_bias', (D,)), ('second_gain', (D,)), ('second_shift', (D,))]

def split_flat(flat_vector):
    pieces = {}
    offset = 0
    for entry_name, dims_of in layout():
        amount = math.prod(dims_of)
        pieces[entry_name] = flat_vector[offset:offset + amount].reshape(dims_of)
        offset = offset + amount
    return pieces

def inner_rows(left_side, right_side):
    return lax.dot_general(left_side, right_side, (((0,), (0,)), ((), ())), preferred_element_type=jnp.float32)

def by_transpose(left_side, right_side):
    return lax.dot_general(left_side, right_side, (((1,), (1,)), ((), ())), preferred_element_type=jnp.float32)

def heads_of(row_block):
    return row_block.reshape(row_block.shape[0], HEADS, HEAD).astype(jnp.float32)

def normalize(values_in):
    centered = values_in - lax.optimization_barrier(jnp.mean(values_in, axis=-1, keepdims=True))
    inv_root = lax.rsqrt(lax.optimization_barrier(jnp.mean(centered * centered, axis=-1, keepdims=True)) + norm_eps)
    return (centered * inv_root, inv_root)

def norm_back(grad_in, normed, inv_root):
    return inv_root * (grad_in - lax.optimization_barrier(jnp.mean(grad_in, axis=-1, keepdims=True)) - normed * lax.optimization_barrier(jnp.mean(grad_in * normed, axis=-1, keepdims=True)))

def gelu_slope(pre_act):
    return 0.5 * (1.0 + lax.erf(pre_act * inv_sqrt_two)) + pre_act * jnp.exp(-0.5 * pre_act * pre_act) * inv_sqrt_tau

def attention_scores(queries, key_rows, length):
    scores = jnp.einsum('qhd,khd->hqk', heads_of(queries), heads_of(key_rows)) * (1.0 / math.sqrt(HEAD))
    key_valid = jnp.arange(scores.shape[-1]) < length
    return jnp.where(key_valid, scores, masked_score)

def forward(tokens, length, prm):
    rows = tokens.shape[0]
    triple = jnp.dot(tokens, prm['triple_weight'], preferred_element_type=jnp.float32)
    queries = (triple[:, :HW] + prm['query_bias'].astype(jnp.float32)).astype(jnp.bfloat16)
    key_rows = triple[:, HW:2 * HW].astype(jnp.bfloat16)
    value_rows = (triple[:, 2 * HW:] + prm['value_bias'].astype(jnp.float32)).astype(jnp.bfloat16)
    scores = attention_scores(queries, key_rows, length)
    top_score = lax.optimization_barrier(jnp.max(scores, axis=-1, keepdims=True))
    log_total = top_score + jnp.log(lax.optimization_barrier(jnp.sum(jnp.exp(scores - top_score), axis=-1, keepdims=True)))
    soft_weights = jnp.exp(scores - log_total).astype(jnp.bfloat16)
    context = jnp.einsum('hqk,khd->qhd', soft_weights.astype(jnp.float32), heads_of(value_rows))
    context = context.reshape(rows, HW).astype(jnp.bfloat16)
    first_sum = tokens.astype(jnp.float32) + jnp.dot(context, prm['output_weight'], preferred_element_type=jnp.float32) + prm['output_bias'].astype(jnp.float32)
    normed_one, root_one = normalize(first_sum)
    middle = normed_one * prm['first_gain'].astype(jnp.float32) + prm['first_shift'].astype(jnp.float32)
    middle_b = middle.astype(jnp.bfloat16)
    pre_act = jnp.dot(middle_b, prm['expand_weight'], preferred_element_type=jnp.float32) + prm['expand_bias'].astype(jnp.float32)
    activated = (0.5 * pre_act * (1.0 + lax.erf(pre_act * inv_sqrt_two))).astype(jnp.bfloat16)
    second_sum = middle + jnp.dot(activated, prm['reduce_weight'], preferred_element_type=jnp.float32) + prm['reduce_bias'].astype(jnp.float32)
    normed_two, root_two = normalize(second_sum)
    block_out = (normed_two * prm['second_gain'].astype(jnp.float32) + prm['second_shift'].astype(jnp.float32)).astype(jnp.bfloat16)
    kept = (queries, key_rows, value_rows, log_total, context, normed_one, root_one, middle_b, pre_act, activated, normed_two, root_two)
    return (block_out, kept)

def backward(tokens, length, cotangent, kept, prm):
    queries, key_rows, value_rows, log_total, context, normed_one, root_one, middle_b, pre_act, activated, normed_two, root_two = kept
    rows = tokens.shape[0]
    grad_out = cotangent.astype(jnp.float32)
    d_second = norm_back(grad_out * prm['second_gain'].astype(jnp.float32), normed_two, root_two)
    d_second_b = d_second.astype(jnp.bfloat16)
    d_pre = by_transpose(d_second_b, prm['reduce_weight']) * gelu_slope(pre_act)
    d_pre_b = d_pre.astype(jnp.bfloat16)
    d_middle = d_second + by_transpose(d_pre_b, prm['expand_weight'])
    d_first = norm_back(d_middle * prm['first_gain'].astype(jnp.float32), normed_one, root_one)
    d_first_b = d_first.astype(jnp.bfloat16)
    d_context = by_transpose(d_first_b, prm['output_weight']).astype(jnp.bfloat16)
    scores = attention_scores(queries, key_rows, length)
    soft_float = jnp.exp(scores - log_total)
    soft_weights = soft_float.astype(jnp.bfloat16)
    d_soft = jnp.einsum('qhd,khd->hqk', heads_of(d_context), heads_of(value_rows))
    delta = lax.optimization_barrier(jnp.sum(d_soft * soft_float, axis=-1, keepdims=True))
    d_scores = (soft_float * (d_soft - delta) * (1.0 / math.sqrt(HEAD))).astype(jnp.bfloat16).astype(jnp.float32)
    d_query = jnp.einsum('hqk,khd->qhd', d_scores, heads_of(key_rows)).reshape(rows, HW)
    d_keys = jnp.einsum('hqk,qhd->khd', d_scores, heads_of(queries)).reshape(rows, HW)
    d_values = jnp.einsum('hqk,qhd->khd', soft_weights.astype(jnp.float32), heads_of(d_context)).reshape(rows, HW)
    d_triple = jnp.concatenate([d_query, d_keys, d_values], axis=1).astype(jnp.bfloat16)
    input_grad = (d_first + by_transpose(d_triple, prm['triple_weight'])).astype(jnp.bfloat16)
    grad_list = [inner_rows(tokens, d_triple), inner_rows(context, d_first_b), inner_rows(middle_b, d_pre_b), inner_rows(activated, d_second_b), lax.optimization_barrier(jnp.sum(d_query, axis=0)), lax.optimization_barrier(jnp.sum(d_values, axis=0)), lax.optimization_barrier(jnp.sum(d_first, axis=0)), lax.optimization_barrier(jnp.sum(d_middle * normed_one, axis=0)), lax.optimization_barrier(jnp.sum(d_middle, axis=0)), lax.optimization_barrier(jnp.sum(d_pre, axis=0)), lax.optimization_barrier(jnp.sum(d_second, axis=0)), lax.optimization_barrier(jnp.sum(grad_out * normed_two, axis=0)), lax.optimization_barrier(jnp.sum(grad_out, axis=0))]
    flat_grad = jnp.concatenate([piece_grad.reshape(-1) for piece_grad in grad_list])
    return (input_grad, flat_grad)

def adamw(param_now, first_now, second_now, grad_total):
    first_new = beta_one * first_now + (1.0 - beta_one) * grad_total
    second_new = beta_two * second_now + (1.0 - beta_two) * grad_total * grad_total
    fix_one = 1.0 - beta_one ** STEP
    fix_two = 1.0 - beta_two ** STEP
    param_new = param_now - learn_rate * (first_new / fix_one / (jnp.sqrt(second_new / fix_two) + adam_eps) + decay_rate * param_now)
    return (param_new, first_new, second_new)

def reference(hidden_states, cotangent, lengths, params, first_moment, second_moment):
    prm = split_flat(params.astype(jnp.bfloat16))
    seq_tokens = hidden_states.reshape(SEQS, TOK_DEV, D)
    seq_cot = cotangent.reshape(SEQS, TOK_DEV, D)

    def per_sequence(total, inputs):
        tokens, cot_rows, length = inputs
        block_out, kept = forward(tokens, length, prm)
        input_grad, flat_grad = backward(tokens, length, cot_rows, kept, prm)
        return (total + flat_grad, (block_out, input_grad))
    weight_grad, (outs, grads_in) = lax.scan(per_sequence, jnp.zeros((PARAMS,), jnp.float32), (seq_tokens, seq_cot, lengths))
    new_params, new_first, new_second = adamw(params, first_moment, second_moment, weight_grad)
    return (outs.reshape(TOKENS, D), grads_in.reshape(TOKENS, D), weight_grad, new_params, new_first, new_second)
```

```python
import math

import jax
import jax.numpy as jnp
from jax import lax
from jax.experimental import pallas as pl
from jax.experimental.pallas import tpu as pltpu
from jax.sharding import PartitionSpec as P

D = 768
HEADS = 12
HEAD = 64
FF = 3072
STEP = 3
HW = 768


norm_eps = 1e-05
adam_eps = 1e-06
beta_one = 0.9
beta_two = 0.98
learn_rate = 0.01
decay_rate = 0.01
masked_score = -1e30
inv_sqrt_two = 1.0 / math.sqrt(2.0)
inv_sqrt_tau = 1.0 / math.sqrt(2.0 * math.pi)


def layout():
    return [
        ("triple_weight", (D, 3 * HW)),
        ("output_weight", (HW, D)),
        ("expand_weight", (D, FF)),
        ("reduce_weight", (FF, D)),
        ("query_bias", (HW,)),
        ("value_bias", (HW,)),
        ("output_bias", (D,)),
        ("first_gain", (D,)),
        ("first_shift", (D,)),
        ("expand_bias", (FF,)),
        ("reduce_bias", (D,)),
        ("second_gain", (D,)),
        ("second_shift", (D,)),
    ]


def split_flat(flat_vector):
    pieces = {}
    offset = 0
    for entry_name, dims_of in layout():
        amount = math.prod(dims_of)
        pieces[entry_name] = flat_vector[offset : offset + amount].reshape(dims_of)
        offset = offset + amount
    return pieces


def inner_rows(left_side, right_side):
    return lax.dot_general(
        left_side, right_side, (((0,), (0,)), ((), ())), preferred_element_type=jnp.float32
    )


def by_transpose(left_side, right_side):
    return lax.dot_general(
        left_side, right_side, (((1,), (1,)), ((), ())), preferred_element_type=jnp.float32
    )


def heads_of(row_block):
    return row_block.reshape(row_block.shape[0], HEADS, HEAD)


def normalize(values_in):
    centered = values_in - jnp.mean(values_in, axis=-1, keepdims=True)
    inv_root = lax.rsqrt(jnp.mean(centered * centered, axis=-1, keepdims=True) + norm_eps)
    return (centered * inv_root, inv_root)


def norm_back(grad_in, normed, inv_root):
    return inv_root * (
        grad_in
        - jnp.mean(grad_in, axis=-1, keepdims=True)
        - normed * jnp.mean(grad_in * normed, axis=-1, keepdims=True)
    )


def gelu_slope(pre_act):
    return (
        0.5 * (1.0 + lax.erf(pre_act * inv_sqrt_two))
        + pre_act * jnp.exp(-0.5 * pre_act * pre_act) * inv_sqrt_tau
    )


def attention_scores(queries, key_rows, length):
    scores = jnp.einsum(
        "qhd,khd->hqk", heads_of(queries), heads_of(key_rows), preferred_element_type=jnp.float32
    ) * (1.0 / math.sqrt(HEAD))
    key_valid = jnp.arange(scores.shape[-1]) < length
    return jnp.where(key_valid, scores, masked_score)


def forward(tokens, length, prm):
    rows = tokens.shape[0]
    triple = jnp.dot(tokens, prm["triple_weight"], preferred_element_type=jnp.float32)
    queries = (triple[:, :HW] + prm["query_bias"].astype(jnp.float32)).astype(jnp.bfloat16)
    key_rows = triple[:, HW : 2 * HW].astype(jnp.bfloat16)
    value_rows = (triple[:, 2 * HW :] + prm["value_bias"].astype(jnp.float32)).astype(jnp.bfloat16)
    scores = attention_scores(queries, key_rows, length)
    top_score = jnp.max(scores, axis=-1, keepdims=True)
    log_total = top_score + jnp.log(jnp.sum(jnp.exp(scores - top_score), axis=-1, keepdims=True))
    soft_weights = jnp.exp(scores - log_total).astype(jnp.bfloat16)
    context = jnp.einsum(
        "hqk,khd->qhd", soft_weights, heads_of(value_rows), preferred_element_type=jnp.float32
    )
    context = context.reshape(rows, HW).astype(jnp.bfloat16)
    first_sum = (
        tokens.astype(jnp.float32)
        + jnp.dot(context, prm["output_weight"], preferred_element_type=jnp.float32)
        + prm["output_bias"].astype(jnp.float32)
    )
    normed_one, root_one = normalize(first_sum)
    middle = normed_one * prm["first_gain"].astype(jnp.float32) + prm["first_shift"].astype(
        jnp.float32
    )
    middle_b = middle.astype(jnp.bfloat16)
    pre_act = jnp.dot(middle_b, prm["expand_weight"], preferred_element_type=jnp.float32) + prm[
        "expand_bias"
    ].astype(jnp.float32)
    activated = (0.5 * pre_act * (1.0 + lax.erf(pre_act * inv_sqrt_two))).astype(jnp.bfloat16)
    second_sum = (
        middle
        + jnp.dot(activated, prm["reduce_weight"], preferred_element_type=jnp.float32)
        + prm["reduce_bias"].astype(jnp.float32)
    )
    normed_two, root_two = normalize(second_sum)
    block_out = (
        normed_two * prm["second_gain"].astype(jnp.float32)
        + prm["second_shift"].astype(jnp.float32)
    ).astype(jnp.bfloat16)
    kept = (
        queries,
        key_rows,
        value_rows,
        log_total,
        context,
        normed_one,
        root_one,
        middle_b,
        pre_act,
        activated,
        normed_two,
        root_two,
    )
    return (block_out, kept)


def backward(tokens, length, cotangent, kept, prm):
    (
        queries,
        key_rows,
        value_rows,
        log_total,
        context,
        normed_one,
        root_one,
        middle_b,
        pre_act,
        activated,
        normed_two,
        root_two,
    ) = kept
    rows = tokens.shape[0]
    grad_out = cotangent.astype(jnp.float32)
    d_second = norm_back(grad_out * prm["second_gain"].astype(jnp.float32), normed_two, root_two)
    d_second_b = d_second.astype(jnp.bfloat16)
    d_pre = by_transpose(d_second_b, prm["reduce_weight"]) * gelu_slope(pre_act)
    d_pre_b = d_pre.astype(jnp.bfloat16)
    d_middle = d_second + by_transpose(d_pre_b, prm["expand_weight"])
    d_first = norm_back(d_middle * prm["first_gain"].astype(jnp.float32), normed_one, root_one)
    d_first_b = d_first.astype(jnp.bfloat16)
    d_context = by_transpose(d_first_b, prm["output_weight"]).astype(jnp.bfloat16)
    scores = attention_scores(queries, key_rows, length)
    soft_float = jnp.exp(scores - log_total)
    soft_weights = soft_float.astype(jnp.bfloat16)
    d_soft = jnp.einsum(
        "qhd,khd->hqk",
        heads_of(d_context),
        heads_of(value_rows),
        preferred_element_type=jnp.float32,
    )
    delta = jnp.sum(d_soft * soft_float, axis=-1, keepdims=True)
    d_scores = (soft_float * (d_soft - delta) * (1.0 / math.sqrt(HEAD))).astype(jnp.bfloat16)
    d_query = jnp.einsum(
        "hqk,khd->qhd", d_scores, heads_of(key_rows), preferred_element_type=jnp.float32
    ).reshape(rows, HW)
    d_keys = jnp.einsum(
        "hqk,qhd->khd", d_scores, heads_of(queries), preferred_element_type=jnp.float32
    ).reshape(rows, HW)
    d_values = jnp.einsum(
        "hqk,qhd->khd", soft_weights, heads_of(d_context), preferred_element_type=jnp.float32
    ).reshape(rows, HW)
    d_triple = jnp.concatenate([d_query, d_keys, d_values], axis=1).astype(jnp.bfloat16)
    input_grad = (d_first + by_transpose(d_triple, prm["triple_weight"])).astype(jnp.bfloat16)
    grad_list = [
        inner_rows(tokens, d_triple),
        inner_rows(context, d_first_b),
        inner_rows(middle_b, d_pre_b),
        inner_rows(activated, d_second_b),
        jnp.sum(d_query, axis=0),
        jnp.sum(d_values, axis=0),
        jnp.sum(d_first, axis=0),
        jnp.sum(d_middle * normed_one, axis=0),
        jnp.sum(d_middle, axis=0),
        jnp.sum(d_pre, axis=0),
        jnp.sum(d_second, axis=0),
        jnp.sum(grad_out * normed_two, axis=0),
        jnp.sum(grad_out, axis=0),
    ]
    flat_grad = jnp.concatenate([piece_grad.reshape(-1) for piece_grad in grad_list])
    return (input_grad, flat_grad)


def adamw(param_now, first_now, second_now, grad_total):
    first_new = beta_one * first_now + (1.0 - beta_one) * grad_total
    second_new = beta_two * second_now + (1.0 - beta_two) * grad_total * grad_total
    fix_one = 1.0 - beta_one**STEP
    fix_two = 1.0 - beta_two**STEP
    param_new = param_now - learn_rate * (
        first_new / fix_one / (jnp.sqrt(second_new / fix_two) + adam_eps) + decay_rate * param_now
    )
    return (param_new, first_new, second_new)

ROW = 768
STEP_ROWS = 576
FRAME = 592
HALF = ROW // 2
LINES = FRAME * 6
LOCAL = 442944
LOCAL_LINES = 3464
ROWS = 16 * STEP_ROWS + 16
OUT_ROW = 2304
EXP_ROW = 3072
RED_ROW = 6144
BIAS_ROW = 9216
VMEM_CAP = 64 * 1024 * 1000

f32 = jnp.float32
bf16 = jnp.bfloat16


def swap_half(block):
    return pltpu.roll(block, 64, 1)


def frame_kernel(meta, flat_ref, out_ref, lines, framed):
    shift, odd, first_col = meta[0], meta[1], meta[2]
    lines[0:8, :] = jnp.zeros((8, 128), f32)
    lines[8 : 8 + LOCAL_LINES, :] = flat_ref[...]
    framed[0:96, :] = jnp.zeros((96, 128), f32)
    framed[LINES - 96 : LINES, :] = jnp.zeros((96, 128), f32)
    low = lax.broadcasted_iota(jnp.int32, (LOCAL_LINES, 128), 1) < 64
    here = lines[8 : 8 + LOCAL_LINES, :]
    before = lines[7 : 7 + LOCAL_LINES, :]
    moved = jnp.where(low, swap_half(before), swap_half(here))
    framed[pl.ds(shift, LOCAL_LINES), :] = jnp.where(odd == 1, moved, here)
    for j in range(3):
        column = framed[pl.ds(first_col + j, FRAME, stride=6), :]
        out_ref[:, 128 * j : 128 * (j + 1)] = column.astype(bf16)


def make_frame(params, meta):
    flat = jnp.pad(params, (0, LOCAL_LINES * 128 - LOCAL)).reshape(LOCAL_LINES, 128)
    return pl.pallas_call(
        frame_kernel,
        out_shape=jax.ShapeDtypeStruct((FRAME, HALF), bf16),
        in_specs=[
            pl.BlockSpec(memory_space=pltpu.SMEM),
            pl.BlockSpec(memory_space=pltpu.VMEM),
        ],
        out_specs=pl.BlockSpec(memory_space=pltpu.VMEM),
        scratch_shapes=[
            pltpu.VMEM((LOCAL_LINES + 16, 128), f32),
            pltpu.VMEM((LINES, 128), f32),
        ],
    )(meta, flat)


def unframe_kernel(meta, mine_ref, other_ref, out_ref, framed):
    shift, odd, first_col, other_col = meta[0], meta[1], meta[2], meta[3]
    for j in range(3):
        framed[pl.ds(first_col + j, FRAME, stride=6), :] = mine_ref[:, 128 * j : 128 * (j + 1)]
        framed[pl.ds(other_col + j, FRAME, stride=6), :] = other_ref[:, 128 * j : 128 * (j + 1)]
    low = lax.broadcasted_iota(jnp.int32, (LOCAL_LINES, 128), 1) < 64
    here = framed[pl.ds(shift, LOCAL_LINES), :]
    after = framed[pl.ds(shift + 1, LOCAL_LINES), :]
    moved = jnp.where(low, swap_half(here), swap_half(after))
    out_ref[...] = jnp.where(odd == 1, moved, here)


def take_frame(mine, other, meta):
    lines = pl.pallas_call(
        unframe_kernel,
        out_shape=jax.ShapeDtypeStruct((LOCAL_LINES, 128), f32),
        in_specs=[
            pl.BlockSpec(memory_space=pltpu.SMEM),
            pl.BlockSpec(memory_space=pltpu.VMEM),
            pl.BlockSpec(memory_space=pltpu.VMEM),
        ],
        out_specs=pl.BlockSpec(memory_space=pltpu.VMEM),
        scratch_shapes=[pltpu.VMEM((LINES + 8, 128), f32)],
    )(meta, mine, other)
    return lines.reshape(LOCAL_LINES * 128)[:LOCAL]


def dot_nn(left_side, right_side):
    return jnp.dot(left_side, right_side, preferred_element_type=f32)


def row_mean(block):
    return jnp.mean(block, axis=-1, keepdims=True)


def layer_kernel(meta, tokens_ref, cot_ref, *refs):
    frames = refs[:32]
    block_ref, input_ref = refs[32:34]
    keeps = refs[34:38]
    sends = refs[38:42]
    (
        weights,
        grads,
        triple_w,
        expand_w,
        tails,
        stage,
        triple_b,
        soft_all,
        context_b,
        act_b,
        slope_all,
        pre_b,
        d_triple_b,
        bias_grads,
        sem_main,
        sem_tail,
        sem_out,
    ) = refs[42:]
    length = meta[0]
    cols = (pl.multiple_of(meta[1], 128), pl.multiple_of(meta[2], 128))

    arrivals = []
    for side in range(2):
        for k in range(16):
            frame = frames[16 * side + k]
            shard = meta[3 + 16 * side + k]
            row = pl.multiple_of(shard * STEP_ROWS, 16)
            main_copy = pltpu.make_async_copy(
                frame.at[pl.ds(0, STEP_ROWS), :],
                weights.at[pl.ds(row, STEP_ROWS), pl.ds(cols[side], HALF)],
                sem_main.at[side, k],
            )
            tail_copy = pltpu.make_async_copy(
                frame.at[pl.ds(STEP_ROWS, 16), :],
                tails.at[shard, :, pl.ds(cols[side], HALF)],
                sem_tail.at[side, k],
            )
            main_copy.start()
            tail_copy.start()
            arrivals.append(main_copy)
            arrivals.append(tail_copy)
    for copy in arrivals:
        copy.wait()
    for s in range(15):
        at = STEP_ROWS * (s + 1)
        joined = weights[at : at + 16, :].astype(f32) + tails[s].astype(f32)
        weights[at : at + 16, :] = joined.astype(bf16)
    weights[BIAS_ROW : BIAS_ROW + 16, :] = tails[15]

    def spread_triple(i, carry):
        for j in range(6):
            at = slice(128 * j, 128 * (j + 1))
            stage[j, 0:384, :] = weights[pl.ds(pl.multiple_of(384 * i, 16), 384), at].astype(f32)
            for part in range(3):
                rows = stage[j, pl.ds(part, 128, stride=3), :]
                triple_w[part, pl.ds(pl.multiple_of(128 * i, 16), 128), at] = rows.astype(bf16)
        return carry

    lax.fori_loop(0, 6, spread_triple, 0)

    def spread_expand(i, carry):
        row = pl.multiple_of(EXP_ROW + 512 * i, 16)
        for j in range(6):
            at = slice(128 * j, 128 * (j + 1))
            stage[j, :, :] = weights[pl.ds(row, 512), at].astype(f32)
            for part in range(4):
                rows = stage[j, pl.ds(part, 128, stride=4), :]
                expand_w[part, pl.ds(pl.multiple_of(128 * i, 16), 128), at] = rows.astype(bf16)
        return carry

    lax.fori_loop(0, 6, spread_expand, 0)

    biases = weights[BIAS_ROW : BIAS_ROW + 16, :].astype(f32)

    def bias(index):
        return biases[index : index + 1, :]

    bias_grads[...] = jnp.zeros((16, ROW), f32)

    def keep_bias(index, block):
        bias_grads[index : index + 1, :] = jnp.sum(block, axis=0, keepdims=True)

    tokens = tokens_ref[...]
    triple_b[0] = (dot_nn(tokens, triple_w[0]) + bias(0)).astype(bf16)
    triple_b[1] = dot_nn(tokens, triple_w[1]).astype(bf16)
    triple_b[2] = (dot_nn(tokens, triple_w[2]) + bias(1)).astype(bf16)

    lane = lax.broadcasted_iota(jnp.int32, (1, 128), 1)
    head_masks = ((lane < 64).astype(f32).astype(bf16), (lane >= 64).astype(f32).astype(bf16))
    key_valid = lax.broadcasted_iota(jnp.int32, (128, 128), 1) < length
    scale = 1.0 / math.sqrt(HEAD)
    for pair in range(6):
        at = slice(128 * pair, 128 * (pair + 1))
        queries, key_rows, value_rows = triple_b[0, :, at], triple_b[1, :, at], triple_b[2, :, at]
        context = jnp.zeros((128, 128), f32)
        for side in range(2):
            scores = by_transpose(queries * head_masks[side], key_rows) * scale
            scores = jnp.where(key_valid, scores, masked_score)
            top_score = jnp.max(scores, axis=-1, keepdims=True)
            log_total = top_score + jnp.log(
                jnp.sum(jnp.exp(scores - top_score), axis=-1, keepdims=True)
            )
            soft_float = jnp.exp(scores - log_total)
            soft_all[2 * pair + side] = soft_float
            context = context + dot_nn(soft_float.astype(bf16), value_rows * head_masks[side])
        context_b[:, at] = context.astype(bf16)

    first_sum = tokens.astype(f32) + dot_nn(context_b[...], weights[OUT_ROW : OUT_ROW + 768, :]) + bias(2)
    normed_one, root_one = normalize(first_sum)
    middle = normed_one * bias(3) + bias(4)
    middle_b = middle.astype(bf16)
    second_sum = middle + bias(9)
    for part in range(4):
        at = slice(768 * part, 768 * (part + 1))
        pre_act = dot_nn(middle_b, expand_w[part]) + bias(5 + part)
        erf_term = 1.0 + lax.erf(pre_act * inv_sqrt_two)
        activated = (0.5 * pre_act * erf_term).astype(bf16)
        act_b[:, at] = activated
        slope_all[:, at] = 0.5 * erf_term + pre_act * jnp.exp(-0.5 * pre_act * pre_act) * inv_sqrt_tau
        red_at = RED_ROW + 768 * part
        second_sum = second_sum + dot_nn(activated, weights[red_at : red_at + 768, :])
    normed_two, root_two = normalize(second_sum)
    block_ref[...] = (normed_two * bias(10) + bias(11)).astype(bf16)

    grad_out = cot_ref[...].astype(f32)
    keep_bias(10, grad_out * normed_two)
    keep_bias(11, grad_out)
    d_second = norm_back(grad_out * bias(10), normed_two, root_two)
    keep_bias(9, d_second)
    d_second_b = d_second.astype(bf16)
    d_middle = d_second
    for part in range(4):
        at = slice(768 * part, 768 * (part + 1))
        red_at = RED_ROW + 768 * part
        d_pre = by_transpose(d_second_b, weights[red_at : red_at + 768, :]) * slope_all[:, at]
        keep_bias(5 + part, d_pre)
        d_pre_b = d_pre.astype(bf16)
        pre_b[:, at] = d_pre_b
        d_middle = d_middle + by_transpose(d_pre_b, expand_w[part])

    def reduce_grad(i, carry):
        at = pl.multiple_of(256 * i, 256)
        block = inner_rows(act_b[:, pl.ds(at, 256)], d_second_b)
        grads[pl.ds(pl.multiple_of(RED_ROW + at, 16), 256), :] = block.astype(bf16)
        return carry

    lax.fori_loop(0, 12, reduce_grad, 0)

    act_b[:, 0:768] = middle_b

    def expand_grad(i, carry):
        left = act_b[:, pl.ds(pl.multiple_of(128 * i, 128), 128)]
        for part in range(4):
            block = inner_rows(left, pre_b[:, 768 * part : 768 * (part + 1)])
            for j in range(6):
                stage[j, pl.ds(part, 128, stride=4), :] = block[:, 128 * j : 128 * (j + 1)]
        row = pl.multiple_of(EXP_ROW + 512 * i, 16)
        for j in range(6):
            grads[pl.ds(row, 512), 128 * j : 128 * (j + 1)] = stage[j].astype(bf16)
        return carry

    lax.fori_loop(0, 6, expand_grad, 0)

    keep_bias(3, d_middle * normed_one)
    keep_bias(4, d_middle)
    d_first = norm_back(d_middle * bias(3), normed_one, root_one)
    keep_bias(2, d_first)
    d_first_b = d_first.astype(bf16)
    d_context_b = by_transpose(d_first_b, weights[OUT_ROW : OUT_ROW + 768, :]).astype(bf16)

    def output_grad(i, carry):
        at = pl.multiple_of(256 * i, 256)
        block = inner_rows(context_b[:, pl.ds(at, 256)], d_first_b)
        grads[pl.ds(pl.multiple_of(OUT_ROW + at, 16), 256), :] = block.astype(bf16)
        return carry

    lax.fori_loop(0, 3, output_grad, 0)

    for pair in range(6):
        at = slice(128 * pair, 128 * (pair + 1))
        queries, key_rows, value_rows = triple_b[0, :, at], triple_b[1, :, at], triple_b[2, :, at]
        d_context = d_context_b[:, at]
        d_query = jnp.zeros((128, 128), f32)
        d_keys = jnp.zeros((128, 128), f32)
        d_values = jnp.zeros((128, 128), f32)
        for side in range(2):
            soft_float = soft_all[2 * pair + side]
            d_part = d_context * head_masks[side]
            d_soft = by_transpose(d_part, value_rows)
            delta = jnp.sum(d_soft * soft_float, axis=-1, keepdims=True)
            d_scores = (soft_float * (d_soft - delta) * scale).astype(bf16)
            d_query = d_query + dot_nn(d_scores, key_rows * head_masks[side])
            d_keys = d_keys + inner_rows(d_scores, queries * head_masks[side])
            d_values = d_values + inner_rows(soft_float.astype(bf16), d_part)
        bias_grads[0:1, at] = jnp.sum(d_query, axis=0, keepdims=True)
        bias_grads[1:2, at] = jnp.sum(d_values, axis=0, keepdims=True)
        d_triple_b[0, :, at] = d_query.astype(bf16)
        d_triple_b[1, :, at] = d_keys.astype(bf16)
        d_triple_b[2, :, at] = d_values.astype(bf16)

    input_grad = d_first
    for part in range(3):
        input_grad = input_grad + by_transpose(d_triple_b[part], triple_w[part])
    input_ref[...] = input_grad.astype(bf16)

    def triple_grad(i, carry):
        left = tokens_ref[:, pl.ds(pl.multiple_of(128 * i, 128), 128)]
        for part in range(3):
            block = inner_rows(left, d_triple_b[part])
            for j in range(6):
                stage[j, pl.ds(part, 128, stride=3), :] = block[:, 128 * j : 128 * (j + 1)]
        row = pl.multiple_of(384 * i, 16)
        for j in range(6):
            grads[pl.ds(row, 384), 128 * j : 128 * (j + 1)] = stage[j, 0:384, :].astype(bf16)
        return carry

    lax.fori_loop(0, 6, triple_grad, 0)
    grads[BIAS_ROW : BIAS_ROW + 16, :] = bias_grads[...].astype(bf16)

    departures = []
    for side in range(2):
        for k in range(16):
            shard = meta[3 + 16 * side + k]
            row = pl.multiple_of(shard * STEP_ROWS, 16)
            target = (keeps if side == 0 else sends)[k // 4]
            copy = pltpu.make_async_copy(
                grads.at[pl.ds(row, FRAME), pl.ds(cols[side], HALF)],
                target.at[k % 4],
                sem_out.at[side, k],
            )
            copy.start()
            departures.append(copy)
    for copy in departures:
        copy.wait()


def run_layer(meta, tokens, cotangent, frames):
    any_spec = pl.BlockSpec(memory_space=pl.ANY)
    vmem_spec = pl.BlockSpec(memory_space=pltpu.VMEM)
    rows = tokens.shape[0]
    out = pl.pallas_call(
        layer_kernel,
        out_shape=[jax.ShapeDtypeStruct((rows, D), bf16)] * 2
        + [jax.ShapeDtypeStruct((4, FRAME, HALF), bf16)] * 8,
        in_specs=[pl.BlockSpec(memory_space=pltpu.SMEM), vmem_spec, vmem_spec] + [any_spec] * 32,
        out_specs=[vmem_spec] * 2 + [any_spec] * 8,
        scratch_shapes=[
            pltpu.VMEM((ROWS, ROW), bf16),
            pltpu.VMEM((ROWS, ROW), bf16),
            pltpu.VMEM((3, D, HW), bf16),
            pltpu.VMEM((4, D, ROW), bf16),
            pltpu.VMEM((16, 16, ROW), bf16),
            pltpu.VMEM((6, 512, 128), f32),
            pltpu.VMEM((3, rows, HW), bf16),
            pltpu.VMEM((HEADS, rows, rows), f32),
            pltpu.VMEM((rows, HW), bf16),
            pltpu.VMEM((rows, FF), bf16),
            pltpu.VMEM((rows, FF), f32),
            pltpu.VMEM((rows, FF), bf16),
            pltpu.VMEM((3, rows, HW), bf16),
            pltpu.VMEM((16, ROW), f32),
            pltpu.SemaphoreType.DMA((2, 16)),
            pltpu.SemaphoreType.DMA((2, 16)),
            pltpu.SemaphoreType.DMA((2, 16)),
        ],
        compiler_params=pltpu.CompilerParams(vmem_limit_bytes=VMEM_CAP),
    )(meta, tokens, cotangent, *frames)
    return out[0], out[1], out[2:6], out[6:10]


def plane_moves(n):
    near, far = [], []
    for s in range(n):
        near += [(s, s ^ 1), (n + s, n + (s ^ 2))]
        far += [(s, s ^ 2), (n + s, n + (s ^ 1))]
    return near, far


def on_device_planes(hidden_states, cotangent, lengths, params, first_moment, second_moment):
    n = 16
    both = ("rep", "shard")
    near, far = plane_moves(n)
    swap = [(0, 1), (1, 0)]
    core = lax.axis_index("rep")
    here = lax.axis_index("shard")
    plane, spot = here // 4, here % 4
    shift, odd = (9 * here) // 2, here % 2
    shape_meta = jnp.stack([shift, odd, 3 * core, 3 - 3 * core]).astype(jnp.int32)
    spots = jnp.array([[0, 1, 2, 3], [0, 2, 1, 3]], jnp.int32)
    slots = jnp.arange(4, dtype=jnp.int32)
    base = ((plane - slots) % 4)[:, None] * 4
    mine_at = base + (spot ^ spots[core])[None, :]
    other_at = base + (spot ^ spots[1 - core])[None, :]
    layer_meta = jnp.concatenate(
        [
            jnp.stack([lengths[0], HALF * core, HALF - HALF * core]).astype(jnp.int32),
            mine_at.reshape(-1),
            other_at.reshape(-1),
        ]
    ).astype(jnp.int32)

    own = make_frame(params, shape_meta)
    mine, other = [], []
    for t in range(4):
        zero = own if t == 0 else lax.ppermute(own, "shard", [(s, (s + 4 * t) % n) for s in range(n)])
        one = lax.ppermute(zero, both, near)
        two = lax.ppermute(zero, both, far)
        three = lax.ppermute(one, both, far)
        group = [zero, one, two, three]
        mine += group
        other += [lax.ppermute(piece, "rep", swap) for piece in group]

    block_out, input_grad, keeps, sends = run_layer(layer_meta, hidden_states, cotangent, mine + other)

    total = None
    for t in range(4):
        keep = keeps[t].astype(f32)
        got = lax.ppermute(sends[t], "rep", swap).astype(f32)
        away = (keep[2:4] + got[2:4]).astype(bf16)
        from_far = lax.ppermute(away, both, far).astype(f32)
        away = (keep[1] + got[1] + from_far[1]).astype(bf16)
        from_near = lax.ppermute(away, both, near).astype(f32)
        partial = keep[0] + got[0] + from_far[0] + from_near
        if t > 0:
            partial = lax.ppermute(
                partial.astype(bf16), "shard", [(s, (s - 4 * t) % n) for s in range(n)]
            ).astype(f32)
        total = partial if total is None else total + partial
    weight_grad = take_frame(total, lax.ppermute(total, "rep", swap), shape_meta)
    new_params, new_first, new_second = adamw(params, first_moment, second_moment, weight_grad)
    return (block_out, input_grad, weight_grad, new_params, new_first, new_second)


def on_device_any(hidden_states, cotangent, lengths, params, first_moment, second_moment):
    length = lengths[0]
    gathered = lax.all_gather(params.astype(jnp.bfloat16), "shard", axis=0, tiled=True)
    prm = split_flat(gathered)
    block_out, kept = forward(hidden_states, length, prm)
    input_grad, flat_grad = backward(hidden_states, length, cotangent, kept, prm)
    owned = lax.psum_scatter(flat_grad, "shard", scatter_dimension=0, tiled=True)
    weight_grad = lax.psum(owned, "rep")
    new_params, new_first, new_second = adamw(params, first_moment, second_moment, weight_grad)
    return (block_out, input_grad, weight_grad, new_params, new_first, new_second)


def solution(mesh):
    placed = (
        P(("rep", "shard"), None),
        P(("rep", "shard"), None),
        P(("rep", "shard")),
        P("shard"),
        P("shard"),
        P("shard"),
    )
    sixteen = mesh.shape["shard"] == 16 and mesh.shape["rep"] == 2
    return jax.shard_map(
        on_device_planes if sixteen else on_device_any,
        mesh=mesh,
        in_specs=placed,
        out_specs=(
            P(("rep", "shard"), None),
            P(("rep", "shard"), None),
            P("shard"),
            P("shard"),
            P("shard"),
            P("shard"),
        ),
        check_vma=False,
    )
```

```python
import math

import jax
import jax.numpy as jnp
from jax import lax
from jax.experimental import pallas as pl
from jax.experimental.pallas import tpu as pltpu
from jax.sharding import PartitionSpec as P

D = 768
HEADS = 12
HEAD = 64
FF = 3072
STEP = 3
HW = 768


norm_eps = 1e-05
adam_eps = 1e-06
beta_one = 0.9
beta_two = 0.98
learn_rate = 0.01
decay_rate = 0.01
masked_score = -1e30
inv_sqrt_two = 1.0 / math.sqrt(2.0)
inv_sqrt_tau = 1.0 / math.sqrt(2.0 * math.pi)


def layout():
    return [
        ("triple_weight", (D, 3 * HW)),
        ("output_weight", (HW, D)),
        ("expand_weight", (D, FF)),
        ("reduce_weight", (FF, D)),
        ("query_bias", (HW,)),
        ("value_bias", (HW,)),
        ("output_bias", (D,)),
        ("first_gain", (D,)),
        ("first_shift", (D,)),
        ("expand_bias", (FF,)),
        ("reduce_bias", (D,)),
        ("second_gain", (D,)),
        ("second_shift", (D,)),
    ]


def split_flat(flat_vector):
    pieces = {}
    offset = 0
    for entry_name, dims_of in layout():
        amount = math.prod(dims_of)
        pieces[entry_name] = flat_vector[offset : offset + amount].reshape(dims_of)
        offset = offset + amount
    return pieces


def inner_rows(left_side, right_side):
    return lax.dot_general(
        left_side, right_side, (((0,), (0,)), ((), ())), preferred_element_type=jnp.float32
    )


def by_transpose(left_side, right_side):
    return lax.dot_general(
        left_side, right_side, (((1,), (1,)), ((), ())), preferred_element_type=jnp.float32
    )


def heads_of(row_block):
    return row_block.reshape(row_block.shape[0], HEADS, HEAD)


def normalize(values_in):
    centered = values_in - jnp.mean(values_in, axis=-1, keepdims=True)
    inv_root = lax.rsqrt(jnp.mean(centered * centered, axis=-1, keepdims=True) + norm_eps)
    return (centered * inv_root, inv_root)


def norm_back(grad_in, normed, inv_root):
    return inv_root * (
        grad_in
        - jnp.mean(grad_in, axis=-1, keepdims=True)
        - normed * jnp.mean(grad_in * normed, axis=-1, keepdims=True)
    )


def gelu_slope(pre_act):
    return (
        0.5 * (1.0 + lax.erf(pre_act * inv_sqrt_two))
        + pre_act * jnp.exp(-0.5 * pre_act * pre_act) * inv_sqrt_tau
    )


def attention_scores(queries, key_rows, length):
    scores = jnp.einsum(
        "qhd,khd->hqk", heads_of(queries), heads_of(key_rows), preferred_element_type=jnp.float32
    ) * (1.0 / math.sqrt(HEAD))
    key_valid = jnp.arange(scores.shape[-1]) < length
    return jnp.where(key_valid, scores, masked_score)


def forward(tokens, length, prm):
    rows = tokens.shape[0]
    triple = jnp.dot(tokens, prm["triple_weight"], preferred_element_type=jnp.float32)
    queries = (triple[:, :HW] + prm["query_bias"].astype(jnp.float32)).astype(jnp.bfloat16)
    key_rows = triple[:, HW : 2 * HW].astype(jnp.bfloat16)
    value_rows = (triple[:, 2 * HW :] + prm["value_bias"].astype(jnp.float32)).astype(jnp.bfloat16)
    scores = attention_scores(queries, key_rows, length)
    top_score = jnp.max(scores, axis=-1, keepdims=True)
    log_total = top_score + jnp.log(jnp.sum(jnp.exp(scores - top_score), axis=-1, keepdims=True))
    soft_weights = jnp.exp(scores - log_total).astype(jnp.bfloat16)
    context = jnp.einsum(
        "hqk,khd->qhd", soft_weights, heads_of(value_rows), preferred_element_type=jnp.float32
    )
    context = context.reshape(rows, HW).astype(jnp.bfloat16)
    first_sum = (
        tokens.astype(jnp.float32)
        + jnp.dot(context, prm["output_weight"], preferred_element_type=jnp.float32)
        + prm["output_bias"].astype(jnp.float32)
    )
    normed_one, root_one = normalize(first_sum)
    middle = normed_one * prm["first_gain"].astype(jnp.float32) + prm["first_shift"].astype(
        jnp.float32
    )
    middle_b = middle.astype(jnp.bfloat16)
    pre_act = jnp.dot(middle_b, prm["expand_weight"], preferred_element_type=jnp.float32) + prm[
        "expand_bias"
    ].astype(jnp.float32)
    activated = (0.5 * pre_act * (1.0 + lax.erf(pre_act * inv_sqrt_two))).astype(jnp.bfloat16)
    second_sum = (
        middle
        + jnp.dot(activated, prm["reduce_weight"], preferred_element_type=jnp.float32)
        + prm["reduce_bias"].astype(jnp.float32)
    )
    normed_two, root_two = normalize(second_sum)
    block_out = (
        normed_two * prm["second_gain"].astype(jnp.float32)
        + prm["second_shift"].astype(jnp.float32)
    ).astype(jnp.bfloat16)
    kept = (
        queries,
        key_rows,
        value_rows,
        log_total,
        context,
        normed_one,
        root_one,
        middle_b,
        pre_act,
        activated,
        normed_two,
        root_two,
    )
    return (block_out, kept)


def backward(tokens, length, cotangent, kept, prm):
    (
        queries,
        key_rows,
        value_rows,
        log_total,
        context,
        normed_one,
        root_one,
        middle_b,
        pre_act,
        activated,
        normed_two,
        root_two,
    ) = kept
    rows = tokens.shape[0]
    grad_out = cotangent.astype(jnp.float32)
    d_second = norm_back(grad_out * prm["second_gain"].astype(jnp.float32), normed_two, root_two)
    d_second_b = d_second.astype(jnp.bfloat16)
    d_pre = by_transpose(d_second_b, prm["reduce_weight"]) * gelu_slope(pre_act)
    d_pre_b = d_pre.astype(jnp.bfloat16)
    d_middle = d_second + by_transpose(d_pre_b, prm["expand_weight"])
    d_first = norm_back(d_middle * prm["first_gain"].astype(jnp.float32), normed_one, root_one)
    d_first_b = d_first.astype(jnp.bfloat16)
    d_context = by_transpose(d_first_b, prm["output_weight"]).astype(jnp.bfloat16)
    scores = attention_scores(queries, key_rows, length)
    soft_float = jnp.exp(scores - log_total)
    soft_weights = soft_float.astype(jnp.bfloat16)
    d_soft = jnp.einsum(
        "qhd,khd->hqk",
        heads_of(d_context),
        heads_of(value_rows),
        preferred_element_type=jnp.float32,
    )
    delta = jnp.sum(d_soft * soft_float, axis=-1, keepdims=True)
    d_scores = (soft_float * (d_soft - delta) * (1.0 / math.sqrt(HEAD))).astype(jnp.bfloat16)
    d_query = jnp.einsum(
        "hqk,khd->qhd", d_scores, heads_of(key_rows), preferred_element_type=jnp.float32
    ).reshape(rows, HW)
    d_keys = jnp.einsum(
        "hqk,qhd->khd", d_scores, heads_of(queries), preferred_element_type=jnp.float32
    ).reshape(rows, HW)
    d_values = jnp.einsum(
        "hqk,qhd->khd", soft_weights, heads_of(d_context), preferred_element_type=jnp.float32
    ).reshape(rows, HW)
    d_triple = jnp.concatenate([d_query, d_keys, d_values], axis=1).astype(jnp.bfloat16)
    input_grad = (d_first + by_transpose(d_triple, prm["triple_weight"])).astype(jnp.bfloat16)
    grad_list = [
        inner_rows(tokens, d_triple),
        inner_rows(context, d_first_b),
        inner_rows(middle_b, d_pre_b),
        inner_rows(activated, d_second_b),
        jnp.sum(d_query, axis=0),
        jnp.sum(d_values, axis=0),
        jnp.sum(d_first, axis=0),
        jnp.sum(d_middle * normed_one, axis=0),
        jnp.sum(d_middle, axis=0),
        jnp.sum(d_pre, axis=0),
        jnp.sum(d_second, axis=0),
        jnp.sum(grad_out * normed_two, axis=0),
        jnp.sum(grad_out, axis=0),
    ]
    flat_grad = jnp.concatenate([piece_grad.reshape(-1) for piece_grad in grad_list])
    return (input_grad, flat_grad)


def adamw(param_now, first_now, second_now, grad_total):
    first_new = beta_one * first_now + (1.0 - beta_one) * grad_total
    second_new = beta_two * second_now + (1.0 - beta_two) * grad_total * grad_total
    fix_one = 1.0 - beta_one**STEP
    fix_two = 1.0 - beta_two**STEP
    param_new = param_now - learn_rate * (
        first_new / fix_one / (jnp.sqrt(second_new / fix_two) + adam_eps) + decay_rate * param_now
    )
    return (param_new, first_new, second_new)

ROW = 768
STEP_ROWS = 576
FRAME = 592
HALF = ROW // 2
LINES = FRAME * 6
LOCAL = 442944
LOCAL_LINES = 3464
ROWS = 16 * STEP_ROWS + 16
OUT_ROW = 2304
EXP_ROW = 3072
RED_ROW = 6144
BIAS_ROW = 9216
VMEM_CAP = 64 * 1024 * 1000

f32 = jnp.float32
bf16 = jnp.bfloat16


def swap_half(block):
    return pltpu.roll(block, 64, 1)


def frame_kernel(meta, flat_ref, out_ref, lines, framed):
    shift, odd, first_col = meta[0], meta[1], meta[2]
    lines[0:8, :] = jnp.zeros((8, 128), f32)
    lines[8 : 8 + LOCAL_LINES, :] = flat_ref[...]
    framed[0:96, :] = jnp.zeros((96, 128), f32)
    framed[LINES - 96 : LINES, :] = jnp.zeros((96, 128), f32)
    low = lax.broadcasted_iota(jnp.int32, (LOCAL_LINES, 128), 1) < 64
    here = lines[8 : 8 + LOCAL_LINES, :]
    before = lines[7 : 7 + LOCAL_LINES, :]
    moved = jnp.where(low, swap_half(before), swap_half(here))
    framed[pl.ds(shift, LOCAL_LINES), :] = jnp.where(odd == 1, moved, here)
    for j in range(3):
        column = framed[pl.ds(first_col + j, FRAME, stride=6), :]
        out_ref[:, 128 * j : 128 * (j + 1)] = column.astype(bf16)


def make_frame(params, meta):
    flat = jnp.pad(params, (0, LOCAL_LINES * 128 - LOCAL)).reshape(LOCAL_LINES, 128)
    return pl.pallas_call(
        frame_kernel,
        out_shape=jax.ShapeDtypeStruct((FRAME, HALF), bf16),
        in_specs=[
            pl.BlockSpec(memory_space=pltpu.SMEM),
            pl.BlockSpec(memory_space=pltpu.VMEM),
        ],
        out_specs=pl.BlockSpec(memory_space=pltpu.VMEM),
        scratch_shapes=[
            pltpu.VMEM((LOCAL_LINES + 16, 128), f32),
            pltpu.VMEM((LINES, 128), f32),
        ],
    )(meta, flat)


def unframe_kernel(meta, mine_ref, other_ref, out_ref, framed):
    shift, odd, first_col, other_col = meta[0], meta[1], meta[2], meta[3]
    for j in range(3):
        framed[pl.ds(first_col + j, FRAME, stride=6), :] = mine_ref[:, 128 * j : 128 * (j + 1)]
        framed[pl.ds(other_col + j, FRAME, stride=6), :] = other_ref[:, 128 * j : 128 * (j + 1)]
    low = lax.broadcasted_iota(jnp.int32, (LOCAL_LINES, 128), 1) < 64
    here = framed[pl.ds(shift, LOCAL_LINES), :]
    after = framed[pl.ds(shift + 1, LOCAL_LINES), :]
    moved = jnp.where(low, swap_half(here), swap_half(after))
    out_ref[...] = jnp.where(odd == 1, moved, here)


def take_frame(mine, other, meta):
    lines = pl.pallas_call(
        unframe_kernel,
        out_shape=jax.ShapeDtypeStruct((LOCAL_LINES, 128), f32),
        in_specs=[
            pl.BlockSpec(memory_space=pltpu.SMEM),
            pl.BlockSpec(memory_space=pltpu.VMEM),
            pl.BlockSpec(memory_space=pltpu.VMEM),
        ],
        out_specs=pl.BlockSpec(memory_space=pltpu.VMEM),
        scratch_shapes=[pltpu.VMEM((LINES + 8, 128), f32)],
    )(meta, mine, other)
    return lines.reshape(LOCAL_LINES * 128)[:LOCAL]


def dot_nn(left_side, right_side):
    return jnp.dot(left_side, right_side, preferred_element_type=f32)


def row_mean(block):
    return jnp.mean(block, axis=-1, keepdims=True)


def layer_kernel(meta, tokens_ref, cot_ref, *refs):
    frames = refs[:32]
    block_ref, input_ref = refs[32:34]
    keeps = refs[34:38]
    sends = refs[38:42]
    (
        weights,
        grads,
        triple_w,
        expand_w,
        tails,
        stage,
        triple_b,
        soft_all,
        context_b,
        act_b,
        slope_all,
        pre_b,
        d_triple_b,
        bias_grads,
        sem_main,
        sem_tail,
        sem_out,
    ) = refs[42:]
    length = meta[0]
    cols = (pl.multiple_of(meta[1], 128), pl.multiple_of(meta[2], 128))

    arrivals = []
    for side in range(2):
        for k in range(16):
            frame = frames[16 * side + k]
            shard = meta[3 + 16 * side + k]
            row = pl.multiple_of(shard * STEP_ROWS, 16)
            main_copy = pltpu.make_async_copy(
                frame.at[pl.ds(0, STEP_ROWS), :],
                weights.at[pl.ds(row, STEP_ROWS), pl.ds(cols[side], HALF)],
                sem_main.at[side, k],
            )
            tail_copy = pltpu.make_async_copy(
                frame.at[pl.ds(STEP_ROWS, 16), :],
                tails.at[shard, :, pl.ds(cols[side], HALF)],
                sem_tail.at[side, k],
            )
            main_copy.start()
            tail_copy.start()
            arrivals.append(main_copy)
            arrivals.append(tail_copy)
    for copy in arrivals:
        copy.wait()
    for s in range(15):
        at = STEP_ROWS * (s + 1)
        joined = weights[at : at + 16, :].astype(f32) + tails[s].astype(f32)
        weights[at : at + 16, :] = joined.astype(bf16)
    weights[BIAS_ROW : BIAS_ROW + 16, :] = tails[15]

    def spread_triple(i, carry):
        for j in range(6):
            at = slice(128 * j, 128 * (j + 1))
            stage[j, 0:384, :] = weights[pl.ds(pl.multiple_of(384 * i, 16), 384), at].astype(f32)
            for part in range(3):
                rows = stage[j, pl.ds(part, 128, stride=3), :]
                triple_w[part, pl.ds(pl.multiple_of(128 * i, 16), 128), at] = rows.astype(bf16)
        return carry

    lax.fori_loop(0, 6, spread_triple, 0)

    def spread_expand(i, carry):
        row = pl.multiple_of(EXP_ROW + 512 * i, 16)
        for j in range(6):
            at = slice(128 * j, 128 * (j + 1))
            stage[j, :, :] = weights[pl.ds(row, 512), at].astype(f32)
            for part in range(4):
                rows = stage[j, pl.ds(part, 128, stride=4), :]
                expand_w[part, pl.ds(pl.multiple_of(128 * i, 16), 128), at] = rows.astype(bf16)
        return carry

    lax.fori_loop(0, 6, spread_expand, 0)

    biases = weights[BIAS_ROW : BIAS_ROW + 16, :].astype(f32)

    def bias(index):
        return biases[index : index + 1, :]

    bias_grads[...] = jnp.zeros((16, ROW), f32)

    def keep_bias(index, block):
        bias_grads[index : index + 1, :] = jnp.sum(block, axis=0, keepdims=True)

    tokens = tokens_ref[...]
    triple_b[0] = (dot_nn(tokens, triple_w[0]) + bias(0)).astype(bf16)
    triple_b[1] = dot_nn(tokens, triple_w[1]).astype(bf16)
    triple_b[2] = (dot_nn(tokens, triple_w[2]) + bias(1)).astype(bf16)

    lane = lax.broadcasted_iota(jnp.int32, (1, 128), 1)
    head_masks = ((lane < 64).astype(f32).astype(bf16), (lane >= 64).astype(f32).astype(bf16))
    key_valid = lax.broadcasted_iota(jnp.int32, (128, 128), 1) < length
    scale = 1.0 / math.sqrt(HEAD)
    for pair in range(6):
        at = slice(128 * pair, 128 * (pair + 1))
        queries, key_rows, value_rows = triple_b[0, :, at], triple_b[1, :, at], triple_b[2, :, at]
        context = jnp.zeros((128, 128), f32)
        for side in range(2):
            scores = by_transpose(queries * head_masks[side], key_rows) * scale
            scores = jnp.where(key_valid, scores, masked_score)
            top_score = jnp.max(scores, axis=-1, keepdims=True)
            log_total = top_score + jnp.log(
                jnp.sum(jnp.exp(scores - top_score), axis=-1, keepdims=True)
            )
            soft_float = jnp.exp(scores - log_total)
            soft_all[2 * pair + side] = soft_float
            context = context + dot_nn(soft_float.astype(bf16), value_rows * head_masks[side])
        context_b[:, at] = context.astype(bf16)

    first_sum = tokens.astype(f32) + dot_nn(context_b[...], weights[OUT_ROW : OUT_ROW + 768, :]) + bias(2)
    normed_one, root_one = normalize(first_sum)
    middle = normed_one * bias(3) + bias(4)
    middle_b = middle.astype(bf16)
    second_sum = middle + bias(9)
    for part in range(4):
        at = slice(768 * part, 768 * (part + 1))
        pre_act = dot_nn(middle_b, expand_w[part]) + bias(5 + part)
        erf_term = 1.0 + lax.erf(pre_act * inv_sqrt_two)
        activated = (0.5 * pre_act * erf_term).astype(bf16)
        act_b[:, at] = activated
        slope_all[:, at] = 0.5 * erf_term + pre_act * jnp.exp(-0.5 * pre_act * pre_act) * inv_sqrt_tau
        red_at = RED_ROW + 768 * part
        second_sum = second_sum + dot_nn(activated, weights[red_at : red_at + 768, :])
    normed_two, root_two = normalize(second_sum)
    block_ref[...] = (normed_two * bias(10) + bias(11)).astype(bf16)

    grad_out = cot_ref[...].astype(f32)
    keep_bias(10, grad_out * normed_two)
    keep_bias(11, grad_out)
    d_second = norm_back(grad_out * bias(10), normed_two, root_two)
    keep_bias(9, d_second)
    d_second_b = d_second.astype(bf16)
    d_middle = d_second
    for part in range(4):
        at = slice(768 * part, 768 * (part + 1))
        red_at = RED_ROW + 768 * part
        d_pre = by_transpose(d_second_b, weights[red_at : red_at + 768, :]) * slope_all[:, at]
        keep_bias(5 + part, d_pre)
        d_pre_b = d_pre.astype(bf16)
        pre_b[:, at] = d_pre_b
        d_middle = d_middle + by_transpose(d_pre_b, expand_w[part])

    def reduce_grad(i, carry):
        at = pl.multiple_of(256 * i, 256)
        block = inner_rows(act_b[:, pl.ds(at, 256)], d_second_b)
        grads[pl.ds(pl.multiple_of(RED_ROW + at, 16), 256), :] = block.astype(bf16)
        return carry

    lax.fori_loop(0, 12, reduce_grad, 0)

    act_b[:, 0:768] = middle_b

    def expand_grad(i, carry):
        left = act_b[:, pl.ds(pl.multiple_of(128 * i, 128), 128)]
        for part in range(4):
            block = inner_rows(left, pre_b[:, 768 * part : 768 * (part + 1)])
            for j in range(6):
                stage[j, pl.ds(part, 128, stride=4), :] = block[:, 128 * j : 128 * (j + 1)]
        row = pl.multiple_of(EXP_ROW + 512 * i, 16)
        for j in range(6):
            grads[pl.ds(row, 512), 128 * j : 128 * (j + 1)] = stage[j].astype(bf16)
        return carry

    lax.fori_loop(0, 6, expand_grad, 0)

    keep_bias(3, d_middle * normed_one)
    keep_bias(4, d_middle)
    d_first = norm_back(d_middle * bias(3), normed_one, root_one)
    keep_bias(2, d_first)
    d_first_b = d_first.astype(bf16)
    d_context_b = by_transpose(d_first_b, weights[OUT_ROW : OUT_ROW + 768, :]).astype(bf16)

    def output_grad(i, carry):
        at = pl.multiple_of(256 * i, 256)
        block = inner_rows(context_b[:, pl.ds(at, 256)], d_first_b)
        grads[pl.ds(pl.multiple_of(OUT_ROW + at, 16), 256), :] = block.astype(bf16)
        return carry

    lax.fori_loop(0, 3, output_grad, 0)

    for pair in range(6):
        at = slice(128 * pair, 128 * (pair + 1))
        queries, key_rows, value_rows = triple_b[0, :, at], triple_b[1, :, at], triple_b[2, :, at]
        d_context = d_context_b[:, at]
        d_query = jnp.zeros((128, 128), f32)
        d_keys = jnp.zeros((128, 128), f32)
        d_values = jnp.zeros((128, 128), f32)
        for side in range(2):
            soft_float = soft_all[2 * pair + side]
            d_part = d_context * head_masks[side]
            d_soft = by_transpose(d_part, value_rows)
            delta = jnp.sum(d_soft * soft_float, axis=-1, keepdims=True)
            d_scores = (soft_float * (d_soft - delta) * scale).astype(bf16)
            d_query = d_query + dot_nn(d_scores, key_rows * head_masks[side])
            d_keys = d_keys + inner_rows(d_scores, queries * head_masks[side])
            d_values = d_values + inner_rows(soft_float.astype(bf16), d_part)
        bias_grads[0:1, at] = jnp.sum(d_query, axis=0, keepdims=True)
        bias_grads[1:2, at] = jnp.sum(d_values, axis=0, keepdims=True)
        d_triple_b[0, :, at] = d_query.astype(bf16)
        d_triple_b[1, :, at] = d_keys.astype(bf16)
        d_triple_b[2, :, at] = d_values.astype(bf16)

    input_grad = d_first
    for part in range(3):
        input_grad = input_grad + by_transpose(d_triple_b[part], triple_w[part])
    input_ref[...] = input_grad.astype(bf16)

    def triple_grad(i, carry):
        left = tokens_ref[:, pl.ds(pl.multiple_of(128 * i, 128), 128)]
        for part in range(3):
            block = inner_rows(left, d_triple_b[part])
            for j in range(6):
                stage[j, pl.ds(part, 128, stride=3), :] = block[:, 128 * j : 128 * (j + 1)]
        row = pl.multiple_of(384 * i, 16)
        for j in range(6):
            grads[pl.ds(row, 384), 128 * j : 128 * (j + 1)] = stage[j, 0:384, :].astype(bf16)
        return carry

    lax.fori_loop(0, 6, triple_grad, 0)
    grads[BIAS_ROW : BIAS_ROW + 16, :] = bias_grads[...].astype(bf16)

    departures = []
    for side in range(2):
        for k in range(16):
            shard = meta[3 + 16 * side + k]
            row = pl.multiple_of(shard * STEP_ROWS, 16)
            target = (keeps if side == 0 else sends)[k // 4]
            copy = pltpu.make_async_copy(
                grads.at[pl.ds(row, FRAME), pl.ds(cols[side], HALF)],
                target.at[k % 4],
                sem_out.at[side, k],
            )
            copy.start()
            departures.append(copy)
    for copy in departures:
        copy.wait()


def run_layer(meta, tokens, cotangent, frames):
    any_spec = pl.BlockSpec(memory_space=pl.ANY)
    vmem_spec = pl.BlockSpec(memory_space=pltpu.VMEM)
    rows = tokens.shape[0]
    out = pl.pallas_call(
        layer_kernel,
        out_shape=[jax.ShapeDtypeStruct((rows, D), bf16)] * 2
        + [jax.ShapeDtypeStruct((4, FRAME, HALF), bf16)] * 8,
        in_specs=[pl.BlockSpec(memory_space=pltpu.SMEM), vmem_spec, vmem_spec] + [any_spec] * 32,
        out_specs=[vmem_spec] * 2 + [any_spec] * 8,
        scratch_shapes=[
            pltpu.VMEM((ROWS, ROW), bf16),
            pltpu.VMEM((ROWS, ROW), bf16),
            pltpu.VMEM((3, D, HW), bf16),
            pltpu.VMEM((4, D, ROW), bf16),
            pltpu.VMEM((16, 16, ROW), bf16),
            pltpu.VMEM((6, 512, 128), f32),
            pltpu.VMEM((3, rows, HW), bf16),
            pltpu.VMEM((HEADS, rows, rows), f32),
            pltpu.VMEM((rows, HW), bf16),
            pltpu.VMEM((rows, FF), bf16),
            pltpu.VMEM((rows, FF), f32),
            pltpu.VMEM((rows, FF), bf16),
            pltpu.VMEM((3, rows, HW), bf16),
            pltpu.VMEM((16, ROW), f32),
            pltpu.SemaphoreType.DMA((2, 16)),
            pltpu.SemaphoreType.DMA((2, 16)),
            pltpu.SemaphoreType.DMA((2, 16)),
        ],
        compiler_params=pltpu.CompilerParams(vmem_limit_bytes=VMEM_CAP),
    )(meta, tokens, cotangent, *frames)
    return out[0], out[1], out[2:6], out[6:10]


def plane_moves(n):
    near, far = [], []
    for s in range(n):
        near += [(s, s ^ 1), (n + s, n + (s ^ 2))]
        far += [(s, s ^ 2), (n + s, n + (s ^ 1))]
    return near, far


def on_device_planes(hidden_states, cotangent, lengths, params, first_moment, second_moment):
    n = 16
    both = ("rep", "shard")
    near, far = plane_moves(n)
    swap = [(0, 1), (1, 0)]
    core = lax.axis_index("rep")
    here = lax.axis_index("shard")
    plane, spot = here // 4, here % 4
    shift, odd = (9 * here) // 2, here % 2
    shape_meta = jnp.stack([shift, odd, 3 * core, 3 - 3 * core]).astype(jnp.int32)
    spots = jnp.array([[0, 1, 2, 3], [0, 2, 1, 3]], jnp.int32)
    slots = jnp.arange(4, dtype=jnp.int32)
    base = ((plane - slots) % 4)[:, None] * 4
    mine_at = base + (spot ^ spots[core])[None, :]
    other_at = base + (spot ^ spots[1 - core])[None, :]
    layer_meta = jnp.concatenate(
        [
            jnp.stack([lengths[0], HALF * core, HALF - HALF * core]).astype(jnp.int32),
            mine_at.reshape(-1),
            other_at.reshape(-1),
        ]
    ).astype(jnp.int32)

    own = make_frame(params, shape_meta)
    mine, other = [], []
    up = [(s, (s + 4) % n) for s in range(n)]
    down = [(s, (s - 4) % n) for s in range(n)]
    zero = None
    for t in range(4):
        zero = own if t == 0 else lax.ppermute(zero, "shard", up)
        one = lax.ppermute(zero, both, near)
        two = lax.ppermute(zero, both, far)
        three = lax.ppermute(one, both, far)
        group = [zero, one, two, three]
        mine += group
        other += [lax.ppermute(piece, "rep", swap) for piece in group]

    block_out, input_grad, keeps, sends = run_layer(layer_meta, hidden_states, cotangent, mine + other)

    far_done = {}
    passed = None
    for t in (3, 2, 1, 0):
        keep = keeps[t].astype(f32)
        send = sends[t]
        if t < 2:
            send, _ = lax.optimization_barrier((send, far_done[t + 2]))
        got = lax.ppermute(send, "rep", swap).astype(f32)
        away = (keep[2:4] + got[2:4]).astype(bf16)
        far_done[t] = lax.ppermute(away, both, far)
        from_far = far_done[t].astype(f32)
        away = (keep[1] + got[1] + from_far[1]).astype(bf16)
        from_near = lax.ppermute(away, both, near).astype(f32)
        total = keep[0] + got[0] + from_far[0] + from_near
        if passed is not None:
            total = total + passed
        if t > 0:
            passed = lax.ppermute(total.astype(bf16), "shard", down).astype(f32)
    weight_grad = take_frame(total, lax.ppermute(total, "rep", swap), shape_meta)
    new_params, new_first, new_second = adamw(params, first_moment, second_moment, weight_grad)
    return (block_out, input_grad, weight_grad, new_params, new_first, new_second)


def on_device_any(hidden_states, cotangent, lengths, params, first_moment, second_moment):
    length = lengths[0]
    gathered = lax.all_gather(params.astype(jnp.bfloat16), "shard", axis=0, tiled=True)
    prm = split_flat(gathered)
    block_out, kept = forward(hidden_states, length, prm)
    input_grad, flat_grad = backward(hidden_states, length, cotangent, kept, prm)
    owned = lax.psum_scatter(flat_grad, "shard", scatter_dimension=0, tiled=True)
    weight_grad = lax.psum(owned, "rep")
    new_params, new_first, new_second = adamw(params, first_moment, second_moment, weight_grad)
    return (block_out, input_grad, weight_grad, new_params, new_first, new_second)


def solution(mesh):
    placed = (
        P(("rep", "shard"), None),
        P(("rep", "shard"), None),
        P(("rep", "shard")),
        P("shard"),
        P("shard"),
        P("shard"),
    )
    sixteen = mesh.shape["shard"] == 16 and mesh.shape["rep"] == 2
    return jax.shard_map(
        on_device_planes if sixteen else on_device_any,
        mesh=mesh,
        in_specs=placed,
        out_specs=(
            P(("rep", "shard"), None),
            P(("rep", "shard"), None),
            P("shard"),
            P("shard"),
            P("shard"),
            P("shard"),
        ),
        check_vma=False,
    )
```

```python
import functools
import math

import jax
import jax.numpy as jnp
import numpy as np
from jax import lax
from jax.experimental import pallas as pl
from jax.experimental.pallas import tpu as pltpu
from jax.sharding import PartitionSpec as P

D = 768
HEADS = 12
HEAD = 64
FF = 3072
STEP = 3
HW = 768


norm_eps = 1e-05
adam_eps = 1e-06
beta_one = 0.9
beta_two = 0.98
learn_rate = 0.01
decay_rate = 0.01
masked_score = -1e30
inv_sqrt_two = 1.0 / math.sqrt(2.0)
inv_sqrt_tau = 1.0 / math.sqrt(2.0 * math.pi)


def layout():
    return [
        ("triple_weight", (D, 3 * HW)),
        ("output_weight", (HW, D)),
        ("expand_weight", (D, FF)),
        ("reduce_weight", (FF, D)),
        ("query_bias", (HW,)),
        ("value_bias", (HW,)),
        ("output_bias", (D,)),
        ("first_gain", (D,)),
        ("first_shift", (D,)),
        ("expand_bias", (FF,)),
        ("reduce_bias", (D,)),
        ("second_gain", (D,)),
        ("second_shift", (D,)),
    ]


def split_flat(flat_vector):
    pieces = {}
    offset = 0
    for entry_name, dims_of in layout():
        amount = math.prod(dims_of)
        pieces[entry_name] = flat_vector[offset : offset + amount].reshape(dims_of)
        offset = offset + amount
    return pieces


def inner_rows(left_side, right_side):
    return lax.dot_general(
        left_side, right_side, (((0,), (0,)), ((), ())), preferred_element_type=jnp.float32
    )


def by_transpose(left_side, right_side):
    return lax.dot_general(
        left_side, right_side, (((1,), (1,)), ((), ())), preferred_element_type=jnp.float32
    )


def heads_of(row_block):
    return row_block.reshape(row_block.shape[0], HEADS, HEAD)


def normalize(values_in):
    centered = values_in - jnp.mean(values_in, axis=-1, keepdims=True)
    inv_root = lax.rsqrt(jnp.mean(centered * centered, axis=-1, keepdims=True) + norm_eps)
    return (centered * inv_root, inv_root)


def norm_back(grad_in, normed, inv_root):
    return inv_root * (
        grad_in
        - jnp.mean(grad_in, axis=-1, keepdims=True)
        - normed * jnp.mean(grad_in * normed, axis=-1, keepdims=True)
    )


def gelu_slope(pre_act):
    return (
        0.5 * (1.0 + lax.erf(pre_act * inv_sqrt_two))
        + pre_act * jnp.exp(-0.5 * pre_act * pre_act) * inv_sqrt_tau
    )


def attention_scores(queries, key_rows, length):
    scores = jnp.einsum(
        "qhd,khd->hqk", heads_of(queries), heads_of(key_rows), preferred_element_type=jnp.float32
    ) * (1.0 / math.sqrt(HEAD))
    key_valid = jnp.arange(scores.shape[-1]) < length
    return jnp.where(key_valid, scores, masked_score)


def forward(tokens, length, prm):
    rows = tokens.shape[0]
    triple = jnp.dot(tokens, prm["triple_weight"], preferred_element_type=jnp.float32)
    queries = (triple[:, :HW] + prm["query_bias"].astype(jnp.float32)).astype(jnp.bfloat16)
    key_rows = triple[:, HW : 2 * HW].astype(jnp.bfloat16)
    value_rows = (triple[:, 2 * HW :] + prm["value_bias"].astype(jnp.float32)).astype(jnp.bfloat16)
    scores = attention_scores(queries, key_rows, length)
    top_score = jnp.max(scores, axis=-1, keepdims=True)
    log_total = top_score + jnp.log(jnp.sum(jnp.exp(scores - top_score), axis=-1, keepdims=True))
    soft_weights = jnp.exp(scores - log_total).astype(jnp.bfloat16)
    context = jnp.einsum(
        "hqk,khd->qhd", soft_weights, heads_of(value_rows), preferred_element_type=jnp.float32
    )
    context = context.reshape(rows, HW).astype(jnp.bfloat16)
    first_sum = (
        tokens.astype(jnp.float32)
        + jnp.dot(context, prm["output_weight"], preferred_element_type=jnp.float32)
        + prm["output_bias"].astype(jnp.float32)
    )
    normed_one, root_one = normalize(first_sum)
    middle = normed_one * prm["first_gain"].astype(jnp.float32) + prm["first_shift"].astype(
        jnp.float32
    )
    middle_b = middle.astype(jnp.bfloat16)
    pre_act = jnp.dot(middle_b, prm["expand_weight"], preferred_element_type=jnp.float32) + prm[
        "expand_bias"
    ].astype(jnp.float32)
    activated = (0.5 * pre_act * (1.0 + lax.erf(pre_act * inv_sqrt_two))).astype(jnp.bfloat16)
    second_sum = (
        middle
        + jnp.dot(activated, prm["reduce_weight"], preferred_element_type=jnp.float32)
        + prm["reduce_bias"].astype(jnp.float32)
    )
    normed_two, root_two = normalize(second_sum)
    block_out = (
        normed_two * prm["second_gain"].astype(jnp.float32)
        + prm["second_shift"].astype(jnp.float32)
    ).astype(jnp.bfloat16)
    kept = (
        queries,
        key_rows,
        value_rows,
        log_total,
        context,
        normed_one,
        root_one,
        middle_b,
        pre_act,
        activated,
        normed_two,
        root_two,
    )
    return (block_out, kept)


def backward(tokens, length, cotangent, kept, prm):
    (
        queries,
        key_rows,
        value_rows,
        log_total,
        context,
        normed_one,
        root_one,
        middle_b,
        pre_act,
        activated,
        normed_two,
        root_two,
    ) = kept
    rows = tokens.shape[0]
    grad_out = cotangent.astype(jnp.float32)
    d_second = norm_back(grad_out * prm["second_gain"].astype(jnp.float32), normed_two, root_two)
    d_second_b = d_second.astype(jnp.bfloat16)
    d_pre = by_transpose(d_second_b, prm["reduce_weight"]) * gelu_slope(pre_act)
    d_pre_b = d_pre.astype(jnp.bfloat16)
    d_middle = d_second + by_transpose(d_pre_b, prm["expand_weight"])
    d_first = norm_back(d_middle * prm["first_gain"].astype(jnp.float32), normed_one, root_one)
    d_first_b = d_first.astype(jnp.bfloat16)
    d_context = by_transpose(d_first_b, prm["output_weight"]).astype(jnp.bfloat16)
    scores = attention_scores(queries, key_rows, length)
    soft_float = jnp.exp(scores - log_total)
    soft_weights = soft_float.astype(jnp.bfloat16)
    d_soft = jnp.einsum(
        "qhd,khd->hqk",
        heads_of(d_context),
        heads_of(value_rows),
        preferred_element_type=jnp.float32,
    )
    delta = jnp.sum(d_soft * soft_float, axis=-1, keepdims=True)
    d_scores = (soft_float * (d_soft - delta) * (1.0 / math.sqrt(HEAD))).astype(jnp.bfloat16)
    d_query = jnp.einsum(
        "hqk,khd->qhd", d_scores, heads_of(key_rows), preferred_element_type=jnp.float32
    ).reshape(rows, HW)
    d_keys = jnp.einsum(
        "hqk,qhd->khd", d_scores, heads_of(queries), preferred_element_type=jnp.float32
    ).reshape(rows, HW)
    d_values = jnp.einsum(
        "hqk,qhd->khd", soft_weights, heads_of(d_context), preferred_element_type=jnp.float32
    ).reshape(rows, HW)
    d_triple = jnp.concatenate([d_query, d_keys, d_values], axis=1).astype(jnp.bfloat16)
    input_grad = (d_first + by_transpose(d_triple, prm["triple_weight"])).astype(jnp.bfloat16)
    grad_list = [
        inner_rows(tokens, d_triple),
        inner_rows(context, d_first_b),
        inner_rows(middle_b, d_pre_b),
        inner_rows(activated, d_second_b),
        jnp.sum(d_query, axis=0),
        jnp.sum(d_values, axis=0),
        jnp.sum(d_first, axis=0),
        jnp.sum(d_middle * normed_one, axis=0),
        jnp.sum(d_middle, axis=0),
        jnp.sum(d_pre, axis=0),
        jnp.sum(d_second, axis=0),
        jnp.sum(grad_out * normed_two, axis=0),
        jnp.sum(grad_out, axis=0),
    ]
    flat_grad = jnp.concatenate([piece_grad.reshape(-1) for piece_grad in grad_list])
    return (input_grad, flat_grad)


def adamw(param_now, first_now, second_now, grad_total):
    first_new = beta_one * first_now + (1.0 - beta_one) * grad_total
    second_new = beta_two * second_now + (1.0 - beta_two) * grad_total * grad_total
    fix_one = 1.0 - beta_one**STEP
    fix_two = 1.0 - beta_two**STEP
    param_new = param_now - learn_rate * (
        first_new / fix_one / (jnp.sqrt(second_new / fix_two) + adam_eps) + decay_rate * param_now
    )
    return (param_new, first_new, second_new)

ROW = 768
STEP_ROWS = 576
FRAME = 592
HALF = ROW // 2
LINES = FRAME * 6
LOCAL = 442944
LOCAL_LINES = 3464
ROWS = 16 * STEP_ROWS + 16
OUT_ROW = 2304
EXP_ROW = 3072
RED_ROW = 6144
BIAS_ROW = 9216
LEFT = 4608
RIGHT = 9 * HALF
VMEM_CAP = 64 * 1024 * 1000

f32 = jnp.float32
bf16 = jnp.bfloat16


def swap_half(block):
    return pltpu.roll(block, 64, 1)


def frame_kernel(meta, flat_ref, out_ref, lines, framed):
    shift, odd, first_col = meta[0], meta[1], meta[2]
    lines[0:8, :] = jnp.zeros((8, 128), f32)
    lines[8 : 8 + LOCAL_LINES, :] = flat_ref[...]
    framed[0:96, :] = jnp.zeros((96, 128), f32)
    framed[LINES - 96 : LINES, :] = jnp.zeros((96, 128), f32)
    low = lax.broadcasted_iota(jnp.int32, (LOCAL_LINES, 128), 1) < 64
    here = lines[8 : 8 + LOCAL_LINES, :]
    before = lines[7 : 7 + LOCAL_LINES, :]
    moved = jnp.where(low, swap_half(before), swap_half(here))
    framed[pl.ds(shift, LOCAL_LINES), :] = jnp.where(odd == 1, moved, here)
    for j in range(3):
        column = framed[pl.ds(first_col + j, FRAME, stride=6), :]
        out_ref[:, 128 * j : 128 * (j + 1)] = column.astype(bf16)


def make_frame(params, meta):
    flat = jnp.pad(params, (0, LOCAL_LINES * 128 - LOCAL)).reshape(LOCAL_LINES, 128)
    return pl.pallas_call(
        frame_kernel,
        out_shape=jax.ShapeDtypeStruct((FRAME, HALF), bf16),
        in_specs=[
            pl.BlockSpec(memory_space=pltpu.SMEM),
            pl.BlockSpec(memory_space=pltpu.VMEM),
        ],
        out_specs=pl.BlockSpec(memory_space=pltpu.VMEM),
        scratch_shapes=[
            pltpu.VMEM((LOCAL_LINES + 16, 128), f32),
            pltpu.VMEM((LINES, 128), f32),
        ],
    )(meta, flat)


def unframe_kernel(meta, mine_ref, other_ref, out_ref, framed):
    shift, odd, first_col, other_col = meta[0], meta[1], meta[2], meta[3]
    for j in range(3):
        framed[pl.ds(first_col + j, FRAME, stride=6), :] = mine_ref[:, 128 * j : 128 * (j + 1)]
        framed[pl.ds(other_col + j, FRAME, stride=6), :] = other_ref[:, 128 * j : 128 * (j + 1)]
    low = lax.broadcasted_iota(jnp.int32, (LOCAL_LINES, 128), 1) < 64
    here = framed[pl.ds(shift, LOCAL_LINES), :]
    after = framed[pl.ds(shift + 1, LOCAL_LINES), :]
    moved = jnp.where(low, swap_half(here), swap_half(after))
    out_ref[...] = jnp.where(odd == 1, moved, here)


def take_frame(mine, other, meta):
    lines = pl.pallas_call(
        unframe_kernel,
        out_shape=jax.ShapeDtypeStruct((LOCAL_LINES, 128), f32),
        in_specs=[
            pl.BlockSpec(memory_space=pltpu.SMEM),
            pl.BlockSpec(memory_space=pltpu.VMEM),
            pl.BlockSpec(memory_space=pltpu.VMEM),
        ],
        out_specs=pl.BlockSpec(memory_space=pltpu.VMEM),
        scratch_shapes=[pltpu.VMEM((LINES + 8, 128), f32)],
    )(meta, mine, other)
    return lines.reshape(LOCAL_LINES * 128)[:LOCAL]


def dot_nn(left_side, right_side):
    return jnp.dot(left_side, right_side, preferred_element_type=f32)


def row_mean(block):
    return jnp.mean(block, axis=-1, keepdims=True)


def layer_kernel(meta, length_ref, tokens_ref, cot_ref, *refs):
    frames = refs[:32]
    block_ref, input_ref, left_ref, right_ref, sums_ref = refs[32:37]
    (
        weights,
        triple_w,
        expand_w,
        tails,
        stage,
        triple_b,
        soft_all,
        slope_all,
        rights,
        sem_main,
        sem_tail,
    ) = refs[37:]
    bias_grads = sums_ref
    length = length_ref[0]
    cols = (pl.multiple_of(meta[4], 128), pl.multiple_of(meta[5], 128))

    def main_copy(frame, shard, side):
        return pltpu.make_async_copy(
            frame.at[pl.ds(0, STEP_ROWS), :],
            weights.at[pl.ds(pl.multiple_of(shard * STEP_ROWS, 16), STEP_ROWS), pl.ds(cols[side], HALF)],
            sem_main.at[side, shard],
        )

    def tail_copy(frame, shard, side):
        return pltpu.make_async_copy(
            frame.at[pl.ds(STEP_ROWS, 16), :],
            tails.at[shard, :, pl.ds(cols[side], HALF)],
            sem_tail.at[side, shard],
        )

    for quad in range(4):
        for t in range(4):

            @pl.when(meta[6 + quad] == t)
            def _():
                for side in range(2):
                    for j in range(4):
                        shard = 4 * quad + meta[10 + 4 * side + j]
                        tail_copy(frames[16 * side + 4 * t + j], shard, side).start()
                        main_copy(frames[16 * side + 4 * t + j], shard, side).start()

    for shard in range(16):
        for side in range(2):
            tail_copy(frames[0], shard, side).wait()

    def arrive(first, last):
        for shard in range(first, last):
            for side in range(2):
                main_copy(frames[0], shard, side).wait()
            if shard > 0:
                at = STEP_ROWS * shard
                joined = weights[at : at + 16, :].astype(f32) + tails[shard - 1].astype(f32)
                weights[at : at + 16, :] = joined.astype(bf16)

    arrive(0, 4)

    def spread_triple(i, carry):
        for j in range(6):
            at = slice(128 * j, 128 * (j + 1))
            stage[j, 0:384, :] = weights[pl.ds(pl.multiple_of(384 * i, 16), 384), at].astype(f32)
            for part in range(3):
                rows = stage[j, pl.ds(part, 128, stride=3), :]
                triple_w[part, pl.ds(pl.multiple_of(128 * i, 16), 128), at] = rows.astype(bf16)
        return carry

    lax.fori_loop(0, 6, spread_triple, 0)

    def spread_expand(i, carry):
        row = pl.multiple_of(EXP_ROW + 512 * i, 16)
        for j in range(6):
            at = slice(128 * j, 128 * (j + 1))
            stage[j, :, :] = weights[pl.ds(row, 512), at].astype(f32)
            for part in range(4):
                rows = stage[j, pl.ds(part, 128, stride=4), :]
                expand_w[part, pl.ds(pl.multiple_of(128 * i, 16), 128), at] = rows.astype(bf16)
        return carry

    biases = tails[15].astype(f32)

    def bias(index):
        return biases[index : index + 1, :]

    bias_grads[...] = jnp.zeros((16, ROW), f32)

    def keep_bias(index, block):
        bias_grads[index : index + 1, :] = jnp.sum(block, axis=0, keepdims=True)

    tokens = tokens_ref[...]
    triple_b[0] = (dot_nn(tokens, triple_w[0]) + bias(0)).astype(bf16)
    triple_b[1] = dot_nn(tokens, triple_w[1]).astype(bf16)
    triple_b[2] = (dot_nn(tokens, triple_w[2]) + bias(1)).astype(bf16)

    lane = lax.broadcasted_iota(jnp.int32, (1, 128), 1)
    head_masks = ((lane < 64).astype(f32).astype(bf16), (lane >= 64).astype(f32).astype(bf16))
    key_valid = lax.broadcasted_iota(jnp.int32, (128, 128), 1) < length
    scale = 1.0 / math.sqrt(HEAD)
    for pair in range(6):
        at = slice(128 * pair, 128 * (pair + 1))
        queries, key_rows, value_rows = triple_b[0, :, at], triple_b[1, :, at], triple_b[2, :, at]
        context = jnp.zeros((128, 128), f32)
        for side in range(2):
            scores = by_transpose(queries * head_masks[side], key_rows) * scale
            scores = jnp.where(key_valid, scores, masked_score)
            top_score = jnp.max(scores, axis=-1, keepdims=True)
            log_total = top_score + jnp.log(
                jnp.sum(jnp.exp(scores - top_score), axis=-1, keepdims=True)
            )
            soft_float = jnp.exp(scores - log_total)
            soft_all[2 * pair + side] = soft_float
            context = context + dot_nn(soft_float.astype(bf16), value_rows * head_masks[side])
        left_ref[:, at] = context.astype(bf16)

    arrive(4, 6)
    first_sum = tokens.astype(f32) + dot_nn(left_ref[:, 0:768], weights[OUT_ROW : OUT_ROW + 768, :]) + bias(2)
    normed_one, root_one = normalize(first_sum)
    middle = normed_one * bias(3) + bias(4)
    middle_b = middle.astype(bf16)
    left_ref[:, 768:1536] = middle_b
    second_sum = middle + bias(9)
    arrive(6, 11)
    lax.fori_loop(0, 6, spread_expand, 0)
    arrive(11, 16)
    for part in range(4):
        at = slice(768 * part, 768 * (part + 1))
        pre_act = dot_nn(middle_b, expand_w[part]) + bias(5 + part)
        erf_term = 1.0 + lax.erf(pre_act * inv_sqrt_two)
        activated = (0.5 * pre_act * erf_term).astype(bf16)
        left_ref[:, 1536 + 768 * part : 1536 + 768 * (part + 1)] = activated
        slope_all[:, at] = 0.5 * erf_term + pre_act * jnp.exp(-0.5 * pre_act * pre_act) * inv_sqrt_tau
        red_at = RED_ROW + 768 * part
        second_sum = second_sum + dot_nn(activated, weights[red_at : red_at + 768, :])
    normed_two, root_two = normalize(second_sum)
    block_ref[...] = (normed_two * bias(10) + bias(11)).astype(bf16)

    grad_out = cot_ref[...].astype(f32)
    keep_bias(10, grad_out * normed_two)
    keep_bias(11, grad_out)
    d_second = norm_back(grad_out * bias(10), normed_two, root_two)
    keep_bias(9, d_second)
    d_second_b = d_second.astype(bf16)
    d_middle = d_second
    for part in range(4):
        at = slice(768 * part, 768 * (part + 1))
        red_at = RED_ROW + 768 * part
        d_pre = by_transpose(d_second_b, weights[red_at : red_at + 768, :]) * slope_all[:, at]
        keep_bias(5 + part, d_pre)
        d_pre_b = d_pre.astype(bf16)
        rights[1 + part] = d_pre_b
        d_middle = d_middle + by_transpose(d_pre_b, expand_w[part])

    rights[5] = d_second_b
    keep_bias(3, d_middle * normed_one)
    keep_bias(4, d_middle)
    d_first = norm_back(d_middle * bias(3), normed_one, root_one)
    keep_bias(2, d_first)
    d_first_b = d_first.astype(bf16)
    d_context_b = by_transpose(d_first_b, weights[OUT_ROW : OUT_ROW + 768, :]).astype(bf16)

    rights[0] = d_first_b
    for pair in range(6):
        at = slice(128 * pair, 128 * (pair + 1))
        queries, key_rows, value_rows = triple_b[0, :, at], triple_b[1, :, at], triple_b[2, :, at]
        d_context = d_context_b[:, at]
        d_query = jnp.zeros((128, 128), f32)
        d_keys = jnp.zeros((128, 128), f32)
        d_values = jnp.zeros((128, 128), f32)
        for side in range(2):
            soft_float = soft_all[2 * pair + side]
            d_part = d_context * head_masks[side]
            d_soft = by_transpose(d_part, value_rows)
            delta = jnp.sum(d_soft * soft_float, axis=-1, keepdims=True)
            d_scores = (soft_float * (d_soft - delta) * scale).astype(bf16)
            d_query = d_query + dot_nn(d_scores, key_rows * head_masks[side])
            d_keys = d_keys + inner_rows(d_scores, queries * head_masks[side])
            d_values = d_values + inner_rows(soft_float.astype(bf16), d_part)
        bias_grads[0:1, at] = jnp.sum(d_query, axis=0, keepdims=True)
        bias_grads[1:2, at] = jnp.sum(d_values, axis=0, keepdims=True)
        rights[6, :, at] = d_query.astype(bf16)
        rights[7, :, at] = d_keys.astype(bf16)
        rights[8, :, at] = d_values.astype(bf16)

    input_grad = d_first
    for part in range(3):
        input_grad = input_grad + by_transpose(rights[6 + part], triple_w[part])
    input_ref[...] = input_grad.astype(bf16)

    for k in range(9):
        right_ref[:, HALF * k : HALF * (k + 1)] = rights[k, :, pl.ds(cols[0], HALF)]
        left_ref[:, 4608 + HALF * k : 4608 + HALF * (k + 1)] = rights[k, :, pl.ds(cols[1], HALF)]


def run_layer(meta, lengths, tokens, cotangent, frames):
    any_spec = pl.BlockSpec(memory_space=pl.ANY)
    vmem_spec = pl.BlockSpec(memory_space=pltpu.VMEM)
    rows = tokens.shape[0]
    thin = jax.ShapeDtypeStruct((rows, D), bf16)
    out = pl.pallas_call(
        layer_kernel,
        out_shape=[
            thin,
            thin,
            jax.ShapeDtypeStruct((rows, LEFT + RIGHT), bf16),
            jax.ShapeDtypeStruct((rows, RIGHT), bf16),
            jax.ShapeDtypeStruct((16, ROW), f32),
        ],
        in_specs=[pl.BlockSpec(memory_space=pltpu.SMEM)] * 2 + [vmem_spec] * 2 + [any_spec] * 32,
        out_specs=[vmem_spec] * 5,
        scratch_shapes=[
            pltpu.VMEM((ROWS, ROW), bf16),
            pltpu.VMEM((3, D, HW), bf16),
            pltpu.VMEM((4, D, ROW), bf16),
            pltpu.VMEM((16, 16, ROW), bf16),
            pltpu.VMEM((6, 512, 128), f32),
            pltpu.VMEM((3, rows, HW), bf16),
            pltpu.VMEM((HEADS, rows, rows), f32),
            pltpu.VMEM((rows, FF), f32),
            pltpu.VMEM((9, rows, HW), bf16),
            pltpu.SemaphoreType.DMA((2, 16)),
            pltpu.SemaphoreType.DMA((2, 16)),
        ],
        compiler_params=pltpu.CompilerParams(vmem_limit_bytes=VMEM_CAP),
    )(meta, lengths, tokens, cotangent, *frames)
    return out


def grad_kernel(
    slot,
    meta,
    tokens_ref,
    tokens_other,
    left_ref,
    left_other,
    right_ref,
    sums_ref,
    sums_other,
    low_ref,
    high_ref,
    left,
    right,
    grads,
    stage,
    sem_in,
    sem_out,
):
    quad = meta[6 + slot]

    def load(pieces):
        copies = []
        for k, (source, first, size, target, at, row) in enumerate(pieces):
            copies.append(
                pltpu.make_async_copy(
                    source.at[:, pl.ds(first, size)],
                    target.at[pl.ds(row, 128), pl.ds(at, size)],
                    sem_in.at[k],
                )
            )
        for copy in copies:
            copy.start()
        for copy in copies:
            copy.wait()

    def left_pieces(first, size, at):
        return [(left_ref, first, size, left, at, 0), (left_other, first, size, left, at, 128)]

    def right_pieces(first, size, at):
        return [
            (right_ref, first, size, right, at, 0),
            (left_other, LEFT + first, size, right, at, 128),
        ]

    def mixed(first, right_first, parts, chunks, row, rows_used):
        def step(i, carry):
            rows = left[:, pl.ds(pl.multiple_of(first + 128 * i, 128), 128)]
            for part in range(parts):
                at = right_first + HALF * part
                block = inner_rows(rows, right[:, at : at + HALF])
                for j in range(3):
                    stage[j, pl.ds(part, 128, stride=parts), :] = block[:, 128 * j : 128 * (j + 1)]
            at = pl.multiple_of(row + 128 * parts * i, 16)
            for j in range(3):
                grads[pl.ds(at, rows_used), 128 * j : 128 * (j + 1)] = stage[j, 0:rows_used, :].astype(bf16)
            return carry

        lax.fori_loop(0, chunks, step, 0)

    def plain(first, right_first, chunks, row):
        def step(i, carry):
            rows = left[:, pl.ds(pl.multiple_of(first + 256 * i, 128), 256)]
            block = inner_rows(rows, right[:, right_first : right_first + HALF])
            grads[pl.ds(pl.multiple_of(row + 256 * i, 16), 256), :] = block.astype(bf16)
            return carry

        lax.fori_loop(0, chunks, step, 0)

    def last_rows(first, right_first):
        block = inner_rows(left[:, first : first + 128], right[:, right_first : right_first + HALF])
        grads[2304:2320, :] = block[0:16].astype(bf16)

    @pl.when(quad == 0)
    def _():
        load(
            [(tokens_ref, 0, 768, left, 0, 0), (tokens_other, 0, 768, left, 0, 128)]
            + left_pieces(0, 128, 768)
            + right_pieces(2304, 1152, 0)
            + right_pieces(0, 384, 1152)
        )
        mixed(0, 0, 3, 6, 0, 384)
        last_rows(768, 1152)

    @pl.when(quad == 1)
    def _():
        load(left_pieces(0, 1280, 0) + right_pieces(0, 1920, 0))
        plain(0, 0, 3, 0)
        mixed(768, 384, 4, 3, 768, 512)
        mixed(1152, 384, 4, 1, 2304, 16)

    @pl.when(quad == 2)
    def _():
        load(left_pieces(1152, 1280, 0) + right_pieces(384, 1920, 0))
        mixed(0, 0, 4, 3, 0, 512)
        plain(384, 1536, 3, 1536)
        last_rows(1152, 1536)

    @pl.when(quad == 3)
    def _():
        load(left_pieces(2304, 2304, 0) + right_pieces(1920, 384, 0))
        plain(0, 0, 9, 0)
        own = pl.ds(pl.multiple_of(meta[4], 128), HALF)
        grads[2304:2320, :] = (sums_ref[:, own] + sums_other[:, own]).astype(bf16)

    departures = []
    for j in (2, 3, 0, 1):
        row = pl.multiple_of(meta[10 + j] * STEP_ROWS, 16)
        target = (low_ref, high_ref)[j // 2].at[j % 2]
        copy = pltpu.make_async_copy(grads.at[pl.ds(row, FRAME), :], target, sem_out.at[j])
        copy.start()
        departures.append(copy)
    for copy in departures:
        copy.wait()


def quad_grads(slot, meta, operands):
    any_spec = pl.BlockSpec(memory_space=pl.ANY)
    vmem_spec = pl.BlockSpec(memory_space=pltpu.VMEM)
    frames = jax.ShapeDtypeStruct((2, FRAME, HALF), bf16)
    return pl.pallas_call(
        functools.partial(grad_kernel, slot),
        out_shape=[frames, frames],
        in_specs=[pl.BlockSpec(memory_space=pltpu.SMEM)] + [any_spec] * 5 + [vmem_spec] * 2,
        out_specs=[any_spec] * 2,
        scratch_shapes=[
            pltpu.VMEM((256, 2304), bf16),
            pltpu.VMEM((256, 1920), bf16),
            pltpu.VMEM((4 * STEP_ROWS + 16, HALF), bf16),
            pltpu.VMEM((3, 512, 128), f32),
            pltpu.SemaphoreType.DMA((8,)),
            pltpu.SemaphoreType.DMA((4,)),
        ],
        cost_estimate=pl.CostEstimate(flops=1000, bytes_accessed=1000, transcendentals=0),
    )(meta, *operands)


def plane_moves(n):
    near, far = [], []
    for s in range(n):
        near += [(s, s ^ 1), (n + s, n + (s ^ 2))]
        far += [(s, s ^ 2), (n + s, n + (s ^ 1))]
    return near, far


def device_table(n):
    rows = []
    for core in range(2):
        for here in range(n):
            plane, spot = divmod(here, 4)
            spots = ((0, 1, 2, 3), (0, 2, 1, 3))
            row = [(9 * here) // 2, here % 2, 3 * core, 3 - 3 * core, HALF * core, HALF - HALF * core]
            row += [(plane - t) % 4 for t in range(4)]
            row += [spot ^ k for k in spots[core]] + [spot ^ k for k in spots[1 - core]]
            rows.append(row)
    return np.array(rows, np.int32)


def on_device_planes(hidden_states, cotangent, lengths, params, first_moment, second_moment):
    n = 16
    both = ("rep", "shard")
    near, far = plane_moves(n)
    swap = [(0, 1), (1, 0)]
    device = lax.axis_index("rep") * n + lax.axis_index("shard")
    meta = lax.dynamic_slice(jnp.asarray(device_table(n)), (device, 0), (1, 18)).reshape(18)

    own = make_frame(params, meta)
    mine, other = [], []
    up = [(s, (s + 4) % n) for s in range(n)]
    down = [(s, (s - 4) % n) for s in range(n)]
    zero = None
    for t in range(4):
        zero = own if t == 0 else lax.ppermute(zero, "shard", up)
        one = lax.ppermute(zero, both, near)
        two = lax.ppermute(zero, both, far)
        three = lax.ppermute(one, both, far)
        group = [zero, one, two, three]
        mine += group
        other += [lax.ppermute(piece, "rep", swap) for piece in group]

    block_out, input_grad, left, right, sums = run_layer(meta, lengths, hidden_states, cotangent, mine + other)

    operands = (
        hidden_states,
        lax.ppermute(hidden_states, "rep", swap),
        left,
        lax.ppermute(left, "rep", swap),
        right,
        sums,
        lax.ppermute(sums, "rep", swap),
    )
    passed = None
    for t in (3, 2, 1, 0):
        low, high = quad_grads(t, meta, operands)
        from_far = lax.ppermute(high, both, far)
        away = (low[1].astype(f32) + from_far[1].astype(f32)).astype(bf16)
        from_near = lax.ppermute(away, both, near)
        total = low[0].astype(f32) + from_far[0].astype(f32) + from_near.astype(f32)
        if passed is not None:
            total = total + passed.astype(f32)
        if t > 0:
            passed = lax.ppermute(total.astype(bf16), "shard", down)
    weight_grad = take_frame(total, lax.ppermute(total, "rep", swap), meta)
    new_params, new_first, new_second = adamw(params, first_moment, second_moment, weight_grad)
    return (block_out, input_grad, weight_grad, new_params, new_first, new_second)


def on_device_any(hidden_states, cotangent, lengths, params, first_moment, second_moment):
    length = lengths[0]
    gathered = lax.all_gather(params.astype(jnp.bfloat16), "shard", axis=0, tiled=True)
    prm = split_flat(gathered)
    block_out, kept = forward(hidden_states, length, prm)
    input_grad, flat_grad = backward(hidden_states, length, cotangent, kept, prm)
    owned = lax.psum_scatter(flat_grad, "shard", scatter_dimension=0, tiled=True)
    weight_grad = lax.psum(owned, "rep")
    new_params, new_first, new_second = adamw(params, first_moment, second_moment, weight_grad)
    return (block_out, input_grad, weight_grad, new_params, new_first, new_second)


def solution(mesh):
    placed = (
        P(("rep", "shard"), None),
        P(("rep", "shard"), None),
        P(("rep", "shard")),
        P("shard"),
        P("shard"),
        P("shard"),
    )
    sixteen = mesh.shape["shard"] == 16 and mesh.shape["rep"] == 2
    return jax.shard_map(
        on_device_planes if sixteen else on_device_any,
        mesh=mesh,
        in_specs=placed,
        out_specs=(
            P(("rep", "shard"), None),
            P(("rep", "shard"), None),
            P("shard"),
            P("shard"),
            P("shard"),
            P("shard"),
        ),
        check_vma=False,
    )
```

```python
import functools
import math

import jax
import jax.numpy as jnp
import numpy as np
from jax import lax
from jax.experimental import pallas as pl
from jax.experimental.pallas import tpu as pltpu
from jax.sharding import PartitionSpec as P

D = 768
HEADS = 12
HEAD = 64
FF = 3072
STEP = 3
HW = 768


norm_eps = 1e-05
adam_eps = 1e-06
beta_one = 0.9
beta_two = 0.98
learn_rate = 0.01
decay_rate = 0.01
masked_score = -1e30
inv_sqrt_two = 1.0 / math.sqrt(2.0)
inv_sqrt_tau = 1.0 / math.sqrt(2.0 * math.pi)


def layout():
    return [
        ("triple_weight", (D, 3 * HW)),
        ("output_weight", (HW, D)),
        ("expand_weight", (D, FF)),
        ("reduce_weight", (FF, D)),
        ("query_bias", (HW,)),
        ("value_bias", (HW,)),
        ("output_bias", (D,)),
        ("first_gain", (D,)),
        ("first_shift", (D,)),
        ("expand_bias", (FF,)),
        ("reduce_bias", (D,)),
        ("second_gain", (D,)),
        ("second_shift", (D,)),
    ]


def split_flat(flat_vector):
    pieces = {}
    offset = 0
    for entry_name, dims_of in layout():
        amount = math.prod(dims_of)
        pieces[entry_name] = flat_vector[offset : offset + amount].reshape(dims_of)
        offset = offset + amount
    return pieces


def inner_rows(left_side, right_side):
    return lax.dot_general(
        left_side, right_side, (((0,), (0,)), ((), ())), preferred_element_type=jnp.float32
    )


def by_transpose(left_side, right_side):
    return lax.dot_general(
        left_side, right_side, (((1,), (1,)), ((), ())), preferred_element_type=jnp.float32
    )


def heads_of(row_block):
    return row_block.reshape(row_block.shape[0], HEADS, HEAD)


def normalize(values_in):
    centered = values_in - jnp.mean(values_in, axis=-1, keepdims=True)
    inv_root = lax.rsqrt(jnp.mean(centered * centered, axis=-1, keepdims=True) + norm_eps)
    return (centered * inv_root, inv_root)


def norm_back(grad_in, normed, inv_root):
    return inv_root * (
        grad_in
        - jnp.mean(grad_in, axis=-1, keepdims=True)
        - normed * jnp.mean(grad_in * normed, axis=-1, keepdims=True)
    )


def gelu_slope(pre_act):
    return (
        0.5 * (1.0 + lax.erf(pre_act * inv_sqrt_two))
        + pre_act * jnp.exp(-0.5 * pre_act * pre_act) * inv_sqrt_tau
    )


def attention_scores(queries, key_rows, length):
    scores = jnp.einsum(
        "qhd,khd->hqk", heads_of(queries), heads_of(key_rows), preferred_element_type=jnp.float32
    ) * (1.0 / math.sqrt(HEAD))
    key_valid = jnp.arange(scores.shape[-1]) < length
    return jnp.where(key_valid, scores, masked_score)


def forward(tokens, length, prm):
    rows = tokens.shape[0]
    triple = jnp.dot(tokens, prm["triple_weight"], preferred_element_type=jnp.float32)
    queries = (triple[:, :HW] + prm["query_bias"].astype(jnp.float32)).astype(jnp.bfloat16)
    key_rows = triple[:, HW : 2 * HW].astype(jnp.bfloat16)
    value_rows = (triple[:, 2 * HW :] + prm["value_bias"].astype(jnp.float32)).astype(jnp.bfloat16)
    scores = attention_scores(queries, key_rows, length)
    top_score = jnp.max(scores, axis=-1, keepdims=True)
    log_total = top_score + jnp.log(jnp.sum(jnp.exp(scores - top_score), axis=-1, keepdims=True))
    soft_weights = jnp.exp(scores - log_total).astype(jnp.bfloat16)
    context = jnp.einsum(
        "hqk,khd->qhd", soft_weights, heads_of(value_rows), preferred_element_type=jnp.float32
    )
    context = context.reshape(rows, HW).astype(jnp.bfloat16)
    first_sum = (
        tokens.astype(jnp.float32)
        + jnp.dot(context, prm["output_weight"], preferred_element_type=jnp.float32)
        + prm["output_bias"].astype(jnp.float32)
    )
    normed_one, root_one = normalize(first_sum)
    middle = normed_one * prm["first_gain"].astype(jnp.float32) + prm["first_shift"].astype(
        jnp.float32
    )
    middle_b = middle.astype(jnp.bfloat16)
    pre_act = jnp.dot(middle_b, prm["expand_weight"], preferred_element_type=jnp.float32) + prm[
        "expand_bias"
    ].astype(jnp.float32)
    activated = (0.5 * pre_act * (1.0 + lax.erf(pre_act * inv_sqrt_two))).astype(jnp.bfloat16)
    second_sum = (
        middle
        + jnp.dot(activated, prm["reduce_weight"], preferred_element_type=jnp.float32)
        + prm["reduce_bias"].astype(jnp.float32)
    )
    normed_two, root_two = normalize(second_sum)
    block_out = (
        normed_two * prm["second_gain"].astype(jnp.float32)
        + prm["second_shift"].astype(jnp.float32)
    ).astype(jnp.bfloat16)
    kept = (
        queries,
        key_rows,
        value_rows,
        log_total,
        context,
        normed_one,
        root_one,
        middle_b,
        pre_act,
        activated,
        normed_two,
        root_two,
    )
    return (block_out, kept)


def backward(tokens, length, cotangent, kept, prm):
    (
        queries,
        key_rows,
        value_rows,
        log_total,
        context,
        normed_one,
        root_one,
        middle_b,
        pre_act,
        activated,
        normed_two,
        root_two,
    ) = kept
    rows = tokens.shape[0]
    grad_out = cotangent.astype(jnp.float32)
    d_second = norm_back(grad_out * prm["second_gain"].astype(jnp.float32), normed_two, root_two)
    d_second_b = d_second.astype(jnp.bfloat16)
    d_pre = by_transpose(d_second_b, prm["reduce_weight"]) * gelu_slope(pre_act)
    d_pre_b = d_pre.astype(jnp.bfloat16)
    d_middle = d_second + by_transpose(d_pre_b, prm["expand_weight"])
    d_first = norm_back(d_middle * prm["first_gain"].astype(jnp.float32), normed_one, root_one)
    d_first_b = d_first.astype(jnp.bfloat16)
    d_context = by_transpose(d_first_b, prm["output_weight"]).astype(jnp.bfloat16)
    scores = attention_scores(queries, key_rows, length)
    soft_float = jnp.exp(scores - log_total)
    soft_weights = soft_float.astype(jnp.bfloat16)
    d_soft = jnp.einsum(
        "qhd,khd->hqk",
        heads_of(d_context),
        heads_of(value_rows),
        preferred_element_type=jnp.float32,
    )
    delta = jnp.sum(d_soft * soft_float, axis=-1, keepdims=True)
    d_scores = (soft_float * (d_soft - delta) * (1.0 / math.sqrt(HEAD))).astype(jnp.bfloat16)
    d_query = jnp.einsum(
        "hqk,khd->qhd", d_scores, heads_of(key_rows), preferred_element_type=jnp.float32
    ).reshape(rows, HW)
    d_keys = jnp.einsum(
        "hqk,qhd->khd", d_scores, heads_of(queries), preferred_element_type=jnp.float32
    ).reshape(rows, HW)
    d_values = jnp.einsum(
        "hqk,qhd->khd", soft_weights, heads_of(d_context), preferred_element_type=jnp.float32
    ).reshape(rows, HW)
    d_triple = jnp.concatenate([d_query, d_keys, d_values], axis=1).astype(jnp.bfloat16)
    input_grad = (d_first + by_transpose(d_triple, prm["triple_weight"])).astype(jnp.bfloat16)
    grad_list = [
        inner_rows(tokens, d_triple),
        inner_rows(context, d_first_b),
        inner_rows(middle_b, d_pre_b),
        inner_rows(activated, d_second_b),
        jnp.sum(d_query, axis=0),
        jnp.sum(d_values, axis=0),
        jnp.sum(d_first, axis=0),
        jnp.sum(d_middle * normed_one, axis=0),
        jnp.sum(d_middle, axis=0),
        jnp.sum(d_pre, axis=0),
        jnp.sum(d_second, axis=0),
        jnp.sum(grad_out * normed_two, axis=0),
        jnp.sum(grad_out, axis=0),
    ]
    flat_grad = jnp.concatenate([piece_grad.reshape(-1) for piece_grad in grad_list])
    return (input_grad, flat_grad)


def adamw(param_now, first_now, second_now, grad_total):
    first_new = beta_one * first_now + (1.0 - beta_one) * grad_total
    second_new = beta_two * second_now + (1.0 - beta_two) * grad_total * grad_total
    fix_one = 1.0 - beta_one**STEP
    fix_two = 1.0 - beta_two**STEP
    param_new = param_now - learn_rate * (
        first_new / fix_one / (jnp.sqrt(second_new / fix_two) + adam_eps) + decay_rate * param_now
    )
    return (param_new, first_new, second_new)

ROW = 768
STEP_ROWS = 576
FRAME = 592
HALF = ROW // 2
LINES = FRAME * 6
LOCAL = 442944
LOCAL_LINES = 3464
ROWS = 16 * STEP_ROWS + 16
OUT_ROW = 2304
EXP_ROW = 3072
RED_ROW = 6144
BIAS_ROW = 9216
LEFT = 4608
BLOCK_LINES = 872
RIGHT = 9 * HALF
VMEM_CAP = 64 * 1024 * 1000

f32 = jnp.float32
bf16 = jnp.bfloat16


def swap_half(block):
    return pltpu.roll(block, 64, 1)


def frame_kernel(flat_ref, out_ref, lines, framed):
    here_at, core = lax.axis_index("shard"), lax.axis_index("rep")
    shift, odd, first_col = (9 * here_at) // 2, here_at % 2, 3 * core
    lines[0:8, :] = jnp.zeros((8, 128), f32)
    lines[LOCAL_LINES : LOCAL_LINES + 16, :] = jnp.zeros((16, 128), f32)
    lines[8:3464, :] = flat_ref[pl.ds(0, 442368)].reshape(3456, 128)
    lines[3464:3468, :] = flat_ref[pl.ds(442368, 512)].reshape(4, 128)
    lines[3468:3469, 0:64] = flat_ref[pl.ds(442880, 64)].reshape(1, 64)
    framed[0:96, :] = jnp.zeros((96, 128), f32)
    framed[LINES - 96 : LINES, :] = jnp.zeros((96, 128), f32)
    low = lax.broadcasted_iota(jnp.int32, (LOCAL_LINES, 128), 1) < 64
    here = lines[8 : 8 + LOCAL_LINES, :]
    before = lines[7 : 7 + LOCAL_LINES, :]
    moved = jnp.where(low, swap_half(before), swap_half(here))
    framed[pl.ds(shift, LOCAL_LINES), :] = jnp.where(odd == 1, moved, here)
    for j in range(3):
        column = framed[pl.ds(first_col + j, FRAME, stride=6), :]
        out_ref[:, 128 * j : 128 * (j + 1)] = column.astype(bf16)


def make_frame(params):
    return pl.pallas_call(
        frame_kernel,
        out_shape=jax.ShapeDtypeStruct((FRAME, HALF), bf16),
        in_specs=[pl.BlockSpec(memory_space=pltpu.VMEM)],
        out_specs=pl.BlockSpec(memory_space=pltpu.VMEM),
        scratch_shapes=[
            pltpu.VMEM((LOCAL_LINES + 16, 128), f32),
            pltpu.VMEM((LINES, 128), f32),
        ],
    )(params)


def finish_kernel(
    meta, mine_ref, other_ref, param_ref, first_ref, second_ref, grad_out, param_out, first_out, second_out, framed
):
    shift, odd, first_col, other_col = meta[0], meta[1], meta[2], meta[3]
    step = pl.program_id(0)

    @pl.when(step == 0)
    def _():
        framed[LINES : LINES + 16, :] = jnp.zeros((16, 128), f32)
        for j in range(3):
            at = slice(128 * j, 128 * (j + 1))
            framed[pl.ds(first_col + j, FRAME, stride=6), :] = mine_ref[:, at]
            framed[pl.ds(other_col + j, FRAME, stride=6), :] = other_ref[:, at]

    low = lax.broadcasted_iota(jnp.int32, (BLOCK_LINES, 128), 1) < 64
    here = framed[pl.ds(shift + BLOCK_LINES * step, BLOCK_LINES), :]
    after = framed[pl.ds(shift + BLOCK_LINES * step + 1, BLOCK_LINES), :]
    moved = jnp.where(low, swap_half(here), swap_half(after))
    grad = jnp.where(odd == 1, moved, here).reshape(BLOCK_LINES * 128)
    grad_out[...] = grad
    new_param, new_first, new_second = adamw(param_ref[...], first_ref[...], second_ref[...], grad)
    param_out[...] = new_param
    first_out[...] = new_first
    second_out[...] = new_second


def finish(mine, other, meta, params, first_moment, second_moment):
    vmem_spec = pl.BlockSpec(memory_space=pltpu.VMEM)
    block_spec = pl.BlockSpec((BLOCK_LINES * 128,), lambda i: (i,))
    return pl.pallas_call(
        finish_kernel,
        grid=(4,),
        out_shape=[jax.ShapeDtypeStruct((LOCAL,), f32)] * 4,
        in_specs=[pl.BlockSpec(memory_space=pltpu.SMEM), vmem_spec, vmem_spec] + [block_spec] * 3,
        out_specs=[block_spec] * 4,
        scratch_shapes=[pltpu.VMEM((LINES + 16, 128), f32)],
    )(meta, mine, other, params, first_moment, second_moment)


def dot_nn(left_side, right_side):
    return jnp.dot(left_side, right_side, preferred_element_type=f32)


def row_mean(block):
    return jnp.mean(block, axis=-1, keepdims=True)


def layer_kernel(meta, length_ref, tokens_ref, cot_ref, *refs):
    frames = refs[:32]
    block_ref, input_ref, left_ref, right_ref, sums_ref = refs[32:37]
    (
        weights,
        triple_w,
        expand_w,
        tails,
        stage,
        triple_b,
        soft_all,
        slope_all,
        rights,
        sem_main,
        sem_tail,
    ) = refs[37:]
    bias_grads = sums_ref
    length = length_ref[0]
    cols = (pl.multiple_of(meta[4], 128), pl.multiple_of(meta[5], 128))

    def main_copy(frame, shard, side):
        return pltpu.make_async_copy(
            frame.at[pl.ds(0, STEP_ROWS), :],
            weights.at[pl.ds(pl.multiple_of(shard * STEP_ROWS, 16), STEP_ROWS), pl.ds(cols[side], HALF)],
            sem_main.at[side, shard],
        )

    def tail_copy(frame, shard, side):
        return pltpu.make_async_copy(
            frame.at[pl.ds(STEP_ROWS, 16), :],
            tails.at[shard, :, pl.ds(cols[side], HALF)],
            sem_tail.at[side, shard],
        )

    def start_copies(quad, mains, ends):
        for t in range(4):

            @pl.when(meta[6 + quad] == t)
            def _():
                for side in range(2):
                    for j in range(4):
                        shard = 4 * quad + meta[10 + 4 * side + j]
                        if mains:
                            main_copy(frames[16 * side + 4 * t + j], shard, side).start()
                        if ends:
                            tail_copy(frames[16 * side + 4 * t + j], shard, side).start()

    start_copies(3, False, True)
    for quad in range(4):
        start_copies(quad, True, quad < 3)

    def arrive(first, last):
        for shard in range(first, last):
            for side in range(2):
                main_copy(frames[0], shard, side).wait()
            if shard > 0:
                for side in range(2):
                    tail_copy(frames[0], shard - 1, side).wait()
                at = STEP_ROWS * shard
                joined = weights[at : at + 16, :].astype(f32) + tails[shard - 1].astype(f32)
                weights[at : at + 16, :] = joined.astype(bf16)

    for side in range(2):
        tail_copy(frames[0], 15, side).wait()
    arrive(0, 4)

    def spread_triple(i, carry):
        for j in range(6):
            at = slice(128 * j, 128 * (j + 1))
            stage[j, 0:384, :] = weights[pl.ds(pl.multiple_of(384 * i, 16), 384), at].astype(f32)
            for part in range(3):
                rows = stage[j, pl.ds(part, 128, stride=3), :]
                triple_w[part, pl.ds(pl.multiple_of(128 * i, 16), 128), at] = rows.astype(bf16)
        return carry

    lax.fori_loop(0, 6, spread_triple, 0)

    def spread_expand(i, carry):
        row = pl.multiple_of(EXP_ROW + 512 * i, 16)
        for j in range(6):
            at = slice(128 * j, 128 * (j + 1))
            stage[j, :, :] = weights[pl.ds(row, 512), at].astype(f32)
            for part in range(4):
                rows = stage[j, pl.ds(part, 128, stride=4), :]
                expand_w[part, pl.ds(pl.multiple_of(128 * i, 16), 128), at] = rows.astype(bf16)
        return carry

    biases = tails[15].astype(f32)

    def bias(index):
        return biases[index : index + 1, :]

    bias_grads[...] = jnp.zeros((16, ROW), f32)

    def keep_bias(index, block):
        bias_grads[index : index + 1, :] = jnp.sum(block, axis=0, keepdims=True)

    tokens = tokens_ref[...]
    triple_b[0] = (dot_nn(tokens, triple_w[0]) + bias(0)).astype(bf16)
    triple_b[1] = dot_nn(tokens, triple_w[1]).astype(bf16)
    triple_b[2] = (dot_nn(tokens, triple_w[2]) + bias(1)).astype(bf16)

    lane = lax.broadcasted_iota(jnp.int32, (1, 128), 1)
    head_masks = ((lane < 64).astype(f32).astype(bf16), (lane >= 64).astype(f32).astype(bf16))
    key_valid = lax.broadcasted_iota(jnp.int32, (128, 128), 1) < length
    scale = 1.0 / math.sqrt(HEAD)
    for pair in range(6):
        at = slice(128 * pair, 128 * (pair + 1))
        queries, key_rows, value_rows = triple_b[0, :, at], triple_b[1, :, at], triple_b[2, :, at]
        context = jnp.zeros((128, 128), f32)
        for side in range(2):
            scores = by_transpose(queries * head_masks[side], key_rows) * scale
            scores = jnp.where(key_valid, scores, masked_score)
            top_score = jnp.max(scores, axis=-1, keepdims=True)
            log_total = top_score + jnp.log(
                jnp.sum(jnp.exp(scores - top_score), axis=-1, keepdims=True)
            )
            soft_float = jnp.exp(scores - log_total)
            soft_all[2 * pair + side] = soft_float
            context = context + dot_nn(soft_float.astype(bf16), value_rows * head_masks[side])
        left_ref[:, at] = context.astype(bf16)

    arrive(4, 6)
    first_sum = tokens.astype(f32) + dot_nn(left_ref[:, 0:768], weights[OUT_ROW : OUT_ROW + 768, :]) + bias(2)
    normed_one, root_one = normalize(first_sum)
    middle = normed_one * bias(3) + bias(4)
    middle_b = middle.astype(bf16)
    left_ref[:, 768:1536] = middle_b
    second_sum = middle + bias(9)
    arrive(6, 11)
    lax.fori_loop(0, 6, spread_expand, 0)
    arrive(11, 16)
    for part in range(4):
        at = slice(768 * part, 768 * (part + 1))
        pre_act = dot_nn(middle_b, expand_w[part]) + bias(5 + part)
        erf_term = 1.0 + lax.erf(pre_act * inv_sqrt_two)
        activated = (0.5 * pre_act * erf_term).astype(bf16)
        left_ref[:, 1536 + 768 * part : 1536 + 768 * (part + 1)] = activated
        slope_all[:, at] = 0.5 * erf_term + pre_act * jnp.exp(-0.5 * pre_act * pre_act) * inv_sqrt_tau
        red_at = RED_ROW + 768 * part
        second_sum = second_sum + dot_nn(activated, weights[red_at : red_at + 768, :])
    normed_two, root_two = normalize(second_sum)
    block_ref[...] = (normed_two * bias(10) + bias(11)).astype(bf16)

    grad_out = cot_ref[...].astype(f32)
    keep_bias(10, grad_out * normed_two)
    keep_bias(11, grad_out)
    d_second = norm_back(grad_out * bias(10), normed_two, root_two)
    keep_bias(9, d_second)
    d_second_b = d_second.astype(bf16)
    d_middle = d_second
    for part in range(4):
        at = slice(768 * part, 768 * (part + 1))
        red_at = RED_ROW + 768 * part
        d_pre = by_transpose(d_second_b, weights[red_at : red_at + 768, :]) * slope_all[:, at]
        keep_bias(5 + part, d_pre)
        d_pre_b = d_pre.astype(bf16)
        rights[1 + part] = d_pre_b
        d_middle = d_middle + by_transpose(d_pre_b, expand_w[part])

    rights[5] = d_second_b
    keep_bias(3, d_middle * normed_one)
    keep_bias(4, d_middle)
    d_first = norm_back(d_middle * bias(3), normed_one, root_one)
    keep_bias(2, d_first)
    d_first_b = d_first.astype(bf16)
    d_context_b = by_transpose(d_first_b, weights[OUT_ROW : OUT_ROW + 768, :]).astype(bf16)

    rights[0] = d_first_b
    for pair in range(6):
        at = slice(128 * pair, 128 * (pair + 1))
        queries, key_rows, value_rows = triple_b[0, :, at], triple_b[1, :, at], triple_b[2, :, at]
        d_context = d_context_b[:, at]
        d_query = jnp.zeros((128, 128), f32)
        d_keys = jnp.zeros((128, 128), f32)
        d_values = jnp.zeros((128, 128), f32)
        for side in range(2):
            soft_float = soft_all[2 * pair + side]
            d_part = d_context * head_masks[side]
            d_soft = by_transpose(d_part, value_rows)
            delta = jnp.sum(d_soft * soft_float, axis=-1, keepdims=True)
            d_scores = (soft_float * (d_soft - delta) * scale).astype(bf16)
            d_query = d_query + dot_nn(d_scores, key_rows * head_masks[side])
            d_keys = d_keys + inner_rows(d_scores, queries * head_masks[side])
            d_values = d_values + inner_rows(soft_float.astype(bf16), d_part)
        bias_grads[0:1, at] = jnp.sum(d_query, axis=0, keepdims=True)
        bias_grads[1:2, at] = jnp.sum(d_values, axis=0, keepdims=True)
        rights[6, :, at] = d_query.astype(bf16)
        rights[7, :, at] = d_keys.astype(bf16)
        rights[8, :, at] = d_values.astype(bf16)

    input_grad = d_first
    for part in range(3):
        input_grad = input_grad + by_transpose(rights[6 + part], triple_w[part])
    input_ref[...] = input_grad.astype(bf16)

    for k in range(9):
        right_ref[:, HALF * k : HALF * (k + 1)] = rights[k, :, pl.ds(cols[0], HALF)]
        left_ref[:, 4608 + HALF * k : 4608 + HALF * (k + 1)] = rights[k, :, pl.ds(cols[1], HALF)]


def run_layer(meta, lengths, tokens, cotangent, frames):
    any_spec = pl.BlockSpec(memory_space=pl.ANY)
    vmem_spec = pl.BlockSpec(memory_space=pltpu.VMEM)
    rows = tokens.shape[0]
    thin = jax.ShapeDtypeStruct((rows, D), bf16)
    out = pl.pallas_call(
        layer_kernel,
        out_shape=[
            thin,
            thin,
            jax.ShapeDtypeStruct((rows, LEFT + RIGHT), bf16),
            jax.ShapeDtypeStruct((rows, RIGHT), bf16),
            jax.ShapeDtypeStruct((16, ROW), f32),
        ],
        in_specs=[pl.BlockSpec(memory_space=pltpu.SMEM)] * 2 + [vmem_spec] * 2 + [any_spec] * 32,
        out_specs=[vmem_spec] * 5,
        scratch_shapes=[
            pltpu.VMEM((ROWS, ROW), bf16),
            pltpu.VMEM((3, D, HW), bf16),
            pltpu.VMEM((4, D, ROW), bf16),
            pltpu.VMEM((16, 16, ROW), bf16),
            pltpu.VMEM((6, 512, 128), f32),
            pltpu.VMEM((3, rows, HW), bf16),
            pltpu.VMEM((HEADS, rows, rows), f32),
            pltpu.VMEM((rows, FF), f32),
            pltpu.VMEM((9, rows, HW), bf16),
            pltpu.SemaphoreType.DMA((2, 16)),
            pltpu.SemaphoreType.DMA((2, 16)),
        ],
        compiler_params=pltpu.CompilerParams(vmem_limit_bytes=VMEM_CAP),
    )(meta, lengths, tokens, cotangent, *frames)
    return out


def grad_kernel(
    slot,
    meta,
    tokens_ref,
    tokens_other,
    left_ref,
    left_other,
    right_ref,
    sums_ref,
    sums_other,
    low_ref,
    high_ref,
    left,
    right,
    grads,
    stage,
    sem_in,
    sem_out,
):
    quad = meta[6 + slot]

    def load(pieces):
        copies = []
        for k, (source, first, size, target, at, row) in enumerate(pieces):
            copies.append(
                pltpu.make_async_copy(
                    source.at[:, pl.ds(first, size)],
                    target.at[pl.ds(row, 128), pl.ds(at, size)],
                    sem_in.at[k],
                )
            )
        for copy in copies:
            copy.start()
        for copy in copies:
            copy.wait()

    def left_pieces(first, size, at):
        return [(left_ref, first, size, left, at, 0), (left_other, first, size, left, at, 128)]

    def right_pieces(first, size, at):
        return [
            (right_ref, first, size, right, at, 0),
            (left_other, LEFT + first, size, right, at, 128),
        ]

    def mixed(first, right_first, parts, chunks, row, rows_used):
        def step(i, carry):
            rows = left[:, pl.ds(pl.multiple_of(first + 128 * i, 128), 128)]
            for part in range(parts):
                at = right_first + HALF * part
                block = inner_rows(rows, right[:, at : at + HALF])
                for j in range(3):
                    stage[j, pl.ds(part, 128, stride=parts), :] = block[:, 128 * j : 128 * (j + 1)]
            at = pl.multiple_of(row + 128 * parts * i, 16)
            for j in range(3):
                grads[pl.ds(at, rows_used), 128 * j : 128 * (j + 1)] = stage[j, 0:rows_used, :].astype(bf16)
            return carry

        lax.fori_loop(0, chunks, step, 0, unroll=True)

    def plain(first, right_first, chunks, row):
        def step(i, carry):
            rows = left[:, pl.ds(pl.multiple_of(first + 256 * i, 128), 256)]
            block = inner_rows(rows, right[:, right_first : right_first + HALF])
            grads[pl.ds(pl.multiple_of(row + 256 * i, 16), 256), :] = block.astype(bf16)
            return carry

        lax.fori_loop(0, chunks, step, 0, unroll=True)

    def last_rows(first, right_first):
        block = inner_rows(left[:, first : first + 128], right[:, right_first : right_first + HALF])
        grads[2304:2320, :] = block[0:16].astype(bf16)

    @pl.when(quad == 0)
    def _():
        load(
            [(tokens_ref, 0, 768, left, 0, 0), (tokens_other, 0, 768, left, 0, 128)]
            + left_pieces(0, 128, 768)
            + right_pieces(2304, 1152, 0)
            + right_pieces(0, 384, 1152)
        )
        mixed(0, 0, 3, 6, 0, 384)
        last_rows(768, 1152)

    @pl.when(quad == 1)
    def _():
        load(left_pieces(0, 1280, 0) + right_pieces(0, 1920, 0))
        plain(0, 0, 3, 0)
        mixed(768, 384, 4, 3, 768, 512)
        mixed(1152, 384, 4, 1, 2304, 16)

    @pl.when(quad == 2)
    def _():
        load(left_pieces(1152, 1280, 0) + right_pieces(384, 1920, 0))
        mixed(0, 0, 4, 3, 0, 512)
        plain(384, 1536, 3, 1536)
        last_rows(1152, 1536)

    @pl.when(quad == 3)
    def _():
        load(left_pieces(2304, 2304, 0) + right_pieces(1920, 384, 0))
        plain(0, 0, 9, 0)
        own = pl.ds(pl.multiple_of(meta[4], 128), HALF)
        grads[2304:2320, :] = (sums_ref[:, own] + sums_other[:, own]).astype(bf16)

    departures = []
    for j in (2, 3, 0, 1):
        row = pl.multiple_of(meta[10 + j] * STEP_ROWS, 16)
        target = (low_ref, high_ref)[j // 2].at[j % 2]
        copy = pltpu.make_async_copy(grads.at[pl.ds(row, FRAME), :], target, sem_out.at[j])
        copy.start()
        departures.append(copy)
    for copy in departures:
        copy.wait()


def quad_grads(slot, meta, operands):
    any_spec = pl.BlockSpec(memory_space=pl.ANY)
    vmem_spec = pl.BlockSpec(memory_space=pltpu.VMEM)
    frames = jax.ShapeDtypeStruct((2, FRAME, HALF), bf16)
    return pl.pallas_call(
        functools.partial(grad_kernel, slot),
        out_shape=[frames, frames],
        in_specs=[pl.BlockSpec(memory_space=pltpu.SMEM)] + [any_spec] * 5 + [vmem_spec] * 2,
        out_specs=[any_spec] * 2,
        scratch_shapes=[
            pltpu.VMEM((256, 2304), bf16),
            pltpu.VMEM((256, 1920), bf16),
            pltpu.VMEM((4 * STEP_ROWS + 16, HALF), bf16),
            pltpu.VMEM((3, 512, 128), f32),
            pltpu.SemaphoreType.DMA((8,)),
            pltpu.SemaphoreType.DMA((4,)),
        ],
        cost_estimate=pl.CostEstimate(flops=1000, bytes_accessed=1000, transcendentals=0),
    )(meta, *operands)


def plane_moves(n):
    near, far = [], []
    for s in range(n):
        near += [(s, s ^ 1), (n + s, n + (s ^ 2))]
        far += [(s, s ^ 2), (n + s, n + (s ^ 1))]
    return near, far


def device_table(n):
    rows = []
    for core in range(2):
        for here in range(n):
            plane, spot = divmod(here, 4)
            spots = ((0, 1, 2, 3), (0, 2, 1, 3))
            row = [(9 * here) // 2, here % 2, 3 * core, 3 - 3 * core, HALF * core, HALF - HALF * core]
            row += [(plane - t) % 4 for t in range(4)]
            row += [spot ^ k for k in spots[core]] + [spot ^ k for k in spots[1 - core]]
            rows.append(row)
    return np.array(rows, np.int32)


def on_device_planes(hidden_states, cotangent, lengths, params, first_moment, second_moment):
    n = 16
    both = ("rep", "shard")
    near, far = plane_moves(n)
    swap = [(0, 1), (1, 0)]
    device = lax.axis_index("rep") * n + lax.axis_index("shard")
    meta = lax.dynamic_slice(jnp.asarray(device_table(n)), (device, 0), (1, 18)).reshape(18)

    own = make_frame(params)
    mine, other = [], []
    up = [(s, (s + 4) % n) for s in range(n)]
    down = [(s, (s - 4) % n) for s in range(n)]
    zero = None
    for t in range(4):
        zero = own if t == 0 else lax.ppermute(zero, "shard", up)
        one = lax.ppermute(zero, both, near)
        two = lax.ppermute(zero, both, far)
        three = lax.ppermute(one, both, far)
        group = [zero, one, two, three]
        mine += group
        other += [lax.ppermute(piece, "rep", swap) for piece in group]

    block_out, input_grad, left, right, sums = run_layer(meta, lengths, hidden_states, cotangent, mine + other)

    operands = (
        hidden_states,
        lax.ppermute(hidden_states, "rep", swap),
        left,
        lax.ppermute(left, "rep", swap),
        right,
        sums,
        lax.ppermute(sums, "rep", swap),
    )
    passed = None
    for t in (3, 2, 1, 0):
        low, high = quad_grads(t, meta, operands)
        from_far = lax.ppermute(high, both, far)
        away = (low[1].astype(f32) + from_far[1].astype(f32)).astype(bf16)
        from_near = lax.ppermute(away, both, near)
        total = low[0].astype(f32) + from_far[0].astype(f32) + from_near.astype(f32)
        if passed is not None:
            total = total + passed.astype(f32)
        if t > 0:
            passed = lax.ppermute(total.astype(bf16), "shard", down)
    weight_grad, new_params, new_first, new_second = finish(
        total, lax.ppermute(total, "rep", swap), meta, params, first_moment, second_moment
    )
    return (block_out, input_grad, weight_grad, new_params, new_first, new_second)


def on_device_any(hidden_states, cotangent, lengths, params, first_moment, second_moment):
    length = lengths[0]
    gathered = lax.all_gather(params.astype(jnp.bfloat16), "shard", axis=0, tiled=True)
    prm = split_flat(gathered)
    block_out, kept = forward(hidden_states, length, prm)
    input_grad, flat_grad = backward(hidden_states, length, cotangent, kept, prm)
    owned = lax.psum_scatter(flat_grad, "shard", scatter_dimension=0, tiled=True)
    weight_grad = lax.psum(owned, "rep")
    new_params, new_first, new_second = adamw(params, first_moment, second_moment, weight_grad)
    return (block_out, input_grad, weight_grad, new_params, new_first, new_second)


def solution(mesh):
    placed = (
        P(("rep", "shard"), None),
        P(("rep", "shard"), None),
        P(("rep", "shard")),
        P("shard"),
        P("shard"),
        P("shard"),
    )
    sixteen = mesh.shape["shard"] == 16 and mesh.shape["rep"] == 2
    return jax.shard_map(
        on_device_planes if sixteen else on_device_any,
        mesh=mesh,
        in_specs=placed,
        out_specs=(
            P(("rep", "shard"), None),
            P(("rep", "shard"), None),
            P("shard"),
            P("shard"),
            P("shard"),
            P("shard"),
        ),
        check_vma=False,
    )
```

```python
import functools
import math

import jax
import jax.numpy as jnp
from jax import lax
from jax.experimental import pallas as pl
from jax.experimental.pallas import tpu as pltpu
from jax.sharding import PartitionSpec as P

D = 768
HEADS = 12
HEAD = 64
FF = 3072
STEP = 3
HW = 768


norm_eps = 1e-05
adam_eps = 1e-06
beta_one = 0.9
beta_two = 0.98
learn_rate = 0.01
decay_rate = 0.01
masked_score = -1e30
inv_sqrt_two = 1.0 / math.sqrt(2.0)
inv_sqrt_tau = 1.0 / math.sqrt(2.0 * math.pi)


def layout():
    return [
        ("triple_weight", (D, 3 * HW)),
        ("output_weight", (HW, D)),
        ("expand_weight", (D, FF)),
        ("reduce_weight", (FF, D)),
        ("query_bias", (HW,)),
        ("value_bias", (HW,)),
        ("output_bias", (D,)),
        ("first_gain", (D,)),
        ("first_shift", (D,)),
        ("expand_bias", (FF,)),
        ("reduce_bias", (D,)),
        ("second_gain", (D,)),
        ("second_shift", (D,)),
    ]


def split_flat(flat_vector):
    pieces = {}
    offset = 0
    for entry_name, dims_of in layout():
        amount = math.prod(dims_of)
        pieces[entry_name] = flat_vector[offset : offset + amount].reshape(dims_of)
        offset = offset + amount
    return pieces


def inner_rows(left_side, right_side):
    return lax.dot_general(
        left_side, right_side, (((0,), (0,)), ((), ())), preferred_element_type=jnp.float32
    )


def by_transpose(left_side, right_side):
    return lax.dot_general(
        left_side, right_side, (((1,), (1,)), ((), ())), preferred_element_type=jnp.float32
    )


def heads_of(row_block):
    return row_block.reshape(row_block.shape[0], HEADS, HEAD)


def normalize(values_in):
    centered = values_in - jnp.mean(values_in, axis=-1, keepdims=True)
    inv_root = lax.rsqrt(jnp.mean(centered * centered, axis=-1, keepdims=True) + norm_eps)
    return (centered * inv_root, inv_root)


def norm_back(grad_in, normed, inv_root):
    return inv_root * (
        grad_in
        - jnp.mean(grad_in, axis=-1, keepdims=True)
        - normed * jnp.mean(grad_in * normed, axis=-1, keepdims=True)
    )


def gelu_slope(pre_act):
    return (
        0.5 * (1.0 + lax.erf(pre_act * inv_sqrt_two))
        + pre_act * jnp.exp(-0.5 * pre_act * pre_act) * inv_sqrt_tau
    )


def attention_scores(queries, key_rows, length):
    scores = jnp.einsum(
        "qhd,khd->hqk", heads_of(queries), heads_of(key_rows), preferred_element_type=jnp.float32
    ) * (1.0 / math.sqrt(HEAD))
    key_valid = jnp.arange(scores.shape[-1]) < length
    return jnp.where(key_valid, scores, masked_score)


def forward(tokens, length, prm):
    rows = tokens.shape[0]
    triple = jnp.dot(tokens, prm["triple_weight"], preferred_element_type=jnp.float32)
    queries = (triple[:, :HW] + prm["query_bias"].astype(jnp.float32)).astype(jnp.bfloat16)
    key_rows = triple[:, HW : 2 * HW].astype(jnp.bfloat16)
    value_rows = (triple[:, 2 * HW :] + prm["value_bias"].astype(jnp.float32)).astype(jnp.bfloat16)
    scores = attention_scores(queries, key_rows, length)
    top_score = jnp.max(scores, axis=-1, keepdims=True)
    log_total = top_score + jnp.log(jnp.sum(jnp.exp(scores - top_score), axis=-1, keepdims=True))
    soft_weights = jnp.exp(scores - log_total).astype(jnp.bfloat16)
    context = jnp.einsum(
        "hqk,khd->qhd", soft_weights, heads_of(value_rows), preferred_element_type=jnp.float32
    )
    context = context.reshape(rows, HW).astype(jnp.bfloat16)
    first_sum = (
        tokens.astype(jnp.float32)
        + jnp.dot(context, prm["output_weight"], preferred_element_type=jnp.float32)
        + prm["output_bias"].astype(jnp.float32)
    )
    normed_one, root_one = normalize(first_sum)
    middle = normed_one * prm["first_gain"].astype(jnp.float32) + prm["first_shift"].astype(
        jnp.float32
    )
    middle_b = middle.astype(jnp.bfloat16)
    pre_act = jnp.dot(middle_b, prm["expand_weight"], preferred_element_type=jnp.float32) + prm[
        "expand_bias"
    ].astype(jnp.float32)
    activated = (0.5 * pre_act * (1.0 + lax.erf(pre_act * inv_sqrt_two))).astype(jnp.bfloat16)
    second_sum = (
        middle
        + jnp.dot(activated, prm["reduce_weight"], preferred_element_type=jnp.float32)
        + prm["reduce_bias"].astype(jnp.float32)
    )
    normed_two, root_two = normalize(second_sum)
    block_out = (
        normed_two * prm["second_gain"].astype(jnp.float32)
        + prm["second_shift"].astype(jnp.float32)
    ).astype(jnp.bfloat16)
    kept = (
        queries,
        key_rows,
        value_rows,
        log_total,
        context,
        normed_one,
        root_one,
        middle_b,
        pre_act,
        activated,
        normed_two,
        root_two,
    )
    return (block_out, kept)


def backward(tokens, length, cotangent, kept, prm):
    (
        queries,
        key_rows,
        value_rows,
        log_total,
        context,
        normed_one,
        root_one,
        middle_b,
        pre_act,
        activated,
        normed_two,
        root_two,
    ) = kept
    rows = tokens.shape[0]
    grad_out = cotangent.astype(jnp.float32)
    d_second = norm_back(grad_out * prm["second_gain"].astype(jnp.float32), normed_two, root_two)
    d_second_b = d_second.astype(jnp.bfloat16)
    d_pre = by_transpose(d_second_b, prm["reduce_weight"]) * gelu_slope(pre_act)
    d_pre_b = d_pre.astype(jnp.bfloat16)
    d_middle = d_second + by_transpose(d_pre_b, prm["expand_weight"])
    d_first = norm_back(d_middle * prm["first_gain"].astype(jnp.float32), normed_one, root_one)
    d_first_b = d_first.astype(jnp.bfloat16)
    d_context = by_transpose(d_first_b, prm["output_weight"]).astype(jnp.bfloat16)
    scores = attention_scores(queries, key_rows, length)
    soft_float = jnp.exp(scores - log_total)
    soft_weights = soft_float.astype(jnp.bfloat16)
    d_soft = jnp.einsum(
        "qhd,khd->hqk",
        heads_of(d_context),
        heads_of(value_rows),
        preferred_element_type=jnp.float32,
    )
    delta = jnp.sum(d_soft * soft_float, axis=-1, keepdims=True)
    d_scores = (soft_float * (d_soft - delta) * (1.0 / math.sqrt(HEAD))).astype(jnp.bfloat16)
    d_query = jnp.einsum(
        "hqk,khd->qhd", d_scores, heads_of(key_rows), preferred_element_type=jnp.float32
    ).reshape(rows, HW)
    d_keys = jnp.einsum(
        "hqk,qhd->khd", d_scores, heads_of(queries), preferred_element_type=jnp.float32
    ).reshape(rows, HW)
    d_values = jnp.einsum(
        "hqk,qhd->khd", soft_weights, heads_of(d_context), preferred_element_type=jnp.float32
    ).reshape(rows, HW)
    d_triple = jnp.concatenate([d_query, d_keys, d_values], axis=1).astype(jnp.bfloat16)
    input_grad = (d_first + by_transpose(d_triple, prm["triple_weight"])).astype(jnp.bfloat16)
    grad_list = [
        inner_rows(tokens, d_triple),
        inner_rows(context, d_first_b),
        inner_rows(middle_b, d_pre_b),
        inner_rows(activated, d_second_b),
        jnp.sum(d_query, axis=0),
        jnp.sum(d_values, axis=0),
        jnp.sum(d_first, axis=0),
        jnp.sum(d_middle * normed_one, axis=0),
        jnp.sum(d_middle, axis=0),
        jnp.sum(d_pre, axis=0),
        jnp.sum(d_second, axis=0),
        jnp.sum(grad_out * normed_two, axis=0),
        jnp.sum(grad_out, axis=0),
    ]
    flat_grad = jnp.concatenate([piece_grad.reshape(-1) for piece_grad in grad_list])
    return (input_grad, flat_grad)


def adamw(param_now, first_now, second_now, grad_total):
    first_new = beta_one * first_now + (1.0 - beta_one) * grad_total
    second_new = beta_two * second_now + (1.0 - beta_two) * grad_total * grad_total
    fix_one = 1.0 - beta_one**STEP
    fix_two = 1.0 - beta_two**STEP
    param_new = param_now - learn_rate * (
        first_new / fix_one / (jnp.sqrt(second_new / fix_two) + adam_eps) + decay_rate * param_now
    )
    return (param_new, first_new, second_new)

ROW = 768
STEP_ROWS = 576
FRAME = 592
HALF = ROW // 2
LINES = FRAME * 6
LOCAL = 442944
LOCAL_LINES = 3464
ROWS = 16 * STEP_ROWS + 16
OUT_ROW = 2304
EXP_ROW = 3072
RED_ROW = 6144
BIAS_ROW = 9216
LEFT = 4608
FRONT = 72
BLOCKS = 2
BLOCK_LINES = 1736
RIGHT = 9 * HALF
MIB = 1024 * 1024

f32 = jnp.float32
bf16 = jnp.bfloat16


def place():
    here, core = lax.axis_index("shard"), lax.axis_index("rep")
    plane, spot = here // 4, here % 4
    flip = [0, core + 1, 2 - core, 3]
    back = [0, 2 - core, core + 1, 3]
    listed = [(9 * here) // 2, here % 2, 3 * core, 3 - 3 * core, HALF * core, HALF - HALF * core]
    listed += [(plane + 4 - t) % 4 for t in range(4)]
    return listed + [spot ^ k for k in flip] + [spot ^ k for k in back]


def swap_half(block):
    return pltpu.roll(block, 64, 1)


def frame_kernel(flat_ref, out_ref, lines):
    shift, odd, first_col = place()[:3]
    lines[0:FRONT, :] = jnp.zeros((FRONT, 128), f32)
    lines[FRONT : FRONT + 3456, :] = flat_ref[pl.ds(0, 442368)].reshape(3456, 128)
    lines[FRONT + 3456 : FRONT + LINES, :] = jnp.zeros((LINES - 3456, 128), f32)
    lines[FRONT + 3456 : FRONT + 3460, :] = flat_ref[pl.ds(442368, 512)].reshape(4, 128)
    lines[FRONT + 3460 : FRONT + 3461, 0:64] = flat_ref[pl.ds(442880, 64)].reshape(1, 64)
    low = lax.broadcasted_iota(jnp.int32, (FRAME, 128), 1) < 64
    for j in range(3):
        at = FRONT + first_col + j - shift
        here = lines[pl.ds(at, FRAME, stride=6), :]
        before = lines[pl.ds(at - 1, FRAME, stride=6), :]
        moved = jnp.where(low, swap_half(before), swap_half(here))
        out_ref[:, 128 * j : 128 * (j + 1)] = jnp.where(odd == 1, moved, here).astype(bf16)


def make_frame(params):
    return pl.pallas_call(
        frame_kernel,
        out_shape=jax.ShapeDtypeStruct((FRAME, HALF), bf16),
        in_specs=[pl.BlockSpec(memory_space=pltpu.VMEM)],
        out_specs=pl.BlockSpec(memory_space=pltpu.VMEM),
        scratch_shapes=[pltpu.VMEM((FRONT + LINES, 128), f32)],
        compiler_params=pltpu.CompilerParams(vmem_limit_bytes=12 * MIB),
    )(params)


def finish_kernel(
    mine_ref, other_ref, param_ref, first_ref, second_ref, grad_out, param_out, first_out, second_out, framed
):
    shift, odd, first_col, other_col = place()[:4]
    step = pl.program_id(0)

    @pl.when(step == 0)
    def _():
        framed[LINES : LINES + 48, :] = jnp.zeros((48, 128), f32)
        for j in range(3):
            at = slice(128 * j, 128 * (j + 1))
            framed[pl.ds(first_col + j, FRAME, stride=6), :] = mine_ref[:, at]
            framed[pl.ds(other_col + j, FRAME, stride=6), :] = other_ref[:, at]

    low = lax.broadcasted_iota(jnp.int32, (BLOCK_LINES, 128), 1) < 64
    here = framed[pl.ds(shift + BLOCK_LINES * step, BLOCK_LINES), :]
    after = framed[pl.ds(shift + BLOCK_LINES * step + 1, BLOCK_LINES), :]
    moved = jnp.where(low, swap_half(here), swap_half(after))
    grad = jnp.where(odd == 1, moved, here).reshape(BLOCK_LINES * 128)
    grad_out[...] = grad
    new_param, new_first, new_second = adamw(param_ref[...], first_ref[...], second_ref[...], grad)
    param_out[...] = new_param
    first_out[...] = new_first
    second_out[...] = new_second


def finish(mine, other, params, first_moment, second_moment):
    vmem_spec = pl.BlockSpec(memory_space=pltpu.VMEM)
    block_spec = pl.BlockSpec((BLOCK_LINES * 128,), lambda i: (i,))
    return pl.pallas_call(
        finish_kernel,
        grid=(BLOCKS,),
        out_shape=[jax.ShapeDtypeStruct((LOCAL,), f32)] * 4,
        in_specs=[vmem_spec, vmem_spec] + [block_spec] * 3,
        out_specs=[block_spec] * 4,
        scratch_shapes=[pltpu.VMEM((LINES + 48, 128), f32)],
        compiler_params=pltpu.CompilerParams(vmem_limit_bytes=30 * MIB),
    )(mine, other, params, first_moment, second_moment)


def dot_nn(left_side, right_side):
    return jnp.dot(left_side, right_side, preferred_element_type=f32)


def row_mean(block):
    return jnp.mean(block, axis=-1, keepdims=True)


def layer_kernel(length_ref, tokens_ref, cot_ref, *refs):
    frames = refs[:32]
    block_ref, input_ref, left_ref, right_ref, sums_ref = refs[32:37]
    (
        weights,
        triple_w,
        expand_w,
        tails,
        stage,
        triple_b,
        soft_all,
        slope_all,
        rights,
        sem_main,
        sem_tail,
    ) = refs[37:]
    bias_grads = sums_ref
    meta = place()
    length = length_ref[0]
    cols = (pl.multiple_of(meta[4], 128), pl.multiple_of(meta[5], 128))

    def main_copy(frame, shard, side):
        return pltpu.make_async_copy(
            frame.at[pl.ds(0, STEP_ROWS), :],
            weights.at[pl.ds(pl.multiple_of(shard * STEP_ROWS, 16), STEP_ROWS), pl.ds(cols[side], HALF)],
            sem_main.at[side, shard],
        )

    def tail_copy(frame, shard, side):
        return pltpu.make_async_copy(
            frame.at[pl.ds(STEP_ROWS, 16), :],
            tails.at[shard, :, pl.ds(cols[side], HALF)],
            sem_tail.at[side, shard],
        )

    def each_frame(t):
        for side in range(2):
            for j in range(4):
                yield frames[16 * side + 4 * t + j], 4 * meta[6 + t] + meta[10 + 4 * side + j], side

    for t in range(4):
        for frame, shard, side in each_frame(t):
            tail_copy(frame, shard, side).start()
    for now in (True, False):
        for t in range(4):

            @pl.when((meta[6 + t] == 0) == now)
            def _():
                for frame, shard, side in each_frame(t):
                    main_copy(frame, shard, side).start()

    def arrive(first, last):
        for shard in range(first, last):
            for side in range(2):
                main_copy(frames[0], shard, side).wait()
            if shard > 0:
                for side in range(2):
                    tail_copy(frames[0], shard - 1, side).wait()
                at = STEP_ROWS * shard
                joined = weights[at : at + 16, :].astype(f32) + tails[shard - 1].astype(f32)
                weights[at : at + 16, :] = joined.astype(bf16)

    for side in range(2):
        tail_copy(frames[0], 15, side).wait()
    arrive(0, 4)

    def spread_triple(i, carry):
        for j in range(6):
            at = slice(128 * j, 128 * (j + 1))
            stage[j, 0:384, :] = weights[pl.ds(pl.multiple_of(384 * i, 16), 384), at].astype(f32)
            for part in range(3):
                rows = stage[j, pl.ds(part, 128, stride=3), :]
                triple_w[part, pl.ds(pl.multiple_of(128 * i, 16), 128), at] = rows.astype(bf16)
        return carry

    lax.fori_loop(0, 6, spread_triple, 0)

    def spread_expand(i, carry):
        row = pl.multiple_of(EXP_ROW + 512 * i, 16)
        for j in range(6):
            at = slice(128 * j, 128 * (j + 1))
            stage[j, :, :] = weights[pl.ds(row, 512), at].astype(f32)
            for part in range(4):
                rows = stage[j, pl.ds(part, 128, stride=4), :]
                expand_w[part, pl.ds(pl.multiple_of(128 * i, 16), 128), at] = rows.astype(bf16)
        return carry

    biases = tails[15].astype(f32)

    def bias(index):
        return biases[index : index + 1, :]

    bias_grads[...] = jnp.zeros((16, ROW), f32)

    def keep_bias(index, block):
        bias_grads[index : index + 1, :] = jnp.sum(block, axis=0, keepdims=True)

    tokens = tokens_ref[...]
    triple_b[0] = (dot_nn(tokens, triple_w[0]) + bias(0)).astype(bf16)
    triple_b[1] = dot_nn(tokens, triple_w[1]).astype(bf16)
    triple_b[2] = (dot_nn(tokens, triple_w[2]) + bias(1)).astype(bf16)

    lane = lax.broadcasted_iota(jnp.int32, (1, 128), 1)
    head_masks = ((lane < 64).astype(f32).astype(bf16), (lane >= 64).astype(f32).astype(bf16))
    key_valid = lax.broadcasted_iota(jnp.int32, (128, 128), 1) < length
    scale = 1.0 / math.sqrt(HEAD)
    for pair in range(6):
        at = slice(128 * pair, 128 * (pair + 1))
        queries, key_rows, value_rows = triple_b[0, :, at], triple_b[1, :, at], triple_b[2, :, at]
        context = jnp.zeros((128, 128), f32)
        for side in range(2):
            scores = by_transpose(queries * head_masks[side], key_rows) * scale
            scores = jnp.where(key_valid, scores, masked_score)
            top_score = jnp.max(scores, axis=-1, keepdims=True)
            log_total = top_score + jnp.log(
                jnp.sum(jnp.exp(scores - top_score), axis=-1, keepdims=True)
            )
            soft_float = jnp.exp(scores - log_total)
            soft_all[2 * pair + side] = soft_float
            context = context + dot_nn(soft_float.astype(bf16), value_rows * head_masks[side])
        left_ref[:, at] = context.astype(bf16)

    arrive(4, 6)
    first_sum = tokens.astype(f32) + dot_nn(left_ref[:, 0:768], weights[OUT_ROW : OUT_ROW + 768, :]) + bias(2)
    normed_one, root_one = normalize(first_sum)
    middle = normed_one * bias(3) + bias(4)
    middle_b = middle.astype(bf16)
    left_ref[:, 768:1536] = middle_b
    second_sum = middle + bias(9)
    arrive(6, 11)
    lax.fori_loop(0, 6, spread_expand, 0)
    arrive(11, 16)
    for part in range(4):
        at = slice(768 * part, 768 * (part + 1))
        pre_act = dot_nn(middle_b, expand_w[part]) + bias(5 + part)
        erf_term = 1.0 + lax.erf(pre_act * inv_sqrt_two)
        activated = (0.5 * pre_act * erf_term).astype(bf16)
        left_ref[:, 1536 + 768 * part : 1536 + 768 * (part + 1)] = activated
        slope_all[:, at] = 0.5 * erf_term + pre_act * jnp.exp(-0.5 * pre_act * pre_act) * inv_sqrt_tau
        red_at = RED_ROW + 768 * part
        second_sum = second_sum + dot_nn(activated, weights[red_at : red_at + 768, :])
    normed_two, root_two = normalize(second_sum)
    block_ref[...] = (normed_two * bias(10) + bias(11)).astype(bf16)

    grad_out = cot_ref[...].astype(f32)
    keep_bias(10, grad_out * normed_two)
    keep_bias(11, grad_out)
    d_second = norm_back(grad_out * bias(10), normed_two, root_two)
    keep_bias(9, d_second)
    d_second_b = d_second.astype(bf16)
    d_middle = d_second
    for part in range(4):
        at = slice(768 * part, 768 * (part + 1))
        red_at = RED_ROW + 768 * part
        d_pre = by_transpose(d_second_b, weights[red_at : red_at + 768, :]) * slope_all[:, at]
        keep_bias(5 + part, d_pre)
        d_pre_b = d_pre.astype(bf16)
        rights[1 + part] = d_pre_b
        d_middle = d_middle + by_transpose(d_pre_b, expand_w[part])

    rights[5] = d_second_b
    keep_bias(3, d_middle * normed_one)
    keep_bias(4, d_middle)
    d_first = norm_back(d_middle * bias(3), normed_one, root_one)
    keep_bias(2, d_first)
    d_first_b = d_first.astype(bf16)
    d_context_b = by_transpose(d_first_b, weights[OUT_ROW : OUT_ROW + 768, :]).astype(bf16)

    rights[0] = d_first_b
    for pair in range(6):
        at = slice(128 * pair, 128 * (pair + 1))
        queries, key_rows, value_rows = triple_b[0, :, at], triple_b[1, :, at], triple_b[2, :, at]
        d_context = d_context_b[:, at]
        d_query = jnp.zeros((128, 128), f32)
        d_keys = jnp.zeros((128, 128), f32)
        d_values = jnp.zeros((128, 128), f32)
        for side in range(2):
            soft_float = soft_all[2 * pair + side]
            d_part = d_context * head_masks[side]
            d_soft = by_transpose(d_part, value_rows)
            delta = jnp.sum(d_soft * soft_float, axis=-1, keepdims=True)
            d_scores = (soft_float * (d_soft - delta) * scale).astype(bf16)
            d_query = d_query + dot_nn(d_scores, key_rows * head_masks[side])
            d_keys = d_keys + inner_rows(d_scores, queries * head_masks[side])
            d_values = d_values + inner_rows(soft_float.astype(bf16), d_part)
        bias_grads[0:1, at] = jnp.sum(d_query, axis=0, keepdims=True)
        bias_grads[1:2, at] = jnp.sum(d_values, axis=0, keepdims=True)
        rights[6, :, at] = d_query.astype(bf16)
        rights[7, :, at] = d_keys.astype(bf16)
        rights[8, :, at] = d_values.astype(bf16)

    input_grad = d_first
    for part in range(3):
        input_grad = input_grad + by_transpose(rights[6 + part], triple_w[part])
    input_ref[...] = input_grad.astype(bf16)

    for k in range(9):
        right_ref[:, HALF * k : HALF * (k + 1)] = rights[k, :, pl.ds(cols[0], HALF)]
        left_ref[:, 4608 + HALF * k : 4608 + HALF * (k + 1)] = rights[k, :, pl.ds(cols[1], HALF)]


def run_layer(lengths, tokens, cotangent, frames):
    any_spec = pl.BlockSpec(memory_space=pl.ANY)
    vmem_spec = pl.BlockSpec(memory_space=pltpu.VMEM)
    rows = tokens.shape[0]
    thin = jax.ShapeDtypeStruct((rows, D), bf16)
    out = pl.pallas_call(
        layer_kernel,
        out_shape=[
            thin,
            thin,
            jax.ShapeDtypeStruct((rows, LEFT + RIGHT), bf16),
            jax.ShapeDtypeStruct((rows, RIGHT), bf16),
            jax.ShapeDtypeStruct((16, ROW), f32),
        ],
        in_specs=[pl.BlockSpec(memory_space=pltpu.SMEM)] + [vmem_spec] * 2 + [any_spec] * 32,
        out_specs=[vmem_spec] * 5,
        scratch_shapes=[
            pltpu.VMEM((ROWS, ROW), bf16),
            pltpu.VMEM((3, D, HW), bf16),
            pltpu.VMEM((4, D, ROW), bf16),
            pltpu.VMEM((16, 16, ROW), bf16),
            pltpu.VMEM((6, 512, 128), f32),
            pltpu.VMEM((3, rows, HW), bf16),
            pltpu.VMEM((HEADS, rows, rows), f32),
            pltpu.VMEM((rows, FF), f32),
            pltpu.VMEM((9, rows, HW), bf16),
            pltpu.SemaphoreType.DMA((2, 16)),
            pltpu.SemaphoreType.DMA((2, 16)),
        ],
        compiler_params=pltpu.CompilerParams(vmem_limit_bytes=42 * MIB),
    )(lengths, tokens, cotangent, *frames)
    return out


def grad_kernel(
    slot,
    tokens_ref,
    tokens_other,
    left_ref,
    left_other,
    right_ref,
    sums_ref,
    sums_other,
    low_ref,
    high_ref,
    left,
    right,
    grads,
    stage,
    sem_in,
    sem_out,
):
    meta = place()
    quad = meta[6 + slot]

    def load(pieces):
        copies = []
        for k, (source, first, size, target, at, row) in enumerate(pieces):
            copies.append(
                pltpu.make_async_copy(
                    source.at[:, pl.ds(first, size)],
                    target.at[pl.ds(row, 128), pl.ds(at, size)],
                    sem_in.at[k],
                )
            )
        for copy in copies:
            copy.start()
        for copy in copies:
            copy.wait()

    def left_pieces(first, size, at):
        return [(left_ref, first, size, left, at, 0), (left_other, first, size, left, at, 128)]

    def right_pieces(first, size, at):
        return [
            (right_ref, first, size, right, at, 0),
            (left_other, LEFT + first, size, right, at, 128),
        ]

    def mixed(first, right_first, parts, chunks, row, rows_used):
        def step(i, carry):
            rows = left[:, pl.ds(pl.multiple_of(first + 128 * i, 128), 128)]
            for part in range(parts):
                at = right_first + HALF * part
                block = inner_rows(rows, right[:, at : at + HALF])
                for j in range(3):
                    stage[j, pl.ds(part, 128, stride=parts), :] = block[:, 128 * j : 128 * (j + 1)]
            at = pl.multiple_of(row + 128 * parts * i, 16)
            for j in range(3):
                grads[pl.ds(at, rows_used), 128 * j : 128 * (j + 1)] = stage[j, 0:rows_used, :].astype(bf16)
            return carry

        lax.fori_loop(0, chunks, step, 0, unroll=min(chunks, 3))

    def plain(first, right_first, chunks, row):
        def step(i, carry):
            rows = left[:, pl.ds(pl.multiple_of(first + 256 * i, 128), 256)]
            block = inner_rows(rows, right[:, right_first : right_first + HALF])
            grads[pl.ds(pl.multiple_of(row + 256 * i, 16), 256), :] = block.astype(bf16)
            return carry

        lax.fori_loop(0, chunks, step, 0, unroll=min(chunks, 3))

    def last_rows(first, right_first):
        block = inner_rows(left[:, first : first + 128], right[:, right_first : right_first + HALF])
        grads[2304:2320, :] = block[0:16].astype(bf16)

    @pl.when(quad == 0)
    def _():
        load(
            [(tokens_ref, 0, 768, left, 0, 0), (tokens_other, 0, 768, left, 0, 128)]
            + left_pieces(0, 128, 768)
            + right_pieces(2304, 1152, 0)
            + right_pieces(0, 384, 1152)
        )
        mixed(0, 0, 3, 6, 0, 384)
        last_rows(768, 1152)

    @pl.when(quad == 1)
    def _():
        load(left_pieces(0, 1280, 0) + right_pieces(0, 1920, 0))
        plain(0, 0, 3, 0)
        mixed(768, 384, 4, 3, 768, 512)
        mixed(1152, 384, 4, 1, 2304, 16)

    @pl.when(quad == 2)
    def _():
        load(left_pieces(1152, 1280, 0) + right_pieces(384, 1920, 0))
        mixed(0, 0, 4, 3, 0, 512)
        plain(384, 1536, 3, 1536)
        last_rows(1152, 1536)

    @pl.when(quad == 3)
    def _():
        load(left_pieces(2304, 2304, 0) + right_pieces(1920, 384, 0))
        plain(0, 0, 9, 0)
        own = pl.ds(pl.multiple_of(meta[4], 128), HALF)
        grads[2304:2320, :] = (sums_ref[:, own] + sums_other[:, own]).astype(bf16)

    departures = []
    for j in (2, 3, 0, 1):
        row = pl.multiple_of(meta[10 + j] * STEP_ROWS, 16)
        target = (low_ref, high_ref)[j // 2].at[j % 2]
        copy = pltpu.make_async_copy(grads.at[pl.ds(row, FRAME), :], target, sem_out.at[j])
        copy.start()
        departures.append(copy)
    for copy in departures:
        copy.wait()


def quad_grads(slot, operands):
    any_spec = pl.BlockSpec(memory_space=pl.ANY)
    hbm_spec = pl.BlockSpec(memory_space=pltpu.HBM)
    vmem_spec = pl.BlockSpec(memory_space=pltpu.VMEM)
    frames = jax.ShapeDtypeStruct((2, FRAME, HALF), bf16)
    return pl.pallas_call(
        functools.partial(grad_kernel, slot),
        out_shape=[frames, frames],
        in_specs=[any_spec] * 2 + [hbm_spec, any_spec, hbm_spec] + [vmem_spec] * 2,
        out_specs=[any_spec] * 2,
        scratch_shapes=[
            pltpu.VMEM((256, 2304), bf16),
            pltpu.VMEM((256, 1920), bf16),
            pltpu.VMEM((4 * STEP_ROWS + 16, HALF), bf16),
            pltpu.VMEM((3, 512, 128), f32),
            pltpu.SemaphoreType.DMA((8,)),
            pltpu.SemaphoreType.DMA((4,)),
        ],
        compiler_params=pltpu.CompilerParams(vmem_limit_bytes=14 * MIB),
        cost_estimate=pl.CostEstimate(flops=1000, bytes_accessed=1000, transcendentals=0),
    )(*operands)


def plane_moves(n):
    near, far = [], []
    for s in range(n):
        near += [(s, s ^ 1), (n + s, n + (s ^ 2))]
        far += [(s, s ^ 2), (n + s, n + (s ^ 1))]
    return near, far


def on_device_planes(hidden_states, cotangent, lengths, params, first_moment, second_moment):
    n = 16
    both = ("rep", "shard")
    near, far = plane_moves(n)
    swap = [(0, 1), (1, 0)]
    own = make_frame(params)
    mine, other = [], []
    up = [(s, (s + 4) % n) for s in range(n)]
    down = [(s, (s - 4) % n) for s in range(n)]
    zero = None
    for t in range(4):
        zero = own if t == 0 else lax.ppermute(zero, "shard", up)
        one = lax.ppermute(zero, both, near)
        two = lax.ppermute(zero, both, far)
        three = lax.ppermute(one, both, far)
        group = [zero, one, two, three]
        mine += group
        other += [lax.ppermute(piece, "rep", swap) for piece in group]

    block_out, input_grad, left, right, sums = run_layer(lengths, hidden_states, cotangent, mine + other)

    operands = (
        hidden_states,
        lax.ppermute(hidden_states, "rep", swap),
        left,
        lax.ppermute(left, "rep", swap),
        right,
        sums,
        lax.ppermute(sums, "rep", swap),
    )
    passed = None
    for t in (3, 2, 1, 0):
        low, high = quad_grads(t, operands)
        from_far = lax.ppermute(high, both, far)
        away = (low[1].astype(f32) + from_far[1].astype(f32)).astype(bf16)
        from_near = lax.ppermute(away, both, near)
        total = low[0].astype(f32) + from_far[0].astype(f32) + from_near.astype(f32)
        if passed is not None:
            total = total + passed.astype(f32)
        if t > 0:
            passed = lax.ppermute(total.astype(bf16), "shard", down)
    weight_grad, new_params, new_first, new_second = finish(
        total, lax.ppermute(total, "rep", swap), params, first_moment, second_moment
    )
    return (block_out, input_grad, weight_grad, new_params, new_first, new_second)


def on_device_any(hidden_states, cotangent, lengths, params, first_moment, second_moment):
    length = lengths[0]
    gathered = lax.all_gather(params.astype(jnp.bfloat16), "shard", axis=0, tiled=True)
    prm = split_flat(gathered)
    block_out, kept = forward(hidden_states, length, prm)
    input_grad, flat_grad = backward(hidden_states, length, cotangent, kept, prm)
    owned = lax.psum_scatter(flat_grad, "shard", scatter_dimension=0, tiled=True)
    weight_grad = lax.psum(owned, "rep")
    new_params, new_first, new_second = adamw(params, first_moment, second_moment, weight_grad)
    return (block_out, input_grad, weight_grad, new_params, new_first, new_second)


def solution(mesh):
    placed = (
        P(("rep", "shard"), None),
        P(("rep", "shard"), None),
        P(("rep", "shard")),
        P("shard"),
        P("shard"),
        P("shard"),
    )
    sixteen = mesh.shape["shard"] == 16 and mesh.shape["rep"] == 2
    return jax.shard_map(
        on_device_planes if sixteen else on_device_any,
        mesh=mesh,
        in_specs=placed,
        out_specs=(
            P(("rep", "shard"), None),
            P(("rep", "shard"), None),
            P("shard"),
            P("shard"),
            P("shard"),
            P("shard"),
        ),
        check_vma=False,
    )
```

```python
import functools
import math

import jax
import jax.numpy as jnp
from jax import lax
from jax.experimental import pallas as pl
from jax.experimental.pallas import tpu as pltpu
from jax.sharding import PartitionSpec as P

D = 768
HEADS = 12
HEAD = 64
FF = 3072
STEP = 3
HW = 768


norm_eps = 1e-05
adam_eps = 1e-06
beta_one = 0.9
beta_two = 0.98
learn_rate = 0.01
decay_rate = 0.01
masked_score = -1e30
inv_sqrt_two = 1.0 / math.sqrt(2.0)
inv_sqrt_tau = 1.0 / math.sqrt(2.0 * math.pi)


def layout():
    return [
        ("triple_weight", (D, 3 * HW)),
        ("output_weight", (HW, D)),
        ("expand_weight", (D, FF)),
        ("reduce_weight", (FF, D)),
        ("query_bias", (HW,)),
        ("value_bias", (HW,)),
        ("output_bias", (D,)),
        ("first_gain", (D,)),
        ("first_shift", (D,)),
        ("expand_bias", (FF,)),
        ("reduce_bias", (D,)),
        ("second_gain", (D,)),
        ("second_shift", (D,)),
    ]


def split_flat(flat_vector):
    pieces = {}
    offset = 0
    for entry_name, dims_of in layout():
        amount = math.prod(dims_of)
        pieces[entry_name] = flat_vector[offset : offset + amount].reshape(dims_of)
        offset = offset + amount
    return pieces


def inner_rows(left_side, right_side):
    return lax.dot_general(
        left_side, right_side, (((0,), (0,)), ((), ())), preferred_element_type=jnp.float32
    )


def by_transpose(left_side, right_side):
    return lax.dot_general(
        left_side, right_side, (((1,), (1,)), ((), ())), preferred_element_type=jnp.float32
    )


def heads_of(row_block):
    return row_block.reshape(row_block.shape[0], HEADS, HEAD)


def normalize(values_in):
    centered = values_in - jnp.mean(values_in, axis=-1, keepdims=True)
    inv_root = lax.rsqrt(jnp.mean(centered * centered, axis=-1, keepdims=True) + norm_eps)
    return (centered * inv_root, inv_root)


def norm_back(grad_in, normed, inv_root):
    return inv_root * (
        grad_in
        - jnp.mean(grad_in, axis=-1, keepdims=True)
        - normed * jnp.mean(grad_in * normed, axis=-1, keepdims=True)
    )


def gelu_slope(pre_act):
    return (
        0.5 * (1.0 + lax.erf(pre_act * inv_sqrt_two))
        + pre_act * jnp.exp(-0.5 * pre_act * pre_act) * inv_sqrt_tau
    )


def attention_scores(queries, key_rows, length):
    scores = jnp.einsum(
        "qhd,khd->hqk", heads_of(queries), heads_of(key_rows), preferred_element_type=jnp.float32
    ) * (1.0 / math.sqrt(HEAD))
    key_valid = jnp.arange(scores.shape[-1]) < length
    return jnp.where(key_valid, scores, masked_score)


def forward(tokens, length, prm):
    rows = tokens.shape[0]
    triple = jnp.dot(tokens, prm["triple_weight"], preferred_element_type=jnp.float32)
    queries = (triple[:, :HW] + prm["query_bias"].astype(jnp.float32)).astype(jnp.bfloat16)
    key_rows = triple[:, HW : 2 * HW].astype(jnp.bfloat16)
    value_rows = (triple[:, 2 * HW :] + prm["value_bias"].astype(jnp.float32)).astype(jnp.bfloat16)
    scores = attention_scores(queries, key_rows, length)
    top_score = jnp.max(scores, axis=-1, keepdims=True)
    log_total = top_score + jnp.log(jnp.sum(jnp.exp(scores - top_score), axis=-1, keepdims=True))
    soft_weights = jnp.exp(scores - log_total).astype(jnp.bfloat16)
    context = jnp.einsum(
        "hqk,khd->qhd", soft_weights, heads_of(value_rows), preferred_element_type=jnp.float32
    )
    context = context.reshape(rows, HW).astype(jnp.bfloat16)
    first_sum = (
        tokens.astype(jnp.float32)
        + jnp.dot(context, prm["output_weight"], preferred_element_type=jnp.float32)
        + prm["output_bias"].astype(jnp.float32)
    )
    normed_one, root_one = normalize(first_sum)
    middle = normed_one * prm["first_gain"].astype(jnp.float32) + prm["first_shift"].astype(
        jnp.float32
    )
    middle_b = middle.astype(jnp.bfloat16)
    pre_act = jnp.dot(middle_b, prm["expand_weight"], preferred_element_type=jnp.float32) + prm[
        "expand_bias"
    ].astype(jnp.float32)
    activated = (0.5 * pre_act * (1.0 + lax.erf(pre_act * inv_sqrt_two))).astype(jnp.bfloat16)
    second_sum = (
        middle
        + jnp.dot(activated, prm["reduce_weight"], preferred_element_type=jnp.float32)
        + prm["reduce_bias"].astype(jnp.float32)
    )
    normed_two, root_two = normalize(second_sum)
    block_out = (
        normed_two * prm["second_gain"].astype(jnp.float32)
        + prm["second_shift"].astype(jnp.float32)
    ).astype(jnp.bfloat16)
    kept = (
        queries,
        key_rows,
        value_rows,
        log_total,
        context,
        normed_one,
        root_one,
        middle_b,
        pre_act,
        activated,
        normed_two,
        root_two,
    )
    return (block_out, kept)


def backward(tokens, length, cotangent, kept, prm):
    (
        queries,
        key_rows,
        value_rows,
        log_total,
        context,
        normed_one,
        root_one,
        middle_b,
        pre_act,
        activated,
        normed_two,
        root_two,
    ) = kept
    rows = tokens.shape[0]
    grad_out = cotangent.astype(jnp.float32)
    d_second = norm_back(grad_out * prm["second_gain"].astype(jnp.float32), normed_two, root_two)
    d_second_b = d_second.astype(jnp.bfloat16)
    d_pre = by_transpose(d_second_b, prm["reduce_weight"]) * gelu_slope(pre_act)
    d_pre_b = d_pre.astype(jnp.bfloat16)
    d_middle = d_second + by_transpose(d_pre_b, prm["expand_weight"])
    d_first = norm_back(d_middle * prm["first_gain"].astype(jnp.float32), normed_one, root_one)
    d_first_b = d_first.astype(jnp.bfloat16)
    d_context = by_transpose(d_first_b, prm["output_weight"]).astype(jnp.bfloat16)
    scores = attention_scores(queries, key_rows, length)
    soft_float = jnp.exp(scores - log_total)
    soft_weights = soft_float.astype(jnp.bfloat16)
    d_soft = jnp.einsum(
        "qhd,khd->hqk",
        heads_of(d_context),
        heads_of(value_rows),
        preferred_element_type=jnp.float32,
    )
    delta = jnp.sum(d_soft * soft_float, axis=-1, keepdims=True)
    d_scores = (soft_float * (d_soft - delta) * (1.0 / math.sqrt(HEAD))).astype(jnp.bfloat16)
    d_query = jnp.einsum(
        "hqk,khd->qhd", d_scores, heads_of(key_rows), preferred_element_type=jnp.float32
    ).reshape(rows, HW)
    d_keys = jnp.einsum(
        "hqk,qhd->khd", d_scores, heads_of(queries), preferred_element_type=jnp.float32
    ).reshape(rows, HW)
    d_values = jnp.einsum(
        "hqk,qhd->khd", soft_weights, heads_of(d_context), preferred_element_type=jnp.float32
    ).reshape(rows, HW)
    d_triple = jnp.concatenate([d_query, d_keys, d_values], axis=1).astype(jnp.bfloat16)
    input_grad = (d_first + by_transpose(d_triple, prm["triple_weight"])).astype(jnp.bfloat16)
    grad_list = [
        inner_rows(tokens, d_triple),
        inner_rows(context, d_first_b),
        inner_rows(middle_b, d_pre_b),
        inner_rows(activated, d_second_b),
        jnp.sum(d_query, axis=0),
        jnp.sum(d_values, axis=0),
        jnp.sum(d_first, axis=0),
        jnp.sum(d_middle * normed_one, axis=0),
        jnp.sum(d_middle, axis=0),
        jnp.sum(d_pre, axis=0),
        jnp.sum(d_second, axis=0),
        jnp.sum(grad_out * normed_two, axis=0),
        jnp.sum(grad_out, axis=0),
    ]
    flat_grad = jnp.concatenate([piece_grad.reshape(-1) for piece_grad in grad_list])
    return (input_grad, flat_grad)


def adamw(param_now, first_now, second_now, grad_total):
    first_new = beta_one * first_now + (1.0 - beta_one) * grad_total
    second_new = beta_two * second_now + (1.0 - beta_two) * grad_total * grad_total
    fix_one = 1.0 - beta_one**STEP
    fix_two = 1.0 - beta_two**STEP
    param_new = param_now - learn_rate * (
        first_new / fix_one / (jnp.sqrt(second_new / fix_two) + adam_eps) + decay_rate * param_now
    )
    return (param_new, first_new, second_new)

ROW = 768
STEP_ROWS = 576
FRAME = 592
HALF = ROW // 2
LINES = FRAME * 6
LOCAL = 442944
LOCAL_LINES = 3464
ROWS = 16 * STEP_ROWS + 16
OUT_ROW = 2304
EXP_ROW = 3072
RED_ROW = 6144
BIAS_ROW = 9216
LEFT = 4608
FRONT = 72
BLOCKS = 2
BLOCK_LINES = 1736
RIGHT = 9 * HALF
MIB = 1024 * 1024

f32 = jnp.float32
bf16 = jnp.bfloat16


def place():
    here, core = lax.axis_index("shard"), lax.axis_index("rep")
    plane, spot = here // 4, here % 4
    flip = [0, core + 1, 2 - core, 3]
    back = [0, 2 - core, core + 1, 3]
    listed = [(9 * here) // 2, here % 2, 3 * core, 3 - 3 * core, HALF * core, HALF - HALF * core]
    listed += [(plane + 4 - t) % 4 for t in range(4)]
    return listed + [spot ^ k for k in flip] + [spot ^ k for k in back]


def swap_half(block):
    return pltpu.roll(block, 64, 1)


def frame_kernel(flat_ref, out_ref, lines):
    shift, odd, first_col = place()[:3]
    lines[0:FRONT, :] = jnp.zeros((FRONT, 128), f32)
    lines[FRONT : FRONT + 3456, :] = flat_ref[pl.ds(0, 442368)].reshape(3456, 128)
    lines[FRONT + 3456 : FRONT + LINES, :] = jnp.zeros((LINES - 3456, 128), f32)
    lines[FRONT + 3456 : FRONT + 3460, :] = flat_ref[pl.ds(442368, 512)].reshape(4, 128)
    lines[FRONT + 3460 : FRONT + 3461, 0:64] = flat_ref[pl.ds(442880, 64)].reshape(1, 64)
    low = lax.broadcasted_iota(jnp.int32, (FRAME, 128), 1) < 64
    for j in range(3):
        at = FRONT + first_col + j - shift
        here = lines[pl.ds(at, FRAME, stride=6), :]
        before = lines[pl.ds(at - 1, FRAME, stride=6), :]
        moved = jnp.where(low, swap_half(before), swap_half(here))
        out_ref[:, 128 * j : 128 * (j + 1)] = jnp.where(odd == 1, moved, here).astype(bf16)


def make_frame(params):
    return pl.pallas_call(
        frame_kernel,
        out_shape=jax.ShapeDtypeStruct((FRAME, HALF), bf16),
        in_specs=[pl.BlockSpec(memory_space=pltpu.VMEM)],
        out_specs=pl.BlockSpec(memory_space=pltpu.VMEM),
        scratch_shapes=[pltpu.VMEM((FRONT + LINES, 128), f32)],
        compiler_params=pltpu.CompilerParams(vmem_limit_bytes=12 * MIB),
    )(params)


def finish_kernel(
    mine_ref, other_ref, param_ref, first_ref, second_ref, grad_out, param_out, first_out, second_out, framed
):
    shift, odd, first_col, other_col = place()[:4]
    step = pl.program_id(0)

    @pl.when(step == 0)
    def _():
        framed[LINES : LINES + 48, :] = jnp.zeros((48, 128), f32)
        for j in range(3):
            at = slice(128 * j, 128 * (j + 1))
            framed[pl.ds(first_col + j, FRAME, stride=6), :] = mine_ref[:, at]
            framed[pl.ds(other_col + j, FRAME, stride=6), :] = other_ref[:, at]

    low = lax.broadcasted_iota(jnp.int32, (BLOCK_LINES, 128), 1) < 64
    here = framed[pl.ds(shift + BLOCK_LINES * step, BLOCK_LINES), :]
    after = framed[pl.ds(shift + BLOCK_LINES * step + 1, BLOCK_LINES), :]
    moved = jnp.where(low, swap_half(here), swap_half(after))
    grad = jnp.where(odd == 1, moved, here).reshape(BLOCK_LINES * 128)
    grad_out[...] = grad
    new_param, new_first, new_second = adamw(param_ref[...], first_ref[...], second_ref[...], grad)
    param_out[...] = new_param
    first_out[...] = new_first
    second_out[...] = new_second


def finish(mine, other, params, first_moment, second_moment):
    vmem_spec = pl.BlockSpec(memory_space=pltpu.VMEM)
    block_spec = pl.BlockSpec((BLOCK_LINES * 128,), lambda i: (i,))
    return pl.pallas_call(
        finish_kernel,
        grid=(BLOCKS,),
        out_shape=[jax.ShapeDtypeStruct((LOCAL,), f32)] * 4,
        in_specs=[vmem_spec, vmem_spec] + [block_spec] * 3,
        out_specs=[block_spec] * 4,
        scratch_shapes=[pltpu.VMEM((LINES + 48, 128), f32)],
        compiler_params=pltpu.CompilerParams(vmem_limit_bytes=30 * MIB),
    )(mine, other, params, first_moment, second_moment)


def dot_nn(left_side, right_side):
    return jnp.dot(left_side, right_side, preferred_element_type=f32)


def row_mean(block):
    return jnp.mean(block, axis=-1, keepdims=True)


def layer_kernel(length_ref, tokens_ref, cot_ref, *refs):
    frames = refs[:32]
    block_ref, input_ref, left_ref, right_ref, sums_ref = refs[32:37]
    (
        weights,
        triple_w,
        expand_w,
        tails,
        stage,
        triple_b,
        soft_all,
        slope_all,
        rights,
        sem_main,
        sem_tail,
    ) = refs[37:]
    bias_grads = sums_ref
    meta = place()
    length = length_ref[0]
    cols = (pl.multiple_of(meta[4], 128), pl.multiple_of(meta[5], 128))

    def main_copy(frame, shard, side):
        return pltpu.make_async_copy(
            frame.at[pl.ds(0, STEP_ROWS), :],
            weights.at[pl.ds(pl.multiple_of(shard * STEP_ROWS, 16), STEP_ROWS), pl.ds(cols[side], HALF)],
            sem_main.at[side, shard],
        )

    def tail_copy(frame, shard, side):
        return pltpu.make_async_copy(
            frame.at[pl.ds(STEP_ROWS, 16), :],
            tails.at[shard, :, pl.ds(cols[side], HALF)],
            sem_tail.at[side, shard],
        )

    def each_frame(t):
        for side in range(2):
            for j in range(4):
                yield frames[16 * side + 4 * t + j], 4 * meta[6 + t] + meta[10 + 4 * side + j], side

    for t in range(4):
        for frame, shard, side in each_frame(t):
            tail_copy(frame, shard, side).start()
    for now in (True, False):
        for t in range(4):

            @pl.when((meta[6 + t] == 0) == now)
            def _():
                for frame, shard, side in each_frame(t):
                    main_copy(frame, shard, side).start()

    def arrive(first, last):
        for shard in range(first, last):
            for side in range(2):
                main_copy(frames[0], shard, side).wait()
            if shard > 0:
                for side in range(2):
                    tail_copy(frames[0], shard - 1, side).wait()
                at = STEP_ROWS * shard
                joined = weights[at : at + 16, :].astype(f32) + tails[shard - 1].astype(f32)
                weights[at : at + 16, :] = joined.astype(bf16)

    for side in range(2):
        tail_copy(frames[0], 15, side).wait()
    arrive(0, 4)

    def spread_triple(i, carry):
        for j in range(6):
            at = slice(128 * j, 128 * (j + 1))
            stage[j, 0:384, :] = weights[pl.ds(pl.multiple_of(384 * i, 16), 384), at].astype(f32)
            for part in range(3):
                rows = stage[j, pl.ds(part, 128, stride=3), :]
                triple_w[part, pl.ds(pl.multiple_of(128 * i, 16), 128), at] = rows.astype(bf16)
        return carry

    lax.fori_loop(0, 6, spread_triple, 0)

    def spread_expand(i, carry):
        row = pl.multiple_of(EXP_ROW + 512 * i, 16)
        for j in range(6):
            at = slice(128 * j, 128 * (j + 1))
            stage[j, :, :] = weights[pl.ds(row, 512), at].astype(f32)
            for part in range(4):
                rows = stage[j, pl.ds(part, 128, stride=4), :]
                expand_w[part, pl.ds(pl.multiple_of(128 * i, 16), 128), at] = rows.astype(bf16)
        return carry

    biases = tails[15].astype(f32)

    def bias(index):
        return biases[index : index + 1, :]

    bias_grads[...] = jnp.zeros((16, ROW), f32)

    def keep_bias(index, block):
        bias_grads[index : index + 1, :] = jnp.sum(block, axis=0, keepdims=True)

    tokens = tokens_ref[...]
    triple_b[0] = (dot_nn(tokens, triple_w[0]) + bias(0)).astype(bf16)
    triple_b[1] = dot_nn(tokens, triple_w[1]).astype(bf16)
    triple_b[2] = (dot_nn(tokens, triple_w[2]) + bias(1)).astype(bf16)

    lane = lax.broadcasted_iota(jnp.int32, (1, 128), 1)
    head_masks = ((lane < 64).astype(f32).astype(bf16), (lane >= 64).astype(f32).astype(bf16))
    key_valid = lax.broadcasted_iota(jnp.int32, (128, 128), 1) < length
    scale = 1.0 / math.sqrt(HEAD)
    for pair in range(6):
        at = slice(128 * pair, 128 * (pair + 1))
        queries, key_rows, value_rows = triple_b[0, :, at], triple_b[1, :, at], triple_b[2, :, at]
        context = jnp.zeros((128, 128), f32)
        for side in range(2):
            scores = by_transpose(queries * head_masks[side], key_rows) * scale
            scores = jnp.where(key_valid, scores, masked_score)
            top_score = jnp.max(scores, axis=-1, keepdims=True)
            log_total = top_score + jnp.log(
                jnp.sum(jnp.exp(scores - top_score), axis=-1, keepdims=True)
            )
            soft_float = jnp.exp(scores - log_total)
            soft_all[2 * pair + side] = soft_float
            context = context + dot_nn(soft_float.astype(bf16), value_rows * head_masks[side])
        left_ref[:, at] = context.astype(bf16)

    arrive(4, 6)
    first_sum = tokens.astype(f32) + dot_nn(left_ref[:, 0:768], weights[OUT_ROW : OUT_ROW + 768, :]) + bias(2)
    normed_one, root_one = normalize(first_sum)
    middle = normed_one * bias(3) + bias(4)
    middle_b = middle.astype(bf16)
    left_ref[:, 768:1536] = middle_b
    second_sum = middle + bias(9)
    arrive(6, 11)
    lax.fori_loop(0, 6, spread_expand, 0)
    arrive(11, 16)
    for part in range(4):
        at = slice(768 * part, 768 * (part + 1))
        pre_act = dot_nn(middle_b, expand_w[part]) + bias(5 + part)
        erf_term = 1.0 + lax.erf(pre_act * inv_sqrt_two)
        activated = (0.5 * pre_act * erf_term).astype(bf16)
        left_ref[:, 1536 + 768 * part : 1536 + 768 * (part + 1)] = activated
        slope_all[:, at] = 0.5 * erf_term + pre_act * jnp.exp(-0.5 * pre_act * pre_act) * inv_sqrt_tau
        red_at = RED_ROW + 768 * part
        second_sum = second_sum + dot_nn(activated, weights[red_at : red_at + 768, :])
    normed_two, root_two = normalize(second_sum)
    block_ref[...] = (normed_two * bias(10) + bias(11)).astype(bf16)

    grad_out = cot_ref[...].astype(f32)
    keep_bias(10, grad_out * normed_two)
    keep_bias(11, grad_out)
    d_second = norm_back(grad_out * bias(10), normed_two, root_two)
    keep_bias(9, d_second)
    d_second_b = d_second.astype(bf16)
    d_middle = d_second
    for part in range(4):
        at = slice(768 * part, 768 * (part + 1))
        red_at = RED_ROW + 768 * part
        d_pre = by_transpose(d_second_b, weights[red_at : red_at + 768, :]) * slope_all[:, at]
        keep_bias(5 + part, d_pre)
        d_pre_b = d_pre.astype(bf16)
        rights[1 + part] = d_pre_b
        d_middle = d_middle + by_transpose(d_pre_b, expand_w[part])

    rights[5] = d_second_b
    keep_bias(3, d_middle * normed_one)
    keep_bias(4, d_middle)
    d_first = norm_back(d_middle * bias(3), normed_one, root_one)
    keep_bias(2, d_first)
    d_first_b = d_first.astype(bf16)
    d_context_b = by_transpose(d_first_b, weights[OUT_ROW : OUT_ROW + 768, :]).astype(bf16)

    rights[0] = d_first_b
    for pair in range(6):
        at = slice(128 * pair, 128 * (pair + 1))
        queries, key_rows, value_rows = triple_b[0, :, at], triple_b[1, :, at], triple_b[2, :, at]
        d_context = d_context_b[:, at]
        d_query = jnp.zeros((128, 128), f32)
        d_keys = jnp.zeros((128, 128), f32)
        d_values = jnp.zeros((128, 128), f32)
        for side in range(2):
            soft_float = soft_all[2 * pair + side]
            d_part = d_context * head_masks[side]
            d_soft = by_transpose(d_part, value_rows)
            delta = jnp.sum(d_soft * soft_float, axis=-1, keepdims=True)
            d_scores = (soft_float * (d_soft - delta) * scale).astype(bf16)
            d_query = d_query + dot_nn(d_scores, key_rows * head_masks[side])
            d_keys = d_keys + inner_rows(d_scores, queries * head_masks[side])
            d_values = d_values + inner_rows(soft_float.astype(bf16), d_part)
        bias_grads[0:1, at] = jnp.sum(d_query, axis=0, keepdims=True)
        bias_grads[1:2, at] = jnp.sum(d_values, axis=0, keepdims=True)
        rights[6, :, at] = d_query.astype(bf16)
        rights[7, :, at] = d_keys.astype(bf16)
        rights[8, :, at] = d_values.astype(bf16)

    input_grad = d_first
    for part in range(3):
        input_grad = input_grad + by_transpose(rights[6 + part], triple_w[part])
    input_ref[...] = input_grad.astype(bf16)

    for k in range(9):
        right_ref[:, HALF * k : HALF * (k + 1)] = rights[k, :, pl.ds(cols[0], HALF)]
        left_ref[:, 4608 + HALF * k : 4608 + HALF * (k + 1)] = rights[k, :, pl.ds(cols[1], HALF)]


def run_layer(lengths, tokens, cotangent, frames):
    any_spec = pl.BlockSpec(memory_space=pl.ANY)
    vmem_spec = pl.BlockSpec(memory_space=pltpu.VMEM)
    rows = tokens.shape[0]
    thin = jax.ShapeDtypeStruct((rows, D), bf16)
    out = pl.pallas_call(
        layer_kernel,
        out_shape=[
            thin,
            thin,
            pltpu.VMEM((rows, LEFT + RIGHT), bf16),
            pltpu.VMEM((rows, RIGHT), bf16),
            jax.ShapeDtypeStruct((16, ROW), f32),
        ],
        in_specs=[pl.BlockSpec(memory_space=pltpu.SMEM)] + [vmem_spec] * 2 + [any_spec] * 32,
        out_specs=[vmem_spec] * 5,
        scratch_shapes=[
            pltpu.VMEM((ROWS, ROW), bf16),
            pltpu.VMEM((3, D, HW), bf16),
            pltpu.VMEM((4, D, ROW), bf16),
            pltpu.VMEM((16, 16, ROW), bf16),
            pltpu.VMEM((6, 512, 128), f32),
            pltpu.VMEM((3, rows, HW), bf16),
            pltpu.VMEM((HEADS, rows, rows), f32),
            pltpu.VMEM((rows, FF), f32),
            pltpu.VMEM((9, rows, HW), bf16),
            pltpu.SemaphoreType.DMA((2, 16)),
            pltpu.SemaphoreType.DMA((2, 16)),
        ],
        compiler_params=pltpu.CompilerParams(vmem_limit_bytes=42 * MIB),
    )(lengths, tokens, cotangent, *frames)
    return out


def grad_kernel(
    slot,
    tokens_ref,
    tokens_other,
    left_ref,
    left_other,
    right_ref,
    sums_ref,
    sums_other,
    low_ref,
    high_ref,
    left,
    right,
    grads,
    stage,
    sem_in,
    sem_out,
):
    meta = place()
    quad = meta[6 + slot]

    def load(pieces):
        copies = []
        for k, (source, first, size, target, at, row) in enumerate(pieces):
            copies.append(
                pltpu.make_async_copy(
                    source.at[:, pl.ds(first, size)],
                    target.at[pl.ds(row, 128), pl.ds(at, size)],
                    sem_in.at[k],
                )
            )
        for copy in copies:
            copy.start()
        for copy in copies:
            copy.wait()

    def left_pieces(first, size, at):
        return [(left_ref, first, size, left, at, 0), (left_other, first, size, left, at, 128)]

    def right_pieces(first, size, at):
        return [
            (right_ref, first, size, right, at, 0),
            (left_other, LEFT + first, size, right, at, 128),
        ]

    def mixed(first, right_first, parts, chunks, row, rows_used):
        def step(i, carry):
            rows = left[:, pl.ds(pl.multiple_of(first + 128 * i, 128), 128)]
            for part in range(parts):
                at = right_first + HALF * part
                block = inner_rows(rows, right[:, at : at + HALF])
                for j in range(3):
                    stage[j, pl.ds(part, 128, stride=parts), :] = block[:, 128 * j : 128 * (j + 1)]
            at = pl.multiple_of(row + 128 * parts * i, 16)
            for j in range(3):
                grads[pl.ds(at, rows_used), 128 * j : 128 * (j + 1)] = stage[j, 0:rows_used, :].astype(bf16)
            return carry

        lax.fori_loop(0, chunks, step, 0, unroll=min(chunks, 3))

    def plain(first, right_first, chunks, row):
        def step(i, carry):
            rows = left[:, pl.ds(pl.multiple_of(first + 256 * i, 128), 256)]
            block = inner_rows(rows, right[:, right_first : right_first + HALF])
            grads[pl.ds(pl.multiple_of(row + 256 * i, 16), 256), :] = block.astype(bf16)
            return carry

        lax.fori_loop(0, chunks, step, 0, unroll=min(chunks, 3))

    def last_rows(first, right_first):
        block = inner_rows(left[:, first : first + 128], right[:, right_first : right_first + HALF])
        grads[2304:2320, :] = block[0:16].astype(bf16)

    @pl.when(quad == 0)
    def _():
        load(
            [(tokens_ref, 0, 768, left, 0, 0), (tokens_other, 0, 768, left, 0, 128)]
            + left_pieces(0, 128, 768)
            + right_pieces(2304, 1152, 0)
            + right_pieces(0, 384, 1152)
        )
        mixed(0, 0, 3, 6, 0, 384)
        last_rows(768, 1152)

    @pl.when(quad == 1)
    def _():
        load(left_pieces(0, 1280, 0) + right_pieces(0, 1920, 0))
        plain(0, 0, 3, 0)
        mixed(768, 384, 4, 3, 768, 512)
        mixed(1152, 384, 4, 1, 2304, 16)

    @pl.when(quad == 2)
    def _():
        load(left_pieces(1152, 1280, 0) + right_pieces(384, 1920, 0))
        mixed(0, 0, 4, 3, 0, 512)
        plain(384, 1536, 3, 1536)
        last_rows(1152, 1536)

    @pl.when(quad == 3)
    def _():
        load(left_pieces(2304, 2304, 0) + right_pieces(1920, 384, 0))
        plain(0, 0, 9, 0)
        own = pl.ds(pl.multiple_of(meta[4], 128), HALF)
        grads[2304:2320, :] = (sums_ref[:, own] + sums_other[:, own]).astype(bf16)

    departures = []
    for j in (2, 3, 0, 1):
        row = pl.multiple_of(meta[10 + j] * STEP_ROWS, 16)
        target = (low_ref, high_ref)[j // 2].at[j % 2]
        copy = pltpu.make_async_copy(grads.at[pl.ds(row, FRAME), :], target, sem_out.at[j])
        copy.start()
        departures.append(copy)
    for copy in departures:
        copy.wait()


def quad_grads(slot, operands):
    any_spec = pl.BlockSpec(memory_space=pl.ANY)
    vmem_spec = pl.BlockSpec(memory_space=pltpu.VMEM)
    frames = jax.ShapeDtypeStruct((2, FRAME, HALF), bf16)
    return pl.pallas_call(
        functools.partial(grad_kernel, slot),
        out_shape=[frames, frames],
        in_specs=[any_spec] * 5 + [vmem_spec] * 2,
        out_specs=[any_spec] * 2,
        scratch_shapes=[
            pltpu.VMEM((256, 2304), bf16),
            pltpu.VMEM((256, 1920), bf16),
            pltpu.VMEM((4 * STEP_ROWS + 16, HALF), bf16),
            pltpu.VMEM((3, 512, 128), f32),
            pltpu.SemaphoreType.DMA((8,)),
            pltpu.SemaphoreType.DMA((4,)),
        ],
        compiler_params=pltpu.CompilerParams(vmem_limit_bytes=14 * MIB),
        cost_estimate=pl.CostEstimate(flops=1000, bytes_accessed=1000, transcendentals=0),
    )(*operands)


def plane_moves(n):
    near, far = [], []
    for s in range(n):
        near += [(s, s ^ 1), (n + s, n + (s ^ 2))]
        far += [(s, s ^ 2), (n + s, n + (s ^ 1))]
    return near, far


def on_device_planes(hidden_states, cotangent, lengths, params, first_moment, second_moment):
    n = 16
    both = ("rep", "shard")
    near, far = plane_moves(n)
    swap = [(0, 1), (1, 0)]
    own = make_frame(params)
    mine, other = [], []
    up = [(s, (s + 4) % n) for s in range(n)]
    down = [(s, (s - 4) % n) for s in range(n)]
    zero = None
    for t in range(4):
        zero = own if t == 0 else lax.ppermute(zero, "shard", up)
        one = lax.ppermute(zero, both, near)
        two = lax.ppermute(zero, both, far)
        three = lax.ppermute(one, both, far)
        group = [zero, one, two, three]
        mine += group
        other += [lax.ppermute(piece, "rep", swap) for piece in group]

    block_out, input_grad, left, right, sums = run_layer(lengths, hidden_states, cotangent, mine + other)

    operands = (
        hidden_states,
        lax.ppermute(hidden_states, "rep", swap),
        left,
        lax.ppermute(left, "rep", swap),
        right,
        sums,
        lax.ppermute(sums, "rep", swap),
    )
    passed = None
    for t in (3, 2, 1, 0):
        low, high = quad_grads(t, operands)
        if t == 0:
            high = lax.optimization_barrier((high, away))[0]
        from_far = lax.ppermute(high, both, far)
        if passed is not None:
            from_far = lax.optimization_barrier((from_far, leaving))[0]
        away = (low[1].astype(f32) + from_far[1].astype(f32)).astype(bf16)
        from_near = lax.ppermute(away, both, near)
        total = low[0].astype(f32) + from_far[0].astype(f32) + from_near.astype(f32)
        if passed is not None:
            total = total + passed.astype(f32)
        if t > 0:
            leaving = total.astype(bf16)
            passed = lax.ppermute(leaving, "shard", down)
    weight_grad, new_params, new_first, new_second = finish(
        total, lax.ppermute(total, "rep", swap), params, first_moment, second_moment
    )
    return (block_out, input_grad, weight_grad, new_params, new_first, new_second)


def on_device_any(hidden_states, cotangent, lengths, params, first_moment, second_moment):
    length = lengths[0]
    gathered = lax.all_gather(params.astype(jnp.bfloat16), "shard", axis=0, tiled=True)
    prm = split_flat(gathered)
    block_out, kept = forward(hidden_states, length, prm)
    input_grad, flat_grad = backward(hidden_states, length, cotangent, kept, prm)
    owned = lax.psum_scatter(flat_grad, "shard", scatter_dimension=0, tiled=True)
    weight_grad = lax.psum(owned, "rep")
    new_params, new_first, new_second = adamw(params, first_moment, second_moment, weight_grad)
    return (block_out, input_grad, weight_grad, new_params, new_first, new_second)


def solution(mesh):
    placed = (
        P(("rep", "shard"), None),
        P(("rep", "shard"), None),
        P(("rep", "shard")),
        P("shard"),
        P("shard"),
        P("shard"),
    )
    sixteen = mesh.shape["shard"] == 16 and mesh.shape["rep"] == 2
    return jax.shard_map(
        on_device_planes if sixteen else on_device_any,
        mesh=mesh,
        in_specs=placed,
        out_specs=(
            P(("rep", "shard"), None),
            P(("rep", "shard"), None),
            P("shard"),
            P("shard"),
            P("shard"),
            P("shard"),
        ),
        check_vma=False,
    )
```

```python
import functools
import math

import jax
import jax.numpy as jnp
from jax import lax
from jax.experimental import pallas as pl
from jax.experimental.pallas import tpu as pltpu
from jax.sharding import PartitionSpec as P

D = 768
HEADS = 12
HEAD = 64
FF = 3072
STEP = 3
HW = 768


norm_eps = 1e-05
adam_eps = 1e-06
beta_one = 0.9
beta_two = 0.98
learn_rate = 0.01
decay_rate = 0.01
masked_score = -1e30
inv_sqrt_two = 1.0 / math.sqrt(2.0)
inv_sqrt_tau = 1.0 / math.sqrt(2.0 * math.pi)


def layout():
    return [
        ("triple_weight", (D, 3 * HW)),
        ("output_weight", (HW, D)),
        ("expand_weight", (D, FF)),
        ("reduce_weight", (FF, D)),
        ("query_bias", (HW,)),
        ("value_bias", (HW,)),
        ("output_bias", (D,)),
        ("first_gain", (D,)),
        ("first_shift", (D,)),
        ("expand_bias", (FF,)),
        ("reduce_bias", (D,)),
        ("second_gain", (D,)),
        ("second_shift", (D,)),
    ]


def split_flat(flat_vector):
    pieces = {}
    offset = 0
    for entry_name, dims_of in layout():
        amount = math.prod(dims_of)
        pieces[entry_name] = flat_vector[offset : offset + amount].reshape(dims_of)
        offset = offset + amount
    return pieces


def inner_rows(left_side, right_side):
    return lax.dot_general(
        left_side, right_side, (((0,), (0,)), ((), ())), preferred_element_type=jnp.float32
    )


def by_transpose(left_side, right_side):
    return lax.dot_general(
        left_side, right_side, (((1,), (1,)), ((), ())), preferred_element_type=jnp.float32
    )


def heads_of(row_block):
    return row_block.reshape(row_block.shape[0], HEADS, HEAD)


def normalize(values_in):
    centered = values_in - jnp.mean(values_in, axis=-1, keepdims=True)
    inv_root = lax.rsqrt(jnp.mean(centered * centered, axis=-1, keepdims=True) + norm_eps)
    return (centered * inv_root, inv_root)


def norm_back(grad_in, normed, inv_root):
    return inv_root * (
        grad_in
        - jnp.mean(grad_in, axis=-1, keepdims=True)
        - normed * jnp.mean(grad_in * normed, axis=-1, keepdims=True)
    )


def gelu_slope(pre_act):
    return (
        0.5 * (1.0 + lax.erf(pre_act * inv_sqrt_two))
        + pre_act * jnp.exp(-0.5 * pre_act * pre_act) * inv_sqrt_tau
    )


def attention_scores(queries, key_rows, length):
    scores = jnp.einsum(
        "qhd,khd->hqk", heads_of(queries), heads_of(key_rows), preferred_element_type=jnp.float32
    ) * (1.0 / math.sqrt(HEAD))
    key_valid = jnp.arange(scores.shape[-1]) < length
    return jnp.where(key_valid, scores, masked_score)


def forward(tokens, length, prm):
    rows = tokens.shape[0]
    triple = jnp.dot(tokens, prm["triple_weight"], preferred_element_type=jnp.float32)
    queries = (triple[:, :HW] + prm["query_bias"].astype(jnp.float32)).astype(jnp.bfloat16)
    key_rows = triple[:, HW : 2 * HW].astype(jnp.bfloat16)
    value_rows = (triple[:, 2 * HW :] + prm["value_bias"].astype(jnp.float32)).astype(jnp.bfloat16)
    scores = attention_scores(queries, key_rows, length)
    top_score = jnp.max(scores, axis=-1, keepdims=True)
    log_total = top_score + jnp.log(jnp.sum(jnp.exp(scores - top_score), axis=-1, keepdims=True))
    soft_weights = jnp.exp(scores - log_total).astype(jnp.bfloat16)
    context = jnp.einsum(
        "hqk,khd->qhd", soft_weights, heads_of(value_rows), preferred_element_type=jnp.float32
    )
    context = context.reshape(rows, HW).astype(jnp.bfloat16)
    first_sum = (
        tokens.astype(jnp.float32)
        + jnp.dot(context, prm["output_weight"], preferred_element_type=jnp.float32)
        + prm["output_bias"].astype(jnp.float32)
    )
    normed_one, root_one = normalize(first_sum)
    middle = normed_one * prm["first_gain"].astype(jnp.float32) + prm["first_shift"].astype(
        jnp.float32
    )
    middle_b = middle.astype(jnp.bfloat16)
    pre_act = jnp.dot(middle_b, prm["expand_weight"], preferred_element_type=jnp.float32) + prm[
        "expand_bias"
    ].astype(jnp.float32)
    activated = (0.5 * pre_act * (1.0 + lax.erf(pre_act * inv_sqrt_two))).astype(jnp.bfloat16)
    second_sum = (
        middle
        + jnp.dot(activated, prm["reduce_weight"], preferred_element_type=jnp.float32)
        + prm["reduce_bias"].astype(jnp.float32)
    )
    normed_two, root_two = normalize(second_sum)
    block_out = (
        normed_two * prm["second_gain"].astype(jnp.float32)
        + prm["second_shift"].astype(jnp.float32)
    ).astype(jnp.bfloat16)
    kept = (
        queries,
        key_rows,
        value_rows,
        log_total,
        context,
        normed_one,
        root_one,
        middle_b,
        pre_act,
        activated,
        normed_two,
        root_two,
    )
    return (block_out, kept)


def backward(tokens, length, cotangent, kept, prm):
    (
        queries,
        key_rows,
        value_rows,
        log_total,
        context,
        normed_one,
        root_one,
        middle_b,
        pre_act,
        activated,
        normed_two,
        root_two,
    ) = kept
    rows = tokens.shape[0]
    grad_out = cotangent.astype(jnp.float32)
    d_second = norm_back(grad_out * prm["second_gain"].astype(jnp.float32), normed_two, root_two)
    d_second_b = d_second.astype(jnp.bfloat16)
    d_pre = by_transpose(d_second_b, prm["reduce_weight"]) * gelu_slope(pre_act)
    d_pre_b = d_pre.astype(jnp.bfloat16)
    d_middle = d_second + by_transpose(d_pre_b, prm["expand_weight"])
    d_first = norm_back(d_middle * prm["first_gain"].astype(jnp.float32), normed_one, root_one)
    d_first_b = d_first.astype(jnp.bfloat16)
    d_context = by_transpose(d_first_b, prm["output_weight"]).astype(jnp.bfloat16)
    scores = attention_scores(queries, key_rows, length)
    soft_float = jnp.exp(scores - log_total)
    soft_weights = soft_float.astype(jnp.bfloat16)
    d_soft = jnp.einsum(
        "qhd,khd->hqk",
        heads_of(d_context),
        heads_of(value_rows),
        preferred_element_type=jnp.float32,
    )
    delta = jnp.sum(d_soft * soft_float, axis=-1, keepdims=True)
    d_scores = (soft_float * (d_soft - delta) * (1.0 / math.sqrt(HEAD))).astype(jnp.bfloat16)
    d_query = jnp.einsum(
        "hqk,khd->qhd", d_scores, heads_of(key_rows), preferred_element_type=jnp.float32
    ).reshape(rows, HW)
    d_keys = jnp.einsum(
        "hqk,qhd->khd", d_scores, heads_of(queries), preferred_element_type=jnp.float32
    ).reshape(rows, HW)
    d_values = jnp.einsum(
        "hqk,qhd->khd", soft_weights, heads_of(d_context), preferred_element_type=jnp.float32
    ).reshape(rows, HW)
    d_triple = jnp.concatenate([d_query, d_keys, d_values], axis=1).astype(jnp.bfloat16)
    input_grad = (d_first + by_transpose(d_triple, prm["triple_weight"])).astype(jnp.bfloat16)
    grad_list = [
        inner_rows(tokens, d_triple),
        inner_rows(context, d_first_b),
        inner_rows(middle_b, d_pre_b),
        inner_rows(activated, d_second_b),
        jnp.sum(d_query, axis=0),
        jnp.sum(d_values, axis=0),
        jnp.sum(d_first, axis=0),
        jnp.sum(d_middle * normed_one, axis=0),
        jnp.sum(d_middle, axis=0),
        jnp.sum(d_pre, axis=0),
        jnp.sum(d_second, axis=0),
        jnp.sum(grad_out * normed_two, axis=0),
        jnp.sum(grad_out, axis=0),
    ]
    flat_grad = jnp.concatenate([piece_grad.reshape(-1) for piece_grad in grad_list])
    return (input_grad, flat_grad)


def adamw(param_now, first_now, second_now, grad_total):
    first_new = beta_one * first_now + (1.0 - beta_one) * grad_total
    second_new = beta_two * second_now + (1.0 - beta_two) * grad_total * grad_total
    fix_one = 1.0 - beta_one**STEP
    fix_two = 1.0 - beta_two**STEP
    param_new = param_now - learn_rate * (
        first_new / fix_one / (jnp.sqrt(second_new / fix_two) + adam_eps) + decay_rate * param_now
    )
    return (param_new, first_new, second_new)

ROW = 768
STEP_ROWS = 576
FRAME = 592
HALF = ROW // 2
LINES = FRAME * 6
LOCAL = 442944
LOCAL_LINES = 3464
ROWS = 16 * STEP_ROWS + 16
OUT_ROW = 2304
EXP_ROW = 3072
RED_ROW = 6144
BIAS_ROW = 9216
LEFT = 4608
FRONT = 72
BLOCKS = 2
BLOCK_LINES = 1736
RIGHT = 9 * HALF
MIB = 1024 * 1024

f32 = jnp.float32
bf16 = jnp.bfloat16


def place():
    here, core = lax.axis_index("shard"), lax.axis_index("rep")
    plane, spot = here // 4, here % 4
    flip = [0, core + 1, 2 - core, 3]
    back = [0, 2 - core, core + 1, 3]
    listed = [(9 * here) // 2, here % 2, 3 * core, 3 - 3 * core, HALF * core, HALF - HALF * core]
    listed += [(plane + 4 - t) % 4 for t in range(4)]
    return listed + [spot ^ k for k in flip] + [spot ^ k for k in back]


def swap_half(block):
    return pltpu.roll(block, 64, 1)


def frame_kernel(flat_ref, out_ref, lines):
    shift, odd, first_col = place()[:3]
    lines[0:FRONT, :] = jnp.zeros((FRONT, 128), f32)
    lines[FRONT : FRONT + 3456, :] = flat_ref[pl.ds(0, 442368)].reshape(3456, 128)
    lines[FRONT + 3456 : FRONT + LINES, :] = jnp.zeros((LINES - 3456, 128), f32)
    lines[FRONT + 3456 : FRONT + 3460, :] = flat_ref[pl.ds(442368, 512)].reshape(4, 128)
    lines[FRONT + 3460 : FRONT + 3461, 0:64] = flat_ref[pl.ds(442880, 64)].reshape(1, 64)
    low = lax.broadcasted_iota(jnp.int32, (FRAME, 128), 1) < 64
    for j in range(3):
        at = FRONT + first_col + j - shift
        here = lines[pl.ds(at, FRAME, stride=6), :]
        before = lines[pl.ds(at - 1, FRAME, stride=6), :]
        moved = jnp.where(low, swap_half(before), swap_half(here))
        out_ref[:, 128 * j : 128 * (j + 1)] = jnp.where(odd == 1, moved, here).astype(bf16)


def make_frame(params):
    return pl.pallas_call(
        frame_kernel,
        out_shape=jax.ShapeDtypeStruct((FRAME, HALF), bf16),
        in_specs=[pl.BlockSpec(memory_space=pltpu.VMEM)],
        out_specs=pl.BlockSpec(memory_space=pltpu.VMEM),
        scratch_shapes=[pltpu.VMEM((FRONT + LINES, 128), f32)],
        compiler_params=pltpu.CompilerParams(vmem_limit_bytes=12 * MIB),
    )(params)


def finish_kernel(
    mine_ref, other_ref, param_ref, first_ref, second_ref, grad_out, param_out, first_out, second_out, framed
):
    shift, odd, first_col, other_col = place()[:4]
    step = pl.program_id(0)

    @pl.when(step == 0)
    def _():
        framed[LINES : LINES + 48, :] = jnp.zeros((48, 128), f32)
        for j in range(3):
            at = slice(128 * j, 128 * (j + 1))
            framed[pl.ds(first_col + j, FRAME, stride=6), :] = mine_ref[:, at]
            framed[pl.ds(other_col + j, FRAME, stride=6), :] = other_ref[:, at]

    low = lax.broadcasted_iota(jnp.int32, (BLOCK_LINES, 128), 1) < 64
    here = framed[pl.ds(shift + BLOCK_LINES * step, BLOCK_LINES), :]
    after = framed[pl.ds(shift + BLOCK_LINES * step + 1, BLOCK_LINES), :]
    moved = jnp.where(low, swap_half(here), swap_half(after))
    grad = jnp.where(odd == 1, moved, here).reshape(BLOCK_LINES * 128)
    grad_out[...] = grad
    new_param, new_first, new_second = adamw(param_ref[...], first_ref[...], second_ref[...], grad)
    param_out[...] = new_param
    first_out[...] = new_first
    second_out[...] = new_second


def finish(mine, other, params, first_moment, second_moment):
    vmem_spec = pl.BlockSpec(memory_space=pltpu.VMEM)
    block_spec = pl.BlockSpec((BLOCK_LINES * 128,), lambda i: (i,))
    return pl.pallas_call(
        finish_kernel,
        grid=(BLOCKS,),
        out_shape=[jax.ShapeDtypeStruct((LOCAL,), f32)] * 4,
        in_specs=[vmem_spec, vmem_spec] + [block_spec] * 3,
        out_specs=[block_spec] * 4,
        scratch_shapes=[pltpu.VMEM((LINES + 48, 128), f32)],
        compiler_params=pltpu.CompilerParams(vmem_limit_bytes=30 * MIB),
    )(mine, other, params, first_moment, second_moment)


def dot_nn(left_side, right_side):
    return jnp.dot(left_side, right_side, preferred_element_type=f32)


def row_mean(block):
    return jnp.mean(block, axis=-1, keepdims=True)


def layer_kernel(length_ref, tokens_ref, cot_ref, *refs):
    frames = refs[:32]
    block_ref, input_ref, left_ref, right_ref, sums_ref = refs[32:37]
    (
        weights,
        triple_w,
        expand_w,
        tails,
        stage,
        triple_b,
        soft_all,
        slope_all,
        rights,
        sem_main,
        sem_tail,
    ) = refs[37:]
    bias_grads = sums_ref
    meta = place()
    length = length_ref[0]
    cols = (pl.multiple_of(meta[4], 128), pl.multiple_of(meta[5], 128))

    def main_copy(frame, shard, side):
        return pltpu.make_async_copy(
            frame.at[pl.ds(0, STEP_ROWS), :],
            weights.at[pl.ds(pl.multiple_of(shard * STEP_ROWS, 16), STEP_ROWS), pl.ds(cols[side], HALF)],
            sem_main.at[side, shard],
        )

    def tail_copy(frame, shard, side):
        return pltpu.make_async_copy(
            frame.at[pl.ds(STEP_ROWS, 16), :],
            tails.at[shard, :, pl.ds(cols[side], HALF)],
            sem_tail.at[side, shard],
        )

    def each_frame(t):
        for side in range(2):
            for j in range(4):
                yield frames[16 * side + 4 * t + j], 4 * meta[6 + t] + meta[10 + 4 * side + j], side

    for t in range(4):
        for frame, shard, side in each_frame(t):
            tail_copy(frame, shard, side).start()
    for now in (True, False):
        for t in range(4):

            @pl.when((meta[6 + t] == 0) == now)
            def _():
                for frame, shard, side in each_frame(t):
                    main_copy(frame, shard, side).start()

    def arrive(first, last):
        for shard in range(first, last):
            for side in range(2):
                main_copy(frames[0], shard, side).wait()
            if shard > 0:
                for side in range(2):
                    tail_copy(frames[0], shard - 1, side).wait()
                at = STEP_ROWS * shard
                joined = weights[at : at + 16, :].astype(f32) + tails[shard - 1].astype(f32)
                weights[at : at + 16, :] = joined.astype(bf16)

    for side in range(2):
        tail_copy(frames[0], 15, side).wait()
    arrive(0, 4)

    def spread_triple(i, carry):
        for j in range(6):
            at = slice(128 * j, 128 * (j + 1))
            stage[j, 0:384, :] = weights[pl.ds(pl.multiple_of(384 * i, 16), 384), at].astype(f32)
            for part in range(3):
                rows = stage[j, pl.ds(part, 128, stride=3), :]
                triple_w[part, pl.ds(pl.multiple_of(128 * i, 16), 128), at] = rows.astype(bf16)
        return carry

    lax.fori_loop(0, 6, spread_triple, 0)

    def spread_expand(i, carry):
        row = pl.multiple_of(EXP_ROW + 512 * i, 16)
        for j in range(6):
            at = slice(128 * j, 128 * (j + 1))
            stage[j, :, :] = weights[pl.ds(row, 512), at].astype(f32)
            for part in range(4):
                rows = stage[j, pl.ds(part, 128, stride=4), :]
                expand_w[part, pl.ds(pl.multiple_of(128 * i, 16), 128), at] = rows.astype(bf16)
        return carry

    biases = tails[15].astype(f32)

    def bias(index):
        return biases[index : index + 1, :]

    bias_grads[...] = jnp.zeros((16, ROW), f32)

    def keep_bias(index, block):
        bias_grads[index : index + 1, :] = jnp.sum(block, axis=0, keepdims=True)

    tokens = tokens_ref[...]
    triple_b[0] = (dot_nn(tokens, triple_w[0]) + bias(0)).astype(bf16)
    triple_b[1] = dot_nn(tokens, triple_w[1]).astype(bf16)
    triple_b[2] = (dot_nn(tokens, triple_w[2]) + bias(1)).astype(bf16)

    lane = lax.broadcasted_iota(jnp.int32, (1, 128), 1)
    head_masks = ((lane < 64).astype(f32).astype(bf16), (lane >= 64).astype(f32).astype(bf16))
    key_valid = lax.broadcasted_iota(jnp.int32, (128, 128), 1) < length
    scale = 1.0 / math.sqrt(HEAD)
    for pair in range(6):
        at = slice(128 * pair, 128 * (pair + 1))
        queries, key_rows, value_rows = triple_b[0, :, at], triple_b[1, :, at], triple_b[2, :, at]
        context = jnp.zeros((128, 128), f32)
        for side in range(2):
            scores = by_transpose(queries * head_masks[side], key_rows) * scale
            scores = jnp.where(key_valid, scores, masked_score)
            top_score = jnp.max(scores, axis=-1, keepdims=True)
            log_total = top_score + jnp.log(
                jnp.sum(jnp.exp(scores - top_score), axis=-1, keepdims=True)
            )
            soft_float = jnp.exp(scores - log_total)
            soft_all[2 * pair + side] = soft_float
            context = context + dot_nn(soft_float.astype(bf16), value_rows * head_masks[side])
        left_ref[:, at] = context.astype(bf16)

    arrive(4, 6)
    first_sum = tokens.astype(f32) + dot_nn(left_ref[:, 0:768], weights[OUT_ROW : OUT_ROW + 768, :]) + bias(2)
    normed_one, root_one = normalize(first_sum)
    middle = normed_one * bias(3) + bias(4)
    middle_b = middle.astype(bf16)
    left_ref[:, 768:1536] = middle_b
    second_sum = middle + bias(9)
    arrive(6, 11)
    lax.fori_loop(0, 6, spread_expand, 0)
    arrive(11, 16)
    for part in range(4):
        at = slice(768 * part, 768 * (part + 1))
        pre_act = dot_nn(middle_b, expand_w[part]) + bias(5 + part)
        erf_term = 1.0 + lax.erf(pre_act * inv_sqrt_two)
        activated = (0.5 * pre_act * erf_term).astype(bf16)
        left_ref[:, 1536 + 768 * part : 1536 + 768 * (part + 1)] = activated
        slope_all[:, at] = 0.5 * erf_term + pre_act * jnp.exp(-0.5 * pre_act * pre_act) * inv_sqrt_tau
        red_at = RED_ROW + 768 * part
        second_sum = second_sum + dot_nn(activated, weights[red_at : red_at + 768, :])
    normed_two, root_two = normalize(second_sum)
    block_ref[...] = (normed_two * bias(10) + bias(11)).astype(bf16)

    grad_out = cot_ref[...].astype(f32)
    keep_bias(10, grad_out * normed_two)
    keep_bias(11, grad_out)
    d_second = norm_back(grad_out * bias(10), normed_two, root_two)
    keep_bias(9, d_second)
    d_second_b = d_second.astype(bf16)
    d_middle = d_second
    for part in range(4):
        at = slice(768 * part, 768 * (part + 1))
        red_at = RED_ROW + 768 * part
        d_pre = by_transpose(d_second_b, weights[red_at : red_at + 768, :]) * slope_all[:, at]
        keep_bias(5 + part, d_pre)
        d_pre_b = d_pre.astype(bf16)
        rights[1 + part] = d_pre_b
        d_middle = d_middle + by_transpose(d_pre_b, expand_w[part])

    rights[5] = d_second_b
    keep_bias(3, d_middle * normed_one)
    keep_bias(4, d_middle)
    d_first = norm_back(d_middle * bias(3), normed_one, root_one)
    keep_bias(2, d_first)
    d_first_b = d_first.astype(bf16)
    d_context_b = by_transpose(d_first_b, weights[OUT_ROW : OUT_ROW + 768, :]).astype(bf16)

    rights[0] = d_first_b
    for pair in range(6):
        at = slice(128 * pair, 128 * (pair + 1))
        queries, key_rows, value_rows = triple_b[0, :, at], triple_b[1, :, at], triple_b[2, :, at]
        d_context = d_context_b[:, at]
        d_query = jnp.zeros((128, 128), f32)
        d_keys = jnp.zeros((128, 128), f32)
        d_values = jnp.zeros((128, 128), f32)
        for side in range(2):
            soft_float = soft_all[2 * pair + side]
            d_part = d_context * head_masks[side]
            d_soft = by_transpose(d_part, value_rows)
            delta = jnp.sum(d_soft * soft_float, axis=-1, keepdims=True)
            d_scores = (soft_float * (d_soft - delta) * scale).astype(bf16)
            d_query = d_query + dot_nn(d_scores, key_rows * head_masks[side])
            d_keys = d_keys + inner_rows(d_scores, queries * head_masks[side])
            d_values = d_values + inner_rows(soft_float.astype(bf16), d_part)
        bias_grads[0:1, at] = jnp.sum(d_query, axis=0, keepdims=True)
        bias_grads[1:2, at] = jnp.sum(d_values, axis=0, keepdims=True)
        rights[6, :, at] = d_query.astype(bf16)
        rights[7, :, at] = d_keys.astype(bf16)
        rights[8, :, at] = d_values.astype(bf16)

    input_grad = d_first
    for part in range(3):
        input_grad = input_grad + by_transpose(rights[6 + part], triple_w[part])
    input_ref[...] = input_grad.astype(bf16)

    for k in range(9):
        right_ref[:, HALF * k : HALF * (k + 1)] = rights[k, :, pl.ds(cols[0], HALF)]
        left_ref[:, 4608 + HALF * k : 4608 + HALF * (k + 1)] = rights[k, :, pl.ds(cols[1], HALF)]


def run_layer(lengths, tokens, cotangent, frames):
    any_spec = pl.BlockSpec(memory_space=pl.ANY)
    vmem_spec = pl.BlockSpec(memory_space=pltpu.VMEM)
    rows = tokens.shape[0]
    thin = jax.ShapeDtypeStruct((rows, D), bf16)
    out = pl.pallas_call(
        layer_kernel,
        out_shape=[
            thin,
            thin,
            pltpu.VMEM((rows, LEFT + RIGHT), bf16),
            pltpu.VMEM((rows, RIGHT), bf16),
            jax.ShapeDtypeStruct((16, ROW), f32),
        ],
        in_specs=[pl.BlockSpec(memory_space=pltpu.SMEM)] + [vmem_spec] * 2 + [any_spec] * 32,
        out_specs=[vmem_spec] * 5,
        scratch_shapes=[
            pltpu.VMEM((ROWS, ROW), bf16),
            pltpu.VMEM((3, D, HW), bf16),
            pltpu.VMEM((4, D, ROW), bf16),
            pltpu.VMEM((16, 16, ROW), bf16),
            pltpu.VMEM((6, 512, 128), f32),
            pltpu.VMEM((3, rows, HW), bf16),
            pltpu.VMEM((HEADS, rows, rows), f32),
            pltpu.VMEM((rows, FF), f32),
            pltpu.VMEM((9, rows, HW), bf16),
            pltpu.SemaphoreType.DMA((2, 16)),
            pltpu.SemaphoreType.DMA((2, 16)),
        ],
        compiler_params=pltpu.CompilerParams(vmem_limit_bytes=35 * MIB),
    )(lengths, tokens, cotangent, *frames)
    return out


def grad_kernel(
    slot,
    tokens_ref,
    tokens_other,
    left_ref,
    left_other,
    right_ref,
    sums_ref,
    sums_other,
    low_ref,
    high_ref,
    left,
    right,
    grads,
    stage,
    sem_in,
    sem_out,
):
    meta = place()
    quad = meta[6 + slot]

    def load(pieces):
        copies = []
        for k, (source, first, size, target, at, row) in enumerate(pieces):
            copies.append(
                pltpu.make_async_copy(
                    source.at[:, pl.ds(first, size)],
                    target.at[pl.ds(row, 128), pl.ds(at, size)],
                    sem_in.at[k],
                )
            )
        for copy in copies:
            copy.start()
        for copy in copies:
            copy.wait()

    def left_pieces(first, size, at):
        return [(left_ref, first, size, left, at, 0), (left_other, first, size, left, at, 128)]

    def right_pieces(first, size, at):
        return [
            (right_ref, first, size, right, at, 0),
            (left_other, LEFT + first, size, right, at, 128),
        ]

    def mixed(first, right_first, parts, chunks, row, rows_used):
        def step(i, carry):
            rows = left[:, pl.ds(pl.multiple_of(first + 128 * i, 128), 128)]
            for part in range(parts):
                at = right_first + HALF * part
                block = inner_rows(rows, right[:, at : at + HALF])
                for j in range(3):
                    stage[j, pl.ds(part, 128, stride=parts), :] = block[:, 128 * j : 128 * (j + 1)]
            at = pl.multiple_of(row + 128 * parts * i, 16)
            for j in range(3):
                grads[pl.ds(at, rows_used), 128 * j : 128 * (j + 1)] = stage[j, 0:rows_used, :].astype(bf16)
            return carry

        lax.fori_loop(0, chunks, step, 0, unroll=min(chunks, 3))

    def plain(first, right_first, chunks, row):
        def step(i, carry):
            rows = left[:, pl.ds(pl.multiple_of(first + 256 * i, 128), 256)]
            block = inner_rows(rows, right[:, right_first : right_first + HALF])
            grads[pl.ds(pl.multiple_of(row + 256 * i, 16), 256), :] = block.astype(bf16)
            return carry

        lax.fori_loop(0, chunks, step, 0, unroll=min(chunks, 3))

    def last_rows(first, right_first):
        block = inner_rows(left[:, first : first + 128], right[:, right_first : right_first + HALF])
        grads[2304:2320, :] = block[0:16].astype(bf16)

    @pl.when(quad == 0)
    def _():
        load(
            [(tokens_ref, 0, 768, left, 0, 0), (tokens_other, 0, 768, left, 0, 128)]
            + left_pieces(0, 128, 768)
            + right_pieces(2304, 1152, 0)
            + right_pieces(0, 384, 1152)
        )
        mixed(0, 0, 3, 6, 0, 384)
        last_rows(768, 1152)

    @pl.when(quad == 1)
    def _():
        load(left_pieces(0, 1280, 0) + right_pieces(0, 1920, 0))
        plain(0, 0, 3, 0)
        mixed(768, 384, 4, 3, 768, 512)
        mixed(1152, 384, 4, 1, 2304, 16)

    @pl.when(quad == 2)
    def _():
        load(left_pieces(1152, 1280, 0) + right_pieces(384, 1920, 0))
        mixed(0, 0, 4, 3, 0, 512)
        plain(384, 1536, 3, 1536)
        last_rows(1152, 1536)

    @pl.when(quad == 3)
    def _():
        load(left_pieces(2304, 2304, 0) + right_pieces(1920, 384, 0))
        plain(0, 0, 9, 0)
        own = pl.ds(pl.multiple_of(meta[4], 128), HALF)
        grads[2304:2320, :] = (sums_ref[:, own] + sums_other[:, own]).astype(bf16)

    departures = []
    for j in (2, 3, 0, 1):
        row = pl.multiple_of(meta[10 + j] * STEP_ROWS, 16)
        target = (low_ref, high_ref)[j // 2].at[j % 2]
        copy = pltpu.make_async_copy(grads.at[pl.ds(row, FRAME), :], target, sem_out.at[j])
        copy.start()
        departures.append(copy)
    for copy in departures:
        copy.wait()


def quad_grads(slot, operands):
    any_spec = pl.BlockSpec(memory_space=pl.ANY)
    vmem_spec = pl.BlockSpec(memory_space=pltpu.VMEM)
    frames = jax.ShapeDtypeStruct((2, FRAME, HALF), bf16)
    return pl.pallas_call(
        functools.partial(grad_kernel, slot),
        out_shape=[frames, frames],
        in_specs=[any_spec] * 5 + [vmem_spec] * 2,
        out_specs=[any_spec] * 2,
        scratch_shapes=[
            pltpu.VMEM((256, 2304), bf16),
            pltpu.VMEM((256, 1920), bf16),
            pltpu.VMEM((4 * STEP_ROWS + 16, HALF), bf16),
            pltpu.VMEM((3, 512, 128), f32),
            pltpu.SemaphoreType.DMA((8,)),
            pltpu.SemaphoreType.DMA((4,)),
        ],
        compiler_params=pltpu.CompilerParams(vmem_limit_bytes=14 * MIB),
        cost_estimate=pl.CostEstimate(flops=1000, bytes_accessed=1000, transcendentals=0),
    )(*operands)


def plane_moves(n):
    near, far = [], []
    for s in range(n):
        near += [(s, s ^ 1), (n + s, n + (s ^ 2))]
        far += [(s, s ^ 2), (n + s, n + (s ^ 1))]
    return near, far


def on_device_planes(hidden_states, cotangent, lengths, params, first_moment, second_moment):
    n = 16
    both = ("rep", "shard")
    near, far = plane_moves(n)
    swap = [(0, 1), (1, 0)]
    own = make_frame(params)
    mine, other = [], []
    up = [(s, (s + 4) % n) for s in range(n)]
    down = [(s, (s - 4) % n) for s in range(n)]
    zero = None
    for t in range(4):
        zero = own if t == 0 else lax.ppermute(zero, "shard", up)
        one = lax.ppermute(zero, both, near)
        two = lax.ppermute(zero, both, far)
        three = lax.ppermute(one, both, far)
        group = [zero, one, two, three]
        mine += group
        other += [lax.ppermute(piece, "rep", swap) for piece in group]

    block_out, input_grad, left, right, sums = run_layer(lengths, hidden_states, cotangent, mine + other)

    operands = (
        hidden_states,
        lax.ppermute(hidden_states, "rep", swap),
        left,
        lax.ppermute(left, "rep", swap),
        right,
        sums,
        lax.ppermute(sums, "rep", swap),
    )
    passed = None
    for t in (3, 2, 1, 0):
        low, high = quad_grads(t, operands)
        if t == 0:
            high = lax.optimization_barrier((high, away))[0]
        from_far = lax.ppermute(high, both, far)
        if passed is not None:
            from_far = lax.optimization_barrier((from_far, leaving))[0]
        away = (low[1].astype(f32) + from_far[1].astype(f32)).astype(bf16)
        from_near = lax.ppermute(away, both, near)
        total = low[0].astype(f32) + from_far[0].astype(f32) + from_near.astype(f32)
        if passed is not None:
            total = total + passed.astype(f32)
        if t > 0:
            leaving = total.astype(bf16)
            passed = lax.ppermute(leaving, "shard", down)
    weight_grad, new_params, new_first, new_second = finish(
        total, lax.ppermute(total, "rep", swap), params, first_moment, second_moment
    )
    return (block_out, input_grad, weight_grad, new_params, new_first, new_second)


def on_device_any(hidden_states, cotangent, lengths, params, first_moment, second_moment):
    length = lengths[0]
    gathered = lax.all_gather(params.astype(jnp.bfloat16), "shard", axis=0, tiled=True)
    prm = split_flat(gathered)
    block_out, kept = forward(hidden_states, length, prm)
    input_grad, flat_grad = backward(hidden_states, length, cotangent, kept, prm)
    owned = lax.psum_scatter(flat_grad, "shard", scatter_dimension=0, tiled=True)
    weight_grad = lax.psum(owned, "rep")
    new_params, new_first, new_second = adamw(params, first_moment, second_moment, weight_grad)
    return (block_out, input_grad, weight_grad, new_params, new_first, new_second)


def solution(mesh):
    placed = (
        P(("rep", "shard"), None),
        P(("rep", "shard"), None),
        P(("rep", "shard")),
        P("shard"),
        P("shard"),
        P("shard"),
    )
    sixteen = mesh.shape["shard"] == 16 and mesh.shape["rep"] == 2
    return jax.shard_map(
        on_device_planes if sixteen else on_device_any,
        mesh=mesh,
        in_specs=placed,
        out_specs=(
            P(("rep", "shard"), None),
            P(("rep", "shard"), None),
            P("shard"),
            P("shard"),
            P("shard"),
            P("shard"),
        ),
        check_vma=False,
    )
```
